128 devices in a mesh: dp: 16 (over z, y_hi, core), seq: 8 (over y_lo, x).
Axes of the slice: x: 4, y: 4 (y_hi: 2, y_lo: 2; y = y_hi * 2 + y_lo), z: 4, core: 2. Of those that a mesh axis runs over, the one named last changes fastest.
Arguments:
- inputs: bfloat16 [16, 2048, 4096], P('dp', 'seq'), may hold values from -10 to 10
- weights: bfloat16 [4096, 1280], P('dp'), may hold values from -0.09375 to 0.09375
- cotangent: bfloat16 [16, 2048, 1024], P('dp', 'seq'), may hold values from -6 to 6
- doc_lengths: int32 [16, 8], P('dp'), may hold values from 1 to 1024, 2048 in all within a row
- kept_flags: int32 [16, 8], P('dp'), may hold values 0 or 1
Outputs:
- attention: bfloat16 [16, 2048, 1024], P('dp', 'seq')
- inputs_grad: bfloat16 [16, 2048, 4096], P('dp', 'seq')
- weights_grad: float32 [4096, 1280], P(('dp', 'seq'))
The draws below stay inside these ranges and needn't reach their ends.
All inputs are finite; a program needn't handle non-finite values. No bound on the sum of `kept_flags` on one device may be relied on, other than what follows from the above.
Results may differ from the reference program's by a relative error of at most 0.013.
Values may be sent and summed in bfloat16 or wider, within the bound.
A program may use at most 128 MiB of HBM per device.

```python
import math
import jax
import jax.numpy as jnp
import numpy as np
from jax import lax

D = 4096
HEAD_DIM = 128
NDOC = 8
HEADS = 8
COLS = 1280
SEQ = 2048
PACKS = 16


def draw_inputs(key, part):
    values = jax.random.normal(key, (PACKS, SEQ, D), jnp.float32)
    values = jnp.clip(values, -5.0, 5.0)
    return values.astype(jnp.bfloat16)


def plant(entries, stream_key, smallest, top_value):
    shape = entries.shape
    spot = [jax.random.randint(jax.random.fold_in(stream_key, axis), (), 0, shape[axis]) for axis in range(len(shape))]
    entries = entries.at[tuple(spot)].set(smallest)
    longest = shape.index(max(shape))
    spot[longest] = (spot[longest] + 1) % shape[longest]
    return entries.at[tuple(spot)].set(top_value)


def steps_of(own_key, extent, pieces, least, largest):
    gain = 1.0
    for position, parts in pieces:
        steps = jax.random.uniform(jax.random.fold_in(jax.random.fold_in(own_key, 6), position), (parts,), jnp.float32, least / len(pieces), largest / len(pieces))
        gain = gain * jnp.repeat(jnp.exp(steps), extent[position] // parts).reshape((-1,) + (1,) * (len(extent) - 1 - position))
    return gain


def length_profile(count, total, most, slope):
    weights = [(1 << 20) // math.isqrt(standing ** slope) + 1 for standing in range(2, count + 1)]
    rest, counts = total - most - (count - 1), [1] * (count - 1)
    while rest > 0:
        candidates = [i for i in range(count - 1) if counts[i] < most]
        pool, left = sum([weights[i] for i in candidates]), rest
        for i in candidates:
            extra = min(most - counts[i], max(1, left * weights[i] // pool), rest)
            counts[i] = counts[i] + extra
            rest = rest - extra
    return np.array([most] + counts)


def ragged_sizes(own_key, count, total, bound, lean):
    if count == 2:
        one = jax.random.randint(own_key, (), max(1, total - bound), min(bound, total - 1) + 1)
        return jnp.stack([one, total - one])
    sizes = jnp.asarray(length_profile(count, total, bound, lean), jnp.int32)
    couples = (count - 1) // 2
    giver, sink = sizes[1:1 + 2 * couples:2], sizes[2:2 + 2 * couples:2]
    room = jnp.minimum(giver - 1, bound - sink)
    moved = jax.random.randint(jax.random.fold_in(own_key, 1), (couples,), 0, 1 << 20) % (room + 1)
    sizes = sizes.at[1:1 + 2 * couples:2].set(giver - moved).at[2:2 + 2 * couples:2].set(sink + moved)
    return sizes[jax.random.permutation(jax.random.fold_in(own_key, 2), count)]


def scatter_about(own_key, shape, deviation, limit, cuts=(), kind=jnp.bfloat16):
    drawn = deviation * jax.random.normal(own_key, shape, jnp.float32)
    if cuts:
        drawn = drawn * steps_of(own_key, shape, cuts, -0.22, 0.18)
    return jnp.clip(drawn, -limit, limit).astype(kind)


def setup_inputs(seed: int = 0) -> dict:
    key_of = jax.random.split(jax.random.key(seed), 6)
    return {
        "inputs": draw_inputs(jax.random.fold_in(key_of[5], 71), 0),
        "weights": scatter_about(key_of[1], (D, COLS), D ** -0.5, 0.09375, ((0, 16),)),
        "cotangent": scatter_about(key_of[2], (PACKS, SEQ, HEADS * HEAD_DIM), 1.0, 6.0, ((0, 16), (1, 8))),
        "doc_lengths": jax.vmap(lambda own: ragged_sizes(own, NDOC, SEQ, SEQ // 2, 2))(jax.random.split(key_of[3], PACKS)).reshape((PACKS, NDOC)).astype(jnp.int32),
        "kept_flags": plant((jax.random.randint(key_of[4], (PACKS, NDOC), 0, 4) < 3).astype(jnp.int32), jax.random.fold_in(key_of[4], 1), 0, 1),
    }


def doc_tables(doc_row, flag_row, positions):
    doc_ends = jnp.cumsum(doc_row).astype(jnp.int32)
    doc_starts = (doc_ends - doc_row).astype(jnp.int32)
    inside = (positions[:, None] >= doc_starts[None, :]) & (positions[:, None] < doc_ends[None, :])
    start_of = lax.optimization_barrier(jnp.sum(jnp.where(inside, doc_starts[None, :], 0), axis=1)).astype(jnp.int32)
    keep_of = lax.optimization_barrier(jnp.sum(jnp.where(inside, flag_row[None, :], 0), axis=1)).astype(jnp.int32)
    return (start_of, keep_of)

def reference(inputs, weights, cotangent, doc_lengths, kept_flags):
    qwidth = HEADS * HEAD_DIM
    softmax_scale = 1.0 / math.sqrt(HEAD_DIM)
    positions = jnp.arange(SEQ, dtype=jnp.int32)

    def one_pack(grad_total, packed):
        tokens, cot_rows, doc_row, flag_row = packed
        start_of, keep_of = doc_tables(doc_row, flag_row, positions)
        projected = jnp.dot(tokens, weights, preferred_element_type=jnp.float32).astype(jnp.bfloat16)
        queries = projected[:, :qwidth].reshape(SEQ, HEADS, HEAD_DIM).transpose(1, 0, 2)
        keys = projected[:, qwidth:qwidth + HEAD_DIM]
        values = projected[:, qwidth + HEAD_DIM:]
        cot_kept = jnp.where(keep_of[:, None] > 0, cot_rows, jnp.zeros_like(cot_rows))
        cot_heads = cot_kept.reshape(SEQ, HEADS, HEAD_DIM).transpose(1, 0, 2)
        allowed = (positions[None, :] >= start_of[:, None]) & (positions[None, :] <= positions[:, None])

        def one_head(pair):
            query_rows, cot_head = pair
            logits = lax.dot_general(query_rows, keys, (((1,), (1,)), ((), ())), preferred_element_type=jnp.float32) * softmax_scale
            logits = jnp.where(allowed, logits, -jnp.inf)
            attn_weights = jax.nn.softmax(logits, axis=1)
            weights_half = attn_weights.astype(jnp.bfloat16)
            out_head = jnp.dot(weights_half, values, preferred_element_type=jnp.float32).astype(jnp.bfloat16)
            weight_grads = lax.dot_general(cot_head, values, (((1,), (1,)), ((), ())), preferred_element_type=jnp.float32)
            row_delta = lax.optimization_barrier(jnp.sum(cot_head.astype(jnp.float32) * out_head.astype(jnp.float32), axis=1))
            score_grads = (attn_weights * (weight_grads - row_delta[:, None])).astype(jnp.bfloat16)
            query_grad = (jnp.dot(score_grads, keys, preferred_element_type=jnp.float32) * softmax_scale).astype(jnp.bfloat16)
            key_grad = lax.dot_general(score_grads, query_rows, (((0,), (0,)), ((), ())), preferred_element_type=jnp.float32) * softmax_scale
            value_grad = lax.dot_general(weights_half, cot_head, (((0,), (0,)), ((), ())), preferred_element_type=jnp.float32)
            return (out_head, query_grad, key_grad, value_grad)
        out_heads, query_grads, key_grads, value_grads = lax.map(one_head, (queries, cot_heads))
        attention = out_heads.transpose(1, 0, 2).reshape(SEQ, qwidth)
        query_part = query_grads.transpose(1, 0, 2).reshape(SEQ, qwidth)
        key_part = lax.optimization_barrier(jnp.sum(key_grads, axis=0)).astype(jnp.bfloat16)
        value_part = lax.optimization_barrier(jnp.sum(value_grads, axis=0)).astype(jnp.bfloat16)
        dprojected = jnp.concatenate([query_part, key_part, value_part], axis=1)
        inputs_grad = lax.dot_general(dprojected, weights, (((1,), (1,)), ((), ())), preferred_element_type=jnp.float32).astype(jnp.bfloat16)
        grad_total = grad_total + lax.dot_general(tokens, dprojected, (((0,), (0,)), ((), ())), preferred_element_type=jnp.float32)
        return (grad_total, (attention, inputs_grad))
    start_grad = jnp.zeros((D, COLS), jnp.float32)
    weights_grad, outputs = lax.scan(one_pack, start_grad, (inputs, cotangent, doc_lengths, kept_flags))
    return (outputs[0], outputs[1], weights_grad)
```

```python
import math

import jax
import jax.numpy as jnp
from jax import lax
from jax.experimental import pallas as pl
from jax.experimental.pallas import tpu as pltpu
from jax.sharding import PartitionSpec as P

MESH = pl.DeviceIdType.MESH
HEAD = 128
HEADS = 8
BLK = 256
WIN = 5
D = 4096
QW = 1024
COLS = 1280
NDOC = 8
SEQN = 8
SCALE = 1.0 / math.sqrt(HEAD)
LOG2E = math.log2(math.e)
F32 = jnp.float32
BF16 = jnp.bfloat16
NT = (((1,), (1,)), ((), ()))
COLORS = ((0, 512, "xyz"), (512, 384, "yzx"), (896, 384, "zxy"))


def place():
    dp = lax.axis_index("dp")
    seq = lax.axis_index("seq")
    z = lax.div(dp, 4)
    y = lax.rem(lax.div(dp, 2), 2) * 2 + lax.div(seq, 4)
    return {"z": z, "y": y, "x": lax.rem(seq, 4), "c": lax.rem(dp, 2)}


def device(at):
    dp = at["z"] * 4 + lax.div(at["y"], 2) * 2 + at["c"]
    return (dp, lax.rem(at["y"], 2) * 4 + at["x"])


def moved(at, axis, step):
    count = 2 if axis == "c" else 4
    there = dict(at)
    there[axis] = lax.rem(at[axis] + step, count)
    return there


def barrier_with(devices):
    sem = pltpu.get_barrier_semaphore()
    for there in devices:
        pl.semaphore_signal(sem, inc=1, device_id=there, device_id_type=MESH)
    pl.semaphore_wait(sem, len(devices))


def seq_peers():
    dp = lax.axis_index("dp")
    seq = lax.axis_index("seq")
    return [(dp, lax.rem(seq + step, SEQN)) for step in range(1, SEQN)]


def project_kernel(x_ref, w_hbm, q_ref, kv_ref, w_vmem, load_sem, send_sem, recv_sem):
    dp = lax.axis_index("dp")
    seq = lax.axis_index("seq")
    loads = [
        pltpu.make_async_copy(
            w_hbm.at[:, pl.ds(first, 256)], w_vmem.at[:, pl.ds(first, 256)], load_sem.at[first // 256]
        )
        for first in (1024, 0, 256, 512, 768)
    ]
    for load in loads:
        load.start()
    barrier_with(seq_peers())
    loads[0].wait()
    kv = jnp.dot(x_ref[...], w_vmem[:, QW:], preferred_element_type=F32)
    kv_ref[WIN - 1] = kv.astype(BF16)

    def copy(step):
        return pltpu.make_async_remote_copy(
            src_ref=kv_ref.at[WIN - 1],
            dst_ref=kv_ref.at[WIN - 1 - step],
            send_sem=send_sem.at[step - 1],
            recv_sem=recv_sem.at[step - 1],
            device_id=(dp, lax.rem(seq + step, SEQN)),
            device_id_type=MESH,
        )

    for step in range(1, WIN):
        @pl.when(seq + step < SEQN)
        def _(step=step):
            copy(step).start()

        @pl.when(seq < step)
        def _(step=step):
            kv_ref[WIN - 1 - step] = jnp.zeros((BLK, 2 * HEAD), BF16)

    for index, first in enumerate((0, 256, 512, 768)):
        loads[index + 1].wait()
        q_ref[:, first : first + 256] = jnp.dot(
            x_ref[...], w_vmem[:, first : first + 256], preferred_element_type=F32
        ).astype(BF16)
    for step in range(1, WIN):
        @pl.when(seq >= step)
        def _(step=step):
            copy(step).wait_recv()

        @pl.when(seq + step < SEQN)
        def _(step=step):
            copy(step).wait_send()


def attend_kernel(
    len_ref, flag_ref, q_ref, kv_ref, cot_ref, o_ref, dq_ref, dkv_ref, s_buf, bias, dkv_acc, kt_buf, vt_buf
):
    seq = lax.axis_index("seq")
    row0 = seq * BLK
    lane_pos = row0 + lax.broadcasted_iota(jnp.int32, (1, BLK), 1)
    sub_pos = row0 + lax.broadcasted_iota(jnp.int32, (BLK, HEAD), 0)
    first_start = jnp.int32(0)
    doc_start = jnp.int32(0)
    starts = jnp.zeros((1, BLK), jnp.int32)
    keep = jnp.zeros((BLK, HEAD), jnp.int32)
    for doc in range(NDOC):
        doc_end = doc_start + len_ref[0, doc]
        first_start = jnp.where((row0 >= doc_start) & (row0 < doc_end), doc_start, first_start)
        starts = jnp.where((lane_pos >= doc_start) & (lane_pos < doc_end), doc_start, starts)
        keep = jnp.where((sub_pos >= doc_start) & (sub_pos < doc_end), flag_ref[0, doc], keep)
        doc_start = doc_end
    base = seq - (WIN - 1)
    low = lax.div(first_start, BLK) - base
    dkv_acc[...] = jnp.zeros_like(dkv_acc)

    def prepare(j, carry):
        key_pos = (base + j) * BLK + lax.broadcasted_iota(jnp.int32, (BLK, BLK), 0)
        allowed = (key_pos >= starts) & (key_pos <= lane_pos)
        bias[j] = jnp.where(allowed, 0.0, -1e30)
        kt_buf[j] = kv_ref[j, :, :HEAD].T
        vt_buf[j] = kv_ref[j, :, HEAD:].T
        return carry

    lax.fori_loop(low, WIN, prepare, 0)

    def one_head(head, carry):
        lanes = pl.ds(pl.multiple_of(head * HEAD, HEAD), HEAD)
        q = q_ref[:, lanes]
        cot = jnp.where(keep > 0, cot_ref[:, lanes], jnp.zeros((), BF16))
        qt = q.T
        ct = cot.T

        def score(j, top):
            s = jnp.dot(kv_ref[j, :, :HEAD], qt, preferred_element_type=F32)
            s = s * (SCALE * LOG2E) + bias[j]
            s_buf[j] = s
            return jnp.maximum(top, jnp.max(s, axis=0, keepdims=True))

        top = lax.fori_loop(low, WIN, score, jnp.full((1, BLK), -1e30, F32))

        def weigh(j, state):
            mass, out = state
            p = jnp.exp2(s_buf[j] - top)
            s_buf[j] = p
            mass = mass + jnp.sum(p, axis=0, keepdims=True)
            out = out + jnp.dot(vt_buf[j], p.astype(BF16), preferred_element_type=F32)
            return (mass, out)

        mass, out = lax.fori_loop(
            low, WIN, weigh, (jnp.zeros((1, BLK), F32), jnp.zeros((HEAD, BLK), F32))
        )
        inverse = 1.0 / mass
        out_half = (out * inverse).astype(BF16)
        o_ref[:, lanes] = out_half.T
        delta = jnp.sum(ct.astype(F32) * out_half.astype(F32), axis=0, keepdims=True)

        def back(j, dqt):
            p = s_buf[j] * inverse
            dp = jnp.dot(kv_ref[j, :, HEAD:], ct, preferred_element_type=F32)
            ds = (p * (dp - delta)).astype(BF16)
            dkv_acc[j, :, :HEAD] += jnp.dot(ds, q, preferred_element_type=F32)
            dkv_acc[j, :, HEAD:] += jnp.dot(p.astype(BF16), cot, preferred_element_type=F32)
            return dqt + jnp.dot(kt_buf[j], ds, preferred_element_type=F32)

        dqt = lax.fori_loop(low, WIN, back, jnp.zeros((HEAD, BLK), F32))
        dq_ref[:, lanes] = (dqt * SCALE).astype(BF16).T
        return carry

    lax.fori_loop(0, HEADS, one_head, 0)
    for j in range(WIN):
        dkv_ref[j, :, :HEAD] = (dkv_acc[j, :, :HEAD] * SCALE).astype(BF16)
        dkv_ref[j, :, HEAD:] = dkv_acc[j, :, HEAD:].astype(BF16)


def cut(dims, axis, index, half):
    return tuple(index if d == axis else slice(None) for d in dims) + (half,)


def gradient_kernel(
    x_ref, dq_ref, dkv_ref, w_hbm, ig_ref, wg_ref,
    w_vmem, dproj, dkv_in,
    d00, d01, d02, d10, d11, d12, d20, d21, d22,
    b00, b01, b02, b10, b11, b12, b20, b21, b22,
    load_sem, pair_send, pair_recv, kv_send, kv_recv, ring_send, ring_recv,
):
    data = ((d00, d01, d02), (d10, d11, d12), (d20, d21, d22))
    bufs = ((b00, b01, b02), (b10, b11, b12), (b20, b21, b22))
    dp = lax.axis_index("dp")
    seq = lax.axis_index("seq")
    at = place()
    load = pltpu.make_async_copy(w_hbm, w_vmem, load_sem)
    load.start()
    partner = device(moved(at, "c", 1))
    far_y = moved(at, "y", 3 - 2 * lax.rem(at["y"], 2))
    ring = [device(there) for there in (moved(at, "z", 1), moved(at, "z", 3), far_y)]
    sem = pltpu.get_barrier_semaphore()
    everyone = seq_peers() + ring + [partner]
    for there in everyone:
        pl.semaphore_signal(sem, inc=1, device_id=there, device_id_type=MESH)
    pl.semaphore_wait(sem, len(everyone))

    def pair_copy(index, src, columns):
        return pltpu.make_async_remote_copy(
            src_ref=src,
            dst_ref=dproj.at[pl.ds(BLK, BLK), columns],
            send_sem=pair_send.at[index],
            recv_sem=pair_recv.at[index],
            device_id=partner,
            device_id_type=MESH,
        )

    def kv_copy(step):
        return pltpu.make_async_remote_copy(
            src_ref=dkv_ref.at[WIN - 1 - step],
            dst_ref=dkv_in.at[step - 1],
            send_sem=kv_send.at[step - 1],
            recv_sem=kv_recv.at[step - 1],
            device_id=(dp, lax.rem(seq + SEQN - step, SEQN)),
            device_id_type=MESH,
        )

    for step in range(1, WIN):
        @pl.when(seq >= step)
        def _(step=step):
            kv_copy(step).start()
    pair_q = pair_copy(0, dq_ref, pl.ds(0, QW))
    pair_q.start()
    dproj[pl.ds(0, BLK), :QW] = dq_ref[...]

    def ring_copy(color, stage, buf, src, there):
        k = (color * 3 + stage) * 6 + buf
        return pltpu.make_async_remote_copy(
            src_ref=src,
            dst_ref=bufs[color][stage].at[buf],
            send_sem=ring_send.at[k],
            recv_sem=ring_recv.at[k],
            device_id=device(there),
            device_id_type=MESH,
        )

    def stage_of(color, stage):
        order = COLORS[color][2]
        dims = [d for d in "zyx" if d in order[stage:]]
        axis = order[stage]
        me = at[axis]
        return (
            dims, axis, me,
            lax.rem(me + 1, 4), lax.rem(me + 2, 4), lax.rem(me + 3, 4),
            moved(at, axis, 1), moved(at, axis, 3),
        )

    started = []

    def open_stage(color, stage):
        dims, axis, me, right, across, left, to_right, to_left = stage_of(color, stage)
        src = data[color][stage]
        for buf, index, half, there in (
            (0, across, 0, to_right),
            (1, across, 1, to_left),
            (3, right, 1, to_right),
            (4, left, 0, to_left),
        ):
            copy = ring_copy(color, stage, buf, src.at[cut(dims, axis, index, half)], there)
            copy.start()
            started.append(copy)

    def pass_on(color, stage):
        dims, axis, me, right, across, left, to_right, to_left = stage_of(color, stage)
        src = data[color][stage]
        for first, buf, index, half, there in ((0, 2, right, 0, to_right), (1, 5, left, 1, to_left)):
            where = cut(dims, axis, index, half)
            ring_copy(color, stage, first, src.at[where], there).wait_recv()
            src[where] = (src[where].astype(F32) + bufs[color][stage][first].astype(F32)).astype(BF16)
            copy = ring_copy(color, stage, buf, src.at[where], there)
            copy.start()
            started.append(copy)

    def close_stage(color, stage):
        dims, axis, me, right, across, left, to_right, to_left = stage_of(color, stage)
        src, got = data[color][stage], bufs[color][stage]
        for half in (0, 1):
            where = cut(dims, axis, me, half)
            total = src[where].astype(F32)
            for buf in (2 + half, 4 + half):
                ring_copy(color, stage, buf, src.at[where], to_right).wait_recv()
                total = total + got[buf].astype(F32)
            if stage < 2:
                data[color][stage + 1][(slice(None),) * (len(dims) - 1) + (half,)] = total.astype(BF16)
            else:
                first, width, _ = COLORS[color]
                wg_ref[16 * half : 16 * half + 16, first : first + width] = total

    def multiply(color):
        first, width, _ = COLORS[color]

        def body(z, carry):
            rows = pl.ds(pl.multiple_of(z * 512, 512), 512)
            part = jnp.dot(x_ref[rows, :], dproj[:, first : first + width], preferred_element_type=F32)
            data[color][0][z] = part.astype(BF16).reshape(4, 4, 2, 16, width)
            return carry

        lax.fori_loop(0, 4, body, 0)

    pair_q.wait_recv()
    for color in (0, 1):
        multiply(color)
        open_stage(color, 0)

    total = dkv_ref[WIN - 1].astype(F32)
    for step in range(1, WIN):
        @pl.when(seq + step < SEQN)
        def _(step=step):
            kv_copy(step).wait_recv()

        @pl.when(seq + step >= SEQN)
        def _(step=step):
            dkv_in[step - 1] = jnp.zeros((BLK, 2 * HEAD), BF16)

        total = total + dkv_in[step - 1].astype(F32)
    dproj[pl.ds(0, BLK), QW:] = total.astype(BF16)
    pair_kv = pair_copy(1, dproj.at[pl.ds(0, BLK), pl.ds(QW, 2 * HEAD)], pl.ds(QW, 2 * HEAD))
    pair_kv.start()
    pair_kv.wait_recv()
    multiply(2)
    open_stage(2, 0)

    load.wait()

    def grad_chunk(n, carry):
        rows = pl.ds(pl.multiple_of(n * 512, 512), 512)
        ig_ref[:, rows] = lax.dot_general(
            dproj[pl.ds(0, BLK), :], w_vmem[rows, :], NT, preferred_element_type=F32
        ).astype(BF16)
        return carry

    lax.fori_loop(0, 8, grad_chunk, 0)

    for stage in range(3):
        for color in range(3):
            pass_on(color, stage)
        for color in range(3):
            close_stage(color, stage)
            if stage < 2:
                open_stage(color, stage + 1)
    for copy in started:
        copy.wait_send()
    pair_q.wait_send()
    pair_kv.wait_send()
    for step in range(1, WIN):
        @pl.when(seq >= step)
        def _(step=step):
            kv_copy(step).wait_send()


VM = pl.BlockSpec(memory_space=pltpu.VMEM)
SM = pl.BlockSpec(memory_space=pltpu.SMEM)
ANY = pl.BlockSpec(memory_space=pl.ANY)
DMA = pltpu.SemaphoreType.DMA
LIMIT = 60 * 1024 * 1024


def shape(dims, kind=BF16):
    return jax.ShapeDtypeStruct(dims, kind)


def shards(inputs, weights, cotangent, doc_lengths, kept_flags):
    tokens = inputs[0]
    full_weights = lax.all_gather(weights, "dp", axis=0, tiled=True)

    core = lax.rem(lax.axis_index("dp"), 2)
    strips = tokens.reshape(BLK, 8, 2, 256).transpose(2, 1, 3, 0)
    mine = lax.dynamic_index_in_dim(strips, core, 0, keepdims=False).reshape(2048, BLK)
    other = lax.dynamic_index_in_dim(strips, 1 - core, 0, keepdims=False).reshape(2048, BLK)
    other = lax.ppermute(other, "dp", [(i, i ^ 1) for i in range(16)])
    columns = jnp.concatenate([mine, other], axis=1)

    queries, pairs = pl.pallas_call(
        project_kernel,
        out_shape=(shape((BLK, QW)), shape((WIN, BLK, 2 * HEAD))),
        in_specs=[VM, ANY],
        out_specs=(VM, VM),
        scratch_shapes=[
            pltpu.VMEM((D, COLS), BF16), DMA((5,)), DMA((WIN - 1,)), DMA((WIN - 1,)),
        ],
        compiler_params=pltpu.CompilerParams(collective_id=0, has_side_effects=True, vmem_limit_bytes=LIMIT),
        name="project",
    )(tokens, full_weights)

    attention, query_grads, pair_grads = pl.pallas_call(
        attend_kernel,
        out_shape=(shape((BLK, QW)), shape((BLK, QW)), shape((WIN, BLK, 2 * HEAD))),
        in_specs=[SM, SM, VM, VM, VM],
        out_specs=(VM, VM, VM),
        scratch_shapes=[
            pltpu.VMEM((WIN, BLK, BLK), F32),
            pltpu.VMEM((WIN, BLK, BLK), F32),
            pltpu.VMEM((WIN, BLK, 2 * HEAD), F32),
            pltpu.VMEM((WIN, HEAD, BLK), BF16),
            pltpu.VMEM((WIN, HEAD, BLK), BF16),
        ],
        compiler_params=pltpu.CompilerParams(vmem_limit_bytes=LIMIT),
        name="attend",
    )(doc_lengths, kept_flags, queries, pairs, cotangent[0])

    held, received = [], []
    for _, width, order in COLORS:
        for stage in range(3):
            dims = (4,) * (3 - stage)
            held.append(pltpu.VMEM(dims + (2, 16, width), BF16))
            received.append(pltpu.VMEM((6,) + dims[1:] + (16, width), BF16))
    inputs_grad, weights_grad = pl.pallas_call(
        gradient_kernel,
        out_shape=(shape((BLK, D)), shape((32, COLS), F32)),
        in_specs=[VM, VM, VM, ANY],
        out_specs=(VM, VM),
        scratch_shapes=[
            pltpu.VMEM((D, COLS), BF16),
            pltpu.VMEM((2 * BLK, COLS), BF16),
            pltpu.VMEM((WIN - 1, BLK, 2 * HEAD), BF16),
        ]
        + held
        + received
        + [DMA, DMA((2,)), DMA((2,)), DMA((WIN - 1,)), DMA((WIN - 1,)), DMA((54,)), DMA((54,))],
        compiler_params=pltpu.CompilerParams(collective_id=1, has_side_effects=True, vmem_limit_bytes=LIMIT),
        name="gradients",
    )(columns, query_grads, pair_grads, full_weights)
    return (attention[None], inputs_grad[None], weights_grad)


def solution(mesh):
    in_specs = (
        P("dp", "seq", None),
        P("dp", None),
        P("dp", "seq", None),
        P("dp", None),
        P("dp", None),
    )
    out_specs = (P("dp", "seq", None), P("dp", "seq", None), P(("dp", "seq"), None))
    return jax.shard_map(shards, mesh=mesh, in_specs=in_specs, out_specs=out_specs, check_vma=False)
```

```python
import math

import jax
import jax.numpy as jnp
from jax import lax
from jax.experimental import pallas as pl
from jax.experimental.pallas import tpu as pltpu
from jax.sharding import PartitionSpec as P

MESH = pl.DeviceIdType.MESH
HEAD = 128
HEADS = 8
BLK = 256
WIN = 5
D = 4096
QW = 1024
COLS = 1280
NDOC = 8
SEQN = 8
SCALE = 1.0 / math.sqrt(HEAD)
LOG2E = math.log2(math.e)
F32 = jnp.float32
BF16 = jnp.bfloat16
NT = (((1,), (1,)), ((), ()))
COLORS = ((0, 512, "xyz"), (512, 384, "yzx"), (896, 384, "zxy"))


def place():
    dp = lax.axis_index("dp")
    seq = lax.axis_index("seq")
    z = lax.div(dp, 4)
    y = lax.rem(lax.div(dp, 2), 2) * 2 + lax.div(seq, 4)
    return {"z": z, "y": y, "x": lax.rem(seq, 4), "c": lax.rem(dp, 2)}


def device(at):
    dp = at["z"] * 4 + lax.div(at["y"], 2) * 2 + at["c"]
    return (dp, lax.rem(at["y"], 2) * 4 + at["x"])


def moved(at, axis, step):
    count = 2 if axis == "c" else 4
    there = dict(at)
    there[axis] = lax.rem(at[axis] + step, count)
    return there


def barrier_with(devices):
    sem = pltpu.get_barrier_semaphore()
    for there in devices:
        pl.semaphore_signal(sem, inc=1, device_id=there, device_id_type=MESH)
    pl.semaphore_wait(sem, len(devices))


def seq_peers():
    dp = lax.axis_index("dp")
    seq = lax.axis_index("seq")
    return [(dp, lax.rem(seq + step, SEQN)) for step in range(1, SEQN)]


def everyone(at):
    far_y = moved(at, "y", 3 - 2 * lax.rem(at["y"], 2))
    ring = [device(there) for there in (moved(at, "z", 1), moved(at, "z", 3), far_y)]
    return seq_peers() + ring + [device(moved(at, "c", 1))]


def spread(k):
    return k + lax.div(k, 2) * (1 - 2 * lax.rem(k, 2))


Z_RIGHT, Z_LEFT, Z_FAR, Y_FAR, X_RIGHT, X_LEFT, X_FAR_RIGHT, X_FAR_LEFT, PAIR, STRIP, PEER = (
    0, 4, 8, 12, 16, 20, 24, 28, 32, 40, 48
)


def project_kernel(
    x_ref, w_hbm, q_ref, kv_ref, w_out, xt_ref, w_all, acc, x_other, load_sem, store_sem, send_sem, recv_sem
):
    dp = lax.axis_index("dp")
    seq = lax.axis_index("seq")
    at = place()
    z, x, c = at["z"], at["x"], at["c"]
    half_y = lax.rem(lax.div(dp, 2), 2)
    partner = device(moved(at, "c", 1))
    far_y = device(moved(at, "y", 3 - 2 * lax.rem(at["y"], 2)))
    z_right, z_left = device(moved(at, "z", 1)), device(moved(at, "z", 3))
    x_right, x_left = device(moved(at, "x", 1)), device(moved(at, "x", 3))

    def shard(step, other_y=0, other_c=0):
        zz = lax.rem(z + step, 4)
        yy = lax.rem(half_y + other_y, 2)
        return zz * 4 + yy * 2 + lax.rem(c + other_c, 2)

    def quarter(i):
        return lax.rem(x + i, 4)

    def copy(slot, ref, there):
        return pltpu.make_async_remote_copy(
            src_ref=ref, dst_ref=ref, send_sem=send_sem.at[slot], recv_sem=recv_sem.at[slot],
            device_id=there, device_id_type=MESH,
        )

    def to_z_right(i):
        return copy(Z_RIGHT + i, w_all.at[dp, quarter(i)], z_right)

    def to_z_left(i):
        return copy(Z_LEFT + i, w_all.at[dp, quarter(i)], z_left)

    def to_z_far(i):
        if i < 2:
            return copy(Z_FAR + i, w_all.at[shard(3), quarter(i)], z_right)
        return copy(Z_FAR + i, w_all.at[shard(1), quarter(i)], z_left)

    def to_far_y(k):
        return copy(Y_FAR + k, w_all.at[shard(spread(k)), x], far_y)

    def to_x_right(k):
        return copy(X_RIGHT + k, w_all.at[shard(spread(k), 1), x], x_right)

    def to_x_left(k):
        return copy(X_LEFT + k, w_all.at[shard(spread(k), 1), x], x_left)

    def to_x_far_right(k):
        return copy(X_FAR_RIGHT + k, w_all.at[shard(spread(k), 1), quarter(3), 0], x_right)

    def to_x_far_left(k):
        return copy(X_FAR_LEFT + k, w_all.at[shard(spread(k), 1), quarter(1), 1], x_left)

    def to_pair(k, other_y):
        return copy(PAIR + 4 * other_y + k, w_all.at[shard(spread(k), other_y)], partner)

    def strip(j):
        return pltpu.make_async_remote_copy(
            src_ref=x_ref.at[:, pl.ds(pl.multiple_of(j * 512 + (1 - c) * 256, 256), 256)],
            dst_ref=x_other.at[j],
            send_sem=send_sem.at[STRIP + j], recv_sem=recv_sem.at[STRIP + j],
            device_id=partner, device_id_type=MESH,
        )

    def keep(s):
        return pltpu.make_async_copy(w_all.at[s], w_out.at[s], store_sem.at[s])

    def multiply(s):
        keep(s).start()
        lanes = pl.ds(pl.multiple_of(s * 256, 256), 256)
        acc[...] += jnp.dot(
            x_ref[:, lanes], w_all[s].reshape(256, COLS), preferred_element_type=F32
        )

    own = pltpu.make_async_copy(w_hbm, w_all.at[dp], load_sem)
    own.start()
    barrier_with(everyone(at))
    own.wait()
    sent = []

    def send(item):
        item.start()
        sent.append(item)

    for i in range(4):
        send(to_z_right(i))
        send(to_z_left(i))
        if i == 0:
            send(to_far_y(0))
    send(to_pair(0, 0))
    for j in range(8):
        send(strip(j))
    acc[...] = jnp.zeros_like(acc)

    def turn_own(j, carry):
        rows = pl.ds(pl.multiple_of(j * 256, 256), 256)
        lanes = pl.ds(pl.multiple_of(j * 512 + c * 256, 256), 256)
        xt_ref[rows, :256] = x_ref[:, lanes].T
        return carry

    lax.fori_loop(0, 8, turn_own, 0)
    to_z_right(0).wait_recv()
    send(to_far_y(2))
    send(to_z_far(0))
    to_z_left(0).wait_recv()
    send(to_far_y(1))
    for k in range(3):
        to_far_y(k).wait_recv()
        send(to_x_right(k))
        send(to_x_left(k))
    to_z_right(1).wait_recv()
    send(to_z_far(1))

    def pass_x(k):
        to_x_right(k).wait_recv()
        send(to_x_far_right(k))
        to_x_left(k).wait_recv()
        send(to_x_far_left(k))

    pass_x(0)
    to_z_far(0).wait_recv()
    send(to_far_y(3))

    for j in range(8):
        strip(j).wait_recv()

    def turn_other(j, carry):
        rows = pl.ds(pl.multiple_of(j * 256, 256), 256)
        xt_ref[rows, 256:] = x_other[j].T
        return carry

    lax.fori_loop(0, 8, turn_other, 0)
    to_z_left(1).wait_recv()
    for i in (2, 3):
        to_z_left(i).wait_recv()
        send(to_z_far(i))
    send(to_pair(1, 0))
    for i in (2, 3):
        to_z_right(i).wait_recv()
    send(to_pair(2, 0))
    pass_x(1)
    to_far_y(3).wait_recv()
    send(to_x_right(3))
    send(to_x_left(3))
    pass_x(2)

    def near(k, carry):
        multiply(shard(spread(k)))
        to_pair(k, 0).wait_recv()
        multiply(shard(spread(k), 0, 1))
        return carry

    lax.fori_loop(0, 3, near, 0)
    for i in (1, 2, 3):
        to_z_far(i).wait_recv()
    send(to_pair(3, 0))
    pass_x(3)
    lax.fori_loop(3, 4, near, 0)

    def far(k, carry):
        to_x_far_right(k).wait_recv()
        to_x_far_left(k).wait_recv()
        to_pair(k, 1).start()
        multiply(shard(spread(k), 1))
        to_pair(k, 1).wait_recv()
        multiply(shard(spread(k), 1, 1))
        return carry

    lax.fori_loop(0, 4, far, 0)

    kv_ref[WIN - 1] = acc[:, QW:].astype(BF16)

    def to_peer(step):
        return pltpu.make_async_remote_copy(
            src_ref=kv_ref.at[WIN - 1],
            dst_ref=kv_ref.at[WIN - 1 - step],
            send_sem=send_sem.at[PEER + step - 1],
            recv_sem=recv_sem.at[PEER + step - 1],
            device_id=(dp, lax.rem(seq + step, SEQN)),
            device_id_type=MESH,
        )

    for step in range(1, WIN):
        @pl.when(seq + step < SEQN)
        def _(step=step):
            to_peer(step).start()

        @pl.when(seq < step)
        def _(step=step):
            kv_ref[WIN - 1 - step] = jnp.zeros((BLK, 2 * HEAD), BF16)

    q_ref[...] = acc[:, :QW].astype(BF16)
    for item in sent:
        item.wait_send()

    def finish(k, carry):
        to_pair(k, 1).wait_send()
        return carry

    lax.fori_loop(0, 4, finish, 0)

    def stored(s, carry):
        keep(s).wait()
        return carry

    lax.fori_loop(0, 16, stored, 0)
    for step in range(1, WIN):
        @pl.when(seq >= step)
        def _(step=step):
            to_peer(step).wait_recv()

        @pl.when(seq + step < SEQN)
        def _(step=step):
            to_peer(step).wait_send()


def attend_kernel(
    len_ref, flag_ref, q_ref, kv_ref, cot_ref, o_ref, dq_ref, dkv_ref, s_buf, bias, dkv_acc, kt_buf, vt_buf
):
    seq = lax.axis_index("seq")
    row0 = seq * BLK
    lane_pos = row0 + lax.broadcasted_iota(jnp.int32, (1, BLK), 1)
    sub_pos = row0 + lax.broadcasted_iota(jnp.int32, (BLK, HEAD), 0)
    first_start = jnp.int32(0)
    doc_start = jnp.int32(0)
    starts = jnp.zeros((1, BLK), jnp.int32)
    keep = jnp.zeros((BLK, HEAD), jnp.int32)
    for doc in range(NDOC):
        doc_end = doc_start + len_ref[0, doc]
        first_start = jnp.where((row0 >= doc_start) & (row0 < doc_end), doc_start, first_start)
        starts = jnp.where((lane_pos >= doc_start) & (lane_pos < doc_end), doc_start, starts)
        keep = jnp.where((sub_pos >= doc_start) & (sub_pos < doc_end), flag_ref[0, doc], keep)
        doc_start = doc_end
    base = seq - (WIN - 1)
    low = lax.div(first_start, BLK) - base
    dkv_acc[...] = jnp.zeros_like(dkv_acc)

    def prepare(j, carry):
        key_pos = (base + j) * BLK + lax.broadcasted_iota(jnp.int32, (BLK, BLK), 0)
        allowed = (key_pos >= starts) & (key_pos <= lane_pos)
        bias[j] = jnp.where(allowed, 0.0, -1e30)
        kt_buf[j] = kv_ref[j, :, :HEAD].T
        vt_buf[j] = kv_ref[j, :, HEAD:].T
        return carry

    lax.fori_loop(low, WIN, prepare, 0)

    def one_head(head, carry):
        lanes = pl.ds(pl.multiple_of(head * HEAD, HEAD), HEAD)
        q = q_ref[:, lanes]
        cot = jnp.where(keep > 0, cot_ref[:, lanes], jnp.zeros((), BF16))
        qt = q.T
        ct = cot.T

        def score(j, top):
            s = jnp.dot(kv_ref[j, :, :HEAD], qt, preferred_element_type=F32)
            s = s * (SCALE * LOG2E) + bias[j]
            s_buf[j] = s
            return jnp.maximum(top, jnp.max(s, axis=0, keepdims=True))

        top = lax.fori_loop(low, WIN, score, jnp.full((1, BLK), -1e30, F32))

        def weigh(j, state):
            mass, out = state
            p = jnp.exp2(s_buf[j] - top)
            s_buf[j] = p
            mass = mass + jnp.sum(p, axis=0, keepdims=True)
            out = out + jnp.dot(vt_buf[j], p.astype(BF16), preferred_element_type=F32)
            return (mass, out)

        mass, out = lax.fori_loop(
            low, WIN, weigh, (jnp.zeros((1, BLK), F32), jnp.zeros((HEAD, BLK), F32))
        )
        inverse = 1.0 / mass
        out_half = (out * inverse).astype(BF16)
        o_ref[:, lanes] = out_half.T
        delta = jnp.sum(ct.astype(F32) * out_half.astype(F32), axis=0, keepdims=True)

        def back(j, dqt):
            p = s_buf[j] * inverse
            dp = jnp.dot(kv_ref[j, :, HEAD:], ct, preferred_element_type=F32)
            ds = (p * (dp - delta)).astype(BF16)
            dkv_acc[j, :, :HEAD] += jnp.dot(ds, q, preferred_element_type=F32)
            dkv_acc[j, :, HEAD:] += jnp.dot(p.astype(BF16), cot, preferred_element_type=F32)
            return dqt + jnp.dot(kt_buf[j], ds, preferred_element_type=F32)

        dqt = lax.fori_loop(low, WIN, back, jnp.zeros((HEAD, BLK), F32))
        dq_ref[:, lanes] = (dqt * SCALE).astype(BF16).T
        return carry

    lax.fori_loop(0, HEADS, one_head, 0)
    for j in range(WIN):
        dkv_ref[j, :, :HEAD] = (dkv_acc[j, :, :HEAD] * SCALE).astype(BF16)
        dkv_ref[j, :, HEAD:] = dkv_acc[j, :, HEAD:].astype(BF16)


def cut(dims, axis, index, half):
    return tuple(index if d == axis else slice(None) for d in dims) + (half,)


def gradient_kernel(
    x_ref, dq_ref, dkv_ref, w_hbm, ig_ref, wg_ref,
    w_vmem, dproj, dkv_in,
    d00, d01, d02, d10, d11, d12, d20, d21, d22,
    b00, b01, b02, b10, b11, b12, b20, b21, b22,
    load_sem, pair_send, pair_recv, kv_send, kv_recv, ring_send, ring_recv,
):
    data = ((d00, d01, d02), (d10, d11, d12), (d20, d21, d22))
    bufs = ((b00, b01, b02), (b10, b11, b12), (b20, b21, b22))
    dp = lax.axis_index("dp")
    seq = lax.axis_index("seq")
    at = place()
    load = pltpu.make_async_copy(w_hbm, w_vmem, load_sem)
    load.start()
    partner = device(moved(at, "c", 1))
    barrier_with(everyone(at))

    def pair_copy(index, src, columns):
        return pltpu.make_async_remote_copy(
            src_ref=src,
            dst_ref=dproj.at[pl.ds(BLK, BLK), columns],
            send_sem=pair_send.at[index],
            recv_sem=pair_recv.at[index],
            device_id=partner,
            device_id_type=MESH,
        )

    def kv_copy(step):
        return pltpu.make_async_remote_copy(
            src_ref=dkv_ref.at[WIN - 1 - step],
            dst_ref=dkv_in.at[step - 1],
            send_sem=kv_send.at[step - 1],
            recv_sem=kv_recv.at[step - 1],
            device_id=(dp, lax.rem(seq + SEQN - step, SEQN)),
            device_id_type=MESH,
        )

    for step in range(1, WIN):
        @pl.when(seq >= step)
        def _(step=step):
            kv_copy(step).start()
    pair_q = pair_copy(0, dq_ref, pl.ds(0, QW))
    pair_q.start()
    dproj[pl.ds(0, BLK), :QW] = dq_ref[...]

    def ring_copy(color, stage, buf, src, there):
        k = (color * 3 + stage) * 6 + buf
        return pltpu.make_async_remote_copy(
            src_ref=src,
            dst_ref=bufs[color][stage].at[buf],
            send_sem=ring_send.at[k],
            recv_sem=ring_recv.at[k],
            device_id=device(there),
            device_id_type=MESH,
        )

    def stage_of(color, stage):
        order = COLORS[color][2]
        dims = [d for d in "zyx" if d in order[stage:]]
        axis = order[stage]
        me = at[axis]
        return (
            dims, axis, me,
            lax.rem(me + 1, 4), lax.rem(me + 2, 4), lax.rem(me + 3, 4),
            moved(at, axis, 1), moved(at, axis, 3),
        )

    started = []

    def open_stage(color, stage):
        dims, axis, me, right, across, left, to_right, to_left = stage_of(color, stage)
        src = data[color][stage]
        for buf, index, half, there in (
            (0, across, 0, to_right),
            (1, across, 1, to_left),
            (3, right, 1, to_right),
            (4, left, 0, to_left),
        ):
            copy = ring_copy(color, stage, buf, src.at[cut(dims, axis, index, half)], there)
            copy.start()
            started.append(copy)

    def pass_on(color, stage):
        dims, axis, me, right, across, left, to_right, to_left = stage_of(color, stage)
        src = data[color][stage]
        for first, buf, index, half, there in ((0, 2, right, 0, to_right), (1, 5, left, 1, to_left)):
            where = cut(dims, axis, index, half)
            ring_copy(color, stage, first, src.at[where], there).wait_recv()
            src[where] = (src[where].astype(F32) + bufs[color][stage][first].astype(F32)).astype(BF16)
            copy = ring_copy(color, stage, buf, src.at[where], there)
            copy.start()
            started.append(copy)

    def close_stage(color, stage):
        dims, axis, me, right, across, left, to_right, to_left = stage_of(color, stage)
        src, got = data[color][stage], bufs[color][stage]
        for half in (0, 1):
            where = cut(dims, axis, me, half)
            total = src[where].astype(F32)
            for buf in (2 + half, 4 + half):
                ring_copy(color, stage, buf, src.at[where], to_right).wait_recv()
                total = total + got[buf].astype(F32)
            if stage < 2:
                data[color][stage + 1][(slice(None),) * (len(dims) - 1) + (half,)] = total.astype(BF16)
            else:
                first, width, _ = COLORS[color]
                wg_ref[16 * half : 16 * half + 16, first : first + width] = total

    def multiply(color):
        first, width, _ = COLORS[color]

        def body(z, carry):
            rows = pl.ds(pl.multiple_of(z * 512, 512), 512)
            part = jnp.dot(x_ref[rows, :], dproj[:, first : first + width], preferred_element_type=F32)
            data[color][0][z] = part.astype(BF16).reshape(4, 4, 2, 16, width)
            return carry

        lax.fori_loop(0, 4, body, 0)

    pair_q.wait_recv()
    for color in (0, 1):
        multiply(color)
        open_stage(color, 0)

    total = dkv_ref[WIN - 1].astype(F32)
    for step in range(1, WIN):
        @pl.when(seq + step < SEQN)
        def _(step=step):
            kv_copy(step).wait_recv()

        @pl.when(seq + step >= SEQN)
        def _(step=step):
            dkv_in[step - 1] = jnp.zeros((BLK, 2 * HEAD), BF16)

        total = total + dkv_in[step - 1].astype(F32)
    dproj[pl.ds(0, BLK), QW:] = total.astype(BF16)
    pair_kv = pair_copy(1, dproj.at[pl.ds(0, BLK), pl.ds(QW, 2 * HEAD)], pl.ds(QW, 2 * HEAD))
    pair_kv.start()
    pair_kv.wait_recv()
    multiply(2)
    open_stage(2, 0)

    load.wait()

    def grad_chunk(n, carry):
        rows = pl.ds(pl.multiple_of(n * 512, 512), 512)
        ig_ref[:, rows] = lax.dot_general(
            dproj[pl.ds(0, BLK), :], w_vmem[rows, :], NT, preferred_element_type=F32
        ).astype(BF16)
        return carry

    lax.fori_loop(0, 8, grad_chunk, 0)

    for stage in range(3):
        for color in range(3):
            pass_on(color, stage)
        for color in range(3):
            close_stage(color, stage)
            if stage < 2:
                open_stage(color, stage + 1)
    for copy in started:
        copy.wait_send()
    pair_q.wait_send()
    pair_kv.wait_send()
    for step in range(1, WIN):
        @pl.when(seq >= step)
        def _(step=step):
            kv_copy(step).wait_send()


VM = pl.BlockSpec(memory_space=pltpu.VMEM)
SM = pl.BlockSpec(memory_space=pltpu.SMEM)
ANY = pl.BlockSpec(memory_space=pl.ANY)
DMA = pltpu.SemaphoreType.DMA
LIMIT = 60 * 1024 * 1024


def shape(dims, kind=BF16):
    return jax.ShapeDtypeStruct(dims, kind)


def shards(inputs, weights, cotangent, doc_lengths, kept_flags):
    tokens = inputs[0]
    queries, pairs, full_weights, columns = pl.pallas_call(
        project_kernel,
        out_shape=(
            shape((BLK, QW)), shape((WIN, BLK, 2 * HEAD)), shape((16, 4, 2, 32, COLS)), shape((2048, 2 * BLK)),
        ),
        in_specs=[VM, ANY],
        out_specs=(VM, VM, ANY, VM),
        scratch_shapes=[
            pltpu.VMEM((16, 4, 2, 32, COLS), BF16),
            pltpu.VMEM((BLK, COLS), F32),
            pltpu.VMEM((8, BLK, 256), BF16),
            DMA, DMA((16,)), DMA((52,)), DMA((52,)),
        ],
        compiler_params=pltpu.CompilerParams(collective_id=0, has_side_effects=True, vmem_limit_bytes=LIMIT),
        name="project",
    )(tokens, weights.reshape(4, 2, 32, COLS))
    full_weights = full_weights.reshape(D, COLS)

    attention, query_grads, pair_grads = pl.pallas_call(
        attend_kernel,
        out_shape=(shape((BLK, QW)), shape((BLK, QW)), shape((WIN, BLK, 2 * HEAD))),
        in_specs=[SM, SM, VM, VM, VM],
        out_specs=(VM, VM, VM),
        scratch_shapes=[
            pltpu.VMEM((WIN, BLK, BLK), F32),
            pltpu.VMEM((WIN, BLK, BLK), F32),
            pltpu.VMEM((WIN, BLK, 2 * HEAD), F32),
            pltpu.VMEM((WIN, HEAD, BLK), BF16),
            pltpu.VMEM((WIN, HEAD, BLK), BF16),
        ],
        compiler_params=pltpu.CompilerParams(vmem_limit_bytes=LIMIT),
        name="attend",
    )(doc_lengths, kept_flags, queries, pairs, cotangent[0])

    held, received = [], []
    for _, width, order in COLORS:
        for stage in range(3):
            dims = (4,) * (3 - stage)
            held.append(pltpu.VMEM(dims + (2, 16, width), BF16))
            received.append(pltpu.VMEM((6,) + dims[1:] + (16, width), BF16))
    inputs_grad, weights_grad = pl.pallas_call(
        gradient_kernel,
        out_shape=(shape((BLK, D)), shape((32, COLS), F32)),
        in_specs=[VM, VM, VM, ANY],
        out_specs=(VM, VM),
        scratch_shapes=[
            pltpu.VMEM((D, COLS), BF16),
            pltpu.VMEM((2 * BLK, COLS), BF16),
            pltpu.VMEM((WIN - 1, BLK, 2 * HEAD), BF16),
        ]
        + held
        + received
        + [DMA, DMA((2,)), DMA((2,)), DMA((WIN - 1,)), DMA((WIN - 1,)), DMA((54,)), DMA((54,))],
        compiler_params=pltpu.CompilerParams(collective_id=1, has_side_effects=True, vmem_limit_bytes=LIMIT),
        name="gradients",
    )(columns, query_grads, pair_grads, full_weights)
    return (attention[None], inputs_grad[None], weights_grad)


def solution(mesh):
    in_specs = (
        P("dp", "seq", None),
        P("dp", None),
        P("dp", "seq", None),
        P("dp", None),
        P("dp", None),
    )
    out_specs = (P("dp", "seq", None), P("dp", "seq", None), P(("dp", "seq"), None))
    return jax.shard_map(shards, mesh=mesh, in_specs=in_specs, out_specs=out_specs, check_vma=False)
```

```python
import math

import jax
import jax.numpy as jnp
from jax import lax
from jax.experimental import pallas as pl
from jax.experimental.pallas import tpu as pltpu
from jax.sharding import PartitionSpec as P

MESH = pl.DeviceIdType.MESH
HEAD = 128
HEADS = 8
BLK = 256
WIN = 5
D = 4096
QW = 1024
COLS = 1280
NDOC = 8
SEQN = 8
SCALE = 1.0 / math.sqrt(HEAD)
LOG2E = math.log2(math.e)
F32 = jnp.float32
BF16 = jnp.bfloat16
NT = (((1,), (1,)), ((), ()))
COLORS = ((0, 512, "xyz"), (512, 384, "yzx"), (896, 384, "zxy"))


def place():
    dp = lax.axis_index("dp")
    seq = lax.axis_index("seq")
    z = lax.div(dp, 4)
    y = lax.rem(lax.div(dp, 2), 2) * 2 + lax.div(seq, 4)
    return {"z": z, "y": y, "x": lax.rem(seq, 4), "c": lax.rem(dp, 2)}


def device(at):
    dp = at["z"] * 4 + lax.div(at["y"], 2) * 2 + at["c"]
    return (dp, lax.rem(at["y"], 2) * 4 + at["x"])


def moved(at, axis, step):
    count = 2 if axis == "c" else 4
    there = dict(at)
    there[axis] = lax.rem(at[axis] + step, count)
    return there


def barrier_with(devices):
    sem = pltpu.get_barrier_semaphore()
    for there in devices:
        pl.semaphore_signal(sem, inc=1, device_id=there, device_id_type=MESH)
    pl.semaphore_wait(sem, len(devices))


def seq_peers():
    dp = lax.axis_index("dp")
    seq = lax.axis_index("seq")
    return [(dp, lax.rem(seq + step, SEQN)) for step in range(1, SEQN)]


def everyone(at):
    far_y = moved(at, "y", 3 - 2 * lax.rem(at["y"], 2))
    ring = [device(there) for there in (moved(at, "z", 1), moved(at, "z", 3), far_y)]
    return seq_peers() + ring + [device(moved(at, "c", 1))]


def spread(k):
    return k + lax.div(k, 2) * (1 - 2 * lax.rem(k, 2))


Z_RIGHT, Z_LEFT, Z_FAR, Y_FAR, X_RIGHT, X_LEFT, X_FAR_RIGHT, X_FAR_LEFT, PAIR, STRIP, PEER = (
    0, 4, 8, 12, 16, 20, 24, 28, 32, 40, 48
)


def project_kernel(
    x_ref, w_hbm, q_ref, kv_ref, w_out, xt_ref, w_all, acc, x_other, load_sem, store_sem, send_sem, recv_sem
):
    dp = lax.axis_index("dp")
    seq = lax.axis_index("seq")
    at = place()
    z, x, c = at["z"], at["x"], at["c"]
    half_y = lax.rem(lax.div(dp, 2), 2)
    partner = device(moved(at, "c", 1))
    far_y = device(moved(at, "y", 3 - 2 * lax.rem(at["y"], 2)))
    z_right, z_left = device(moved(at, "z", 1)), device(moved(at, "z", 3))
    x_right, x_left = device(moved(at, "x", 1)), device(moved(at, "x", 3))

    def shard(step, other_y=0, other_c=0):
        zz = lax.rem(z + step, 4)
        yy = lax.rem(half_y + other_y, 2)
        return zz * 4 + yy * 2 + lax.rem(c + other_c, 2)

    def quarter(i):
        return lax.rem(x + i, 4)

    def copy(slot, ref, there):
        return pltpu.make_async_remote_copy(
            src_ref=ref, dst_ref=ref, send_sem=send_sem.at[slot], recv_sem=recv_sem.at[slot],
            device_id=there, device_id_type=MESH,
        )

    def to_z_right(i):
        return copy(Z_RIGHT + i, w_all.at[dp, quarter(i)], z_right)

    def to_z_left(i):
        return copy(Z_LEFT + i, w_all.at[dp, quarter(i)], z_left)

    def to_z_far(i):
        if i < 2:
            return copy(Z_FAR + i, w_all.at[shard(3), quarter(i)], z_right)
        return copy(Z_FAR + i, w_all.at[shard(1), quarter(i)], z_left)

    def to_far_y(k):
        return copy(Y_FAR + k, w_all.at[shard(spread(k)), x], far_y)

    def to_x_right(k):
        return copy(X_RIGHT + k, w_all.at[shard(spread(k), 1), x], x_right)

    def to_x_left(k):
        return copy(X_LEFT + k, w_all.at[shard(spread(k), 1), x], x_left)

    def to_x_far_right(k):
        return copy(X_FAR_RIGHT + k, w_all.at[shard(spread(k), 1), quarter(3), 0], x_right)

    def to_x_far_left(k):
        return copy(X_FAR_LEFT + k, w_all.at[shard(spread(k), 1), quarter(1), 1], x_left)

    def to_pair(k, other_y):
        return copy(PAIR + 4 * other_y + k, w_all.at[shard(spread(k), other_y)], partner)

    def strip(j):
        return pltpu.make_async_remote_copy(
            src_ref=x_ref.at[:, pl.ds(pl.multiple_of(j * 512 + (1 - c) * 256, 256), 256)],
            dst_ref=x_other.at[j],
            send_sem=send_sem.at[STRIP + j], recv_sem=recv_sem.at[STRIP + j],
            device_id=partner, device_id_type=MESH,
        )

    def keep(s):
        return pltpu.make_async_copy(w_all.at[s], w_out.at[s], store_sem.at[s])

    def multiply(s):
        keep(s).start()
        lanes = pl.ds(pl.multiple_of(s * 256, 256), 256)
        acc[...] += jnp.dot(
            x_ref[:, lanes], w_all[s].reshape(256, COLS), preferred_element_type=F32
        )

    own = pltpu.make_async_copy(w_hbm, w_all.at[dp], load_sem)
    own.start()
    barrier_with(everyone(at))
    own.wait()
    sent = []

    def send(item):
        item.start()
        sent.append(item)

    for i in range(4):
        send(to_z_right(i))
        send(to_z_left(i))
        if i == 0:
            send(to_far_y(0))
    send(to_pair(0, 0))
    for j in range(8):
        send(strip(j))
    acc[...] = jnp.zeros_like(acc)

    def turn_own(j, carry):
        rows = pl.ds(pl.multiple_of(j * 256, 256), 256)
        lanes = pl.ds(pl.multiple_of(j * 512 + c * 256, 256), 256)
        xt_ref[rows, :256] = x_ref[:, lanes].T
        return carry

    lax.fori_loop(0, 8, turn_own, 0)
    to_z_right(0).wait_recv()
    send(to_far_y(2))
    send(to_z_far(0))
    to_z_left(0).wait_recv()
    send(to_far_y(1))
    for k in range(3):
        to_far_y(k).wait_recv()
        send(to_x_right(k))
        send(to_x_left(k))
    to_z_right(1).wait_recv()
    send(to_z_far(1))

    def pass_x(k):
        to_x_right(k).wait_recv()
        send(to_x_far_right(k))
        to_x_left(k).wait_recv()
        send(to_x_far_left(k))

    pass_x(0)
    to_z_far(0).wait_recv()
    send(to_far_y(3))

    for j in range(8):
        strip(j).wait_recv()

    def turn_other(j, carry):
        rows = pl.ds(pl.multiple_of(j * 256, 256), 256)
        xt_ref[rows, 256:] = x_other[j].T
        return carry

    lax.fori_loop(0, 8, turn_other, 0)
    to_z_left(1).wait_recv()
    for i in (2, 3):
        to_z_left(i).wait_recv()
        send(to_z_far(i))
    send(to_pair(1, 0))
    for i in (2, 3):
        to_z_right(i).wait_recv()
    send(to_pair(2, 0))
    pass_x(1)
    to_far_y(3).wait_recv()
    send(to_x_right(3))
    send(to_x_left(3))
    pass_x(2)

    def near(k, carry):
        multiply(shard(spread(k)))
        to_pair(k, 0).wait_recv()
        multiply(shard(spread(k), 0, 1))
        return carry

    lax.fori_loop(0, 3, near, 0)
    for i in (1, 2, 3):
        to_z_far(i).wait_recv()
    send(to_pair(3, 0))
    pass_x(3)
    lax.fori_loop(3, 4, near, 0)

    def far(k, carry):
        to_x_far_right(k).wait_recv()
        to_x_far_left(k).wait_recv()
        to_pair(k, 1).start()
        multiply(shard(spread(k), 1))
        to_pair(k, 1).wait_recv()
        multiply(shard(spread(k), 1, 1))
        return carry

    lax.fori_loop(0, 4, far, 0)

    kv_ref[WIN - 1] = acc[:, QW:].astype(BF16)

    def to_peer(step):
        return pltpu.make_async_remote_copy(
            src_ref=kv_ref.at[WIN - 1],
            dst_ref=kv_ref.at[WIN - 1 - step],
            send_sem=send_sem.at[PEER + step - 1],
            recv_sem=recv_sem.at[PEER + step - 1],
            device_id=(dp, lax.rem(seq + step, SEQN)),
            device_id_type=MESH,
        )

    for step in range(1, WIN):
        @pl.when(seq + step < SEQN)
        def _(step=step):
            to_peer(step).start()

        @pl.when(seq < step)
        def _(step=step):
            kv_ref[WIN - 1 - step] = jnp.zeros((BLK, 2 * HEAD), BF16)

    q_ref[...] = acc[:, :QW].astype(BF16)
    for item in sent:
        item.wait_send()

    def finish(k, carry):
        to_pair(k, 1).wait_send()
        return carry

    lax.fori_loop(0, 4, finish, 0)

    def stored(s, carry):
        keep(s).wait()
        return carry

    lax.fori_loop(0, 16, stored, 0)
    for step in range(1, WIN):
        @pl.when(seq >= step)
        def _(step=step):
            to_peer(step).wait_recv()

        @pl.when(seq + step < SEQN)
        def _(step=step):
            to_peer(step).wait_send()


def attend_kernel(
    len_ref, flag_ref, q_ref, kv_ref, cot_ref, o_ref, dq_ref, dkv_ref,
    s_buf, bias, kt_buf, vt_buf, qt, ct, qr, cr, total,
):
    seq = lax.axis_index("seq")
    row0 = seq * BLK
    lane_pos = row0 + lax.broadcasted_iota(jnp.int32, (1, BLK), 1)
    sub_pos = row0 + lax.broadcasted_iota(jnp.int32, (BLK, HEAD), 0)
    first_start = jnp.int32(0)
    doc_start = jnp.int32(0)
    starts = jnp.zeros((1, BLK), jnp.int32)
    keep = jnp.zeros((BLK, HEAD), jnp.int32)
    for doc in range(NDOC):
        doc_end = doc_start + len_ref[0, doc]
        first_start = jnp.where((row0 >= doc_start) & (row0 < doc_end), doc_start, first_start)
        starts = jnp.where((lane_pos >= doc_start) & (lane_pos < doc_end), doc_start, starts)
        keep = jnp.where((sub_pos >= doc_start) & (sub_pos < doc_end), flag_ref[0, doc], keep)
        doc_start = doc_end
    base = seq - (WIN - 1)
    low = lax.div(first_start, BLK) - base

    def clear(j, carry):
        dkv_ref[j] = jnp.zeros((BLK, 2 * HEAD), BF16)
        return carry

    lax.fori_loop(0, low, clear, 0)

    def prepare(j, carry):
        key_pos = (base + j) * BLK + lax.broadcasted_iota(jnp.int32, (BLK, BLK), 0)
        allowed = (key_pos >= starts) & (key_pos <= lane_pos)
        bias[j] = jnp.where(allowed, 0.0, -1e30)
        kt_buf[j] = kv_ref[j, :, :HEAD].T
        vt_buf[j] = kv_ref[j, :, HEAD:].T
        return carry

    lax.fori_loop(low, WIN, prepare, 0)

    for head in range(HEADS):
        lanes, rows = slice(head * HEAD, (head + 1) * HEAD), slice(head * BLK, (head + 1) * BLK)
        q = q_ref[:, lanes]
        cot = jnp.where(keep > 0, cot_ref[:, lanes], jnp.zeros((), BF16))
        qr[rows, :] = q
        cr[rows, :] = cot
        qt[:, rows] = q.T
        ct[:, rows] = cot.T

    def score(j, top):
        s = jnp.dot(kv_ref[j, :, :HEAD], qt[...], preferred_element_type=F32)
        s = s * (SCALE * LOG2E) + jnp.concatenate([bias[j]] * HEADS, axis=1)
        s_buf[j] = s
        return jnp.maximum(top, jnp.max(s, axis=0, keepdims=True))

    top = lax.fori_loop(low, WIN, score, jnp.full((1, HEADS * BLK), -1e30, F32))
    total[...] = jnp.zeros_like(total)

    def weigh(j, mass):
        p = jnp.exp2(s_buf[j] - top)
        s_buf[j] = p
        total[...] += jnp.dot(vt_buf[j], p.astype(BF16), preferred_element_type=F32)
        return mass + jnp.sum(p, axis=0, keepdims=True)

    mass = lax.fori_loop(low, WIN, weigh, jnp.zeros((1, HEADS * BLK), F32))
    inverse = 1.0 / mass
    out = (total[...] * inverse).astype(BF16)
    for head in range(HEADS):
        o_ref[:, head * HEAD : (head + 1) * HEAD] = out[:, head * BLK : (head + 1) * BLK].T
    delta = jnp.sum(ct[...].astype(F32) * out.astype(F32), axis=0, keepdims=True)
    total[...] = jnp.zeros_like(total)

    def back(j, carry):
        p = s_buf[j] * inverse
        dp = jnp.dot(kv_ref[j, :, HEAD:], ct[...], preferred_element_type=F32)
        ds = (p * (dp - delta)).astype(BF16)
        total[...] += jnp.dot(kt_buf[j], ds, preferred_element_type=F32)
        dk = jnp.dot(ds, qr[...], preferred_element_type=F32) * SCALE
        dkv_ref[j, :, :HEAD] = dk.astype(BF16)
        dkv_ref[j, :, HEAD:] = jnp.dot(p.astype(BF16), cr[...], preferred_element_type=F32).astype(BF16)
        return carry

    lax.fori_loop(low, WIN, back, 0)
    for head in range(HEADS):
        dq = (total[:, head * BLK : (head + 1) * BLK] * SCALE).astype(BF16)
        dq_ref[:, head * HEAD : (head + 1) * HEAD] = dq.T


def cut(dims, axis, index, half):
    return tuple(index if d == axis else slice(None) for d in dims) + (half,)


def gradient_kernel(
    x_ref, dq_ref, dkv_ref, w_hbm, ig_ref, wg_ref,
    w_vmem, dproj, dkv_in,
    d00, d01, d02, d10, d11, d12, d20, d21, d22,
    b00, b01, b02, b10, b11, b12, b20, b21, b22,
    load_sem, pair_send, pair_recv, kv_send, kv_recv, ring_send, ring_recv,
):
    data = ((d00, d01, d02), (d10, d11, d12), (d20, d21, d22))
    bufs = ((b00, b01, b02), (b10, b11, b12), (b20, b21, b22))
    dp = lax.axis_index("dp")
    seq = lax.axis_index("seq")
    at = place()
    load = pltpu.make_async_copy(w_hbm, w_vmem, load_sem)
    load.start()
    partner = device(moved(at, "c", 1))
    barrier_with(everyone(at))

    def pair_copy(index, src, columns):
        return pltpu.make_async_remote_copy(
            src_ref=src,
            dst_ref=dproj.at[pl.ds(BLK, BLK), columns],
            send_sem=pair_send.at[index],
            recv_sem=pair_recv.at[index],
            device_id=partner,
            device_id_type=MESH,
        )

    def kv_copy(step):
        return pltpu.make_async_remote_copy(
            src_ref=dkv_ref.at[WIN - 1 - step],
            dst_ref=dkv_in.at[step - 1],
            send_sem=kv_send.at[step - 1],
            recv_sem=kv_recv.at[step - 1],
            device_id=(dp, lax.rem(seq + SEQN - step, SEQN)),
            device_id_type=MESH,
        )

    for step in range(1, WIN):
        @pl.when(seq >= step)
        def _(step=step):
            kv_copy(step).start()
    pair_q = pair_copy(0, dq_ref, pl.ds(0, QW))
    pair_q.start()
    dproj[pl.ds(0, BLK), :QW] = dq_ref[...]

    def ring_copy(color, stage, buf, src, there):
        k = (color * 3 + stage) * 6 + buf
        return pltpu.make_async_remote_copy(
            src_ref=src,
            dst_ref=bufs[color][stage].at[buf],
            send_sem=ring_send.at[k],
            recv_sem=ring_recv.at[k],
            device_id=device(there),
            device_id_type=MESH,
        )

    def stage_of(color, stage):
        order = COLORS[color][2]
        dims = [d for d in "zyx" if d in order[stage:]]
        axis = order[stage]
        me = at[axis]
        return (
            dims, axis, me,
            lax.rem(me + 1, 4), lax.rem(me + 2, 4), lax.rem(me + 3, 4),
            moved(at, axis, 1), moved(at, axis, 3),
        )

    started = []

    def open_stage(color, stage):
        dims, axis, me, right, across, left, to_right, to_left = stage_of(color, stage)
        src = data[color][stage]
        for buf, index, half, there in (
            (0, across, 0, to_right),
            (1, across, 1, to_left),
            (3, right, 1, to_right),
            (4, left, 0, to_left),
        ):
            copy = ring_copy(color, stage, buf, src.at[cut(dims, axis, index, half)], there)
            copy.start()
            started.append(copy)

    def pass_on(color, stage):
        dims, axis, me, right, across, left, to_right, to_left = stage_of(color, stage)
        src = data[color][stage]
        for first, buf, index, half, there in ((0, 2, right, 0, to_right), (1, 5, left, 1, to_left)):
            where = cut(dims, axis, index, half)
            ring_copy(color, stage, first, src.at[where], there).wait_recv()
            src[where] = (src[where].astype(F32) + bufs[color][stage][first].astype(F32)).astype(BF16)
            copy = ring_copy(color, stage, buf, src.at[where], there)
            copy.start()
            started.append(copy)

    def close_stage(color, stage):
        dims, axis, me, right, across, left, to_right, to_left = stage_of(color, stage)
        src, got = data[color][stage], bufs[color][stage]
        for half in (0, 1):
            where = cut(dims, axis, me, half)
            total = src[where].astype(F32)
            for buf in (2 + half, 4 + half):
                ring_copy(color, stage, buf, src.at[where], to_right).wait_recv()
                total = total + got[buf].astype(F32)
            if stage < 2:
                data[color][stage + 1][(slice(None),) * (len(dims) - 1) + (half,)] = total.astype(BF16)
            else:
                first, width, _ = COLORS[color]
                wg_ref[16 * half : 16 * half + 16, first : first + width] = total

    def multiply(color):
        first, width, _ = COLORS[color]

        def body(z, carry):
            rows = pl.ds(pl.multiple_of(z * 512, 512), 512)
            part = jnp.dot(x_ref[rows, :], dproj[:, first : first + width], preferred_element_type=F32)
            data[color][0][z] = part.astype(BF16).reshape(4, 4, 2, 16, width)
            return carry

        lax.fori_loop(0, 4, body, 0)

    pair_q.wait_recv()
    for color in (0, 1):
        multiply(color)
        open_stage(color, 0)

    total = dkv_ref[WIN - 1].astype(F32)
    for step in range(1, WIN):
        @pl.when(seq + step < SEQN)
        def _(step=step):
            kv_copy(step).wait_recv()

        @pl.when(seq + step >= SEQN)
        def _(step=step):
            dkv_in[step - 1] = jnp.zeros((BLK, 2 * HEAD), BF16)

        total = total + dkv_in[step - 1].astype(F32)
    dproj[pl.ds(0, BLK), QW:] = total.astype(BF16)
    pair_kv = pair_copy(1, dproj.at[pl.ds(0, BLK), pl.ds(QW, 2 * HEAD)], pl.ds(QW, 2 * HEAD))
    pair_kv.start()
    pair_kv.wait_recv()
    multiply(2)
    open_stage(2, 0)

    load.wait()

    def grad_chunk(n, carry):
        rows = pl.ds(pl.multiple_of(n * 512, 512), 512)
        ig_ref[:, rows] = lax.dot_general(
            dproj[pl.ds(0, BLK), :], w_vmem[rows, :], NT, preferred_element_type=F32
        ).astype(BF16)
        return carry

    lax.fori_loop(0, 8, grad_chunk, 0)

    for stage in range(3):
        for color in range(3):
            pass_on(color, stage)
        for color in range(3):
            close_stage(color, stage)
            if stage < 2:
                open_stage(color, stage + 1)
    for copy in started:
        copy.wait_send()
    pair_q.wait_send()
    pair_kv.wait_send()
    for step in range(1, WIN):
        @pl.when(seq >= step)
        def _(step=step):
            kv_copy(step).wait_send()


VM = pl.BlockSpec(memory_space=pltpu.VMEM)
SM = pl.BlockSpec(memory_space=pltpu.SMEM)
ANY = pl.BlockSpec(memory_space=pl.ANY)
DMA = pltpu.SemaphoreType.DMA
LIMIT = 60 * 1024 * 1024


def shape(dims, kind=BF16):
    return jax.ShapeDtypeStruct(dims, kind)


def shards(inputs, weights, cotangent, doc_lengths, kept_flags):
    tokens = inputs[0]
    queries, pairs, full_weights, columns = pl.pallas_call(
        project_kernel,
        out_shape=(
            shape((BLK, QW)), shape((WIN, BLK, 2 * HEAD)), shape((16, 4, 2, 32, COLS)), shape((2048, 2 * BLK)),
        ),
        in_specs=[VM, ANY],
        out_specs=(VM, VM, ANY, VM),
        scratch_shapes=[
            pltpu.VMEM((16, 4, 2, 32, COLS), BF16),
            pltpu.VMEM((BLK, COLS), F32),
            pltpu.VMEM((8, BLK, 256), BF16),
            DMA, DMA((16,)), DMA((52,)), DMA((52,)),
        ],
        compiler_params=pltpu.CompilerParams(collective_id=0, has_side_effects=True, vmem_limit_bytes=LIMIT),
        name="project",
    )(tokens, weights.reshape(4, 2, 32, COLS))
    full_weights = full_weights.reshape(D, COLS)

    attention, query_grads, pair_grads = pl.pallas_call(
        attend_kernel,
        out_shape=(shape((BLK, QW)), shape((BLK, QW)), shape((WIN, BLK, 2 * HEAD))),
        in_specs=[SM, SM, VM, VM, VM],
        out_specs=(VM, VM, VM),
        scratch_shapes=[
            pltpu.VMEM((WIN, BLK, HEADS * BLK), F32),
            pltpu.VMEM((WIN, BLK, BLK), F32),
            pltpu.VMEM((WIN, HEAD, BLK), BF16),
            pltpu.VMEM((WIN, HEAD, BLK), BF16),
            pltpu.VMEM((HEAD, HEADS * BLK), BF16),
            pltpu.VMEM((HEAD, HEADS * BLK), BF16),
            pltpu.VMEM((HEADS * BLK, HEAD), BF16),
            pltpu.VMEM((HEADS * BLK, HEAD), BF16),
            pltpu.VMEM((HEAD, HEADS * BLK), F32),
        ],
        compiler_params=pltpu.CompilerParams(vmem_limit_bytes=LIMIT),
        name="attend",
    )(doc_lengths, kept_flags, queries, pairs, cotangent[0])

    held, received = [], []
    for _, width, order in COLORS:
        for stage in range(3):
            dims = (4,) * (3 - stage)
            held.append(pltpu.VMEM(dims + (2, 16, width), BF16))
            received.append(pltpu.VMEM((6,) + dims[1:] + (16, width), BF16))
    inputs_grad, weights_grad = pl.pallas_call(
        gradient_kernel,
        out_shape=(shape((BLK, D)), shape((32, COLS), F32)),
        in_specs=[VM, VM, VM, ANY],
        out_specs=(VM, VM),
        scratch_shapes=[
            pltpu.VMEM((D, COLS), BF16),
            pltpu.VMEM((2 * BLK, COLS), BF16),
            pltpu.VMEM((WIN - 1, BLK, 2 * HEAD), BF16),
        ]
        + held
        + received
        + [DMA, DMA((2,)), DMA((2,)), DMA((WIN - 1,)), DMA((WIN - 1,)), DMA((54,)), DMA((54,))],
        compiler_params=pltpu.CompilerParams(collective_id=1, has_side_effects=True, vmem_limit_bytes=LIMIT),
        name="gradients",
    )(columns, query_grads, pair_grads, full_weights)
    return (attention[None], inputs_grad[None], weights_grad)


def solution(mesh):
    in_specs = (
        P("dp", "seq", None),
        P("dp", None),
        P("dp", "seq", None),
        P("dp", None),
        P("dp", None),
    )
    out_specs = (P("dp", "seq", None), P("dp", "seq", None), P(("dp", "seq"), None))
    return jax.shard_map(shards, mesh=mesh, in_specs=in_specs, out_specs=out_specs, check_vma=False)
```

```python
import math

import jax
import jax.numpy as jnp
from jax import lax
from jax.experimental import pallas as pl
from jax.experimental.pallas import tpu as pltpu
from jax.sharding import PartitionSpec as P

MESH = pl.DeviceIdType.MESH
HEAD = 128
HEADS = 8
BLK = 256
WIN = 5
D = 4096
QW = 1024
COLS = 1280
NDOC = 8
SEQN = 8
SCALE = 1.0 / math.sqrt(HEAD)
LOG2E = math.log2(math.e)
F32 = jnp.float32
BF16 = jnp.bfloat16
NT = (((1,), (1,)), ((), ()))
COLORS = ((0, 512, "xyz"), (512, 384, "yzx"), (896, 384, "zxy"))


def place():
    dp = lax.axis_index("dp")
    seq = lax.axis_index("seq")
    z = lax.div(dp, 4)
    y = lax.rem(lax.div(dp, 2), 2) * 2 + lax.div(seq, 4)
    return {"z": z, "y": y, "x": lax.rem(seq, 4), "c": lax.rem(dp, 2)}


def device(at):
    dp = at["z"] * 4 + lax.div(at["y"], 2) * 2 + at["c"]
    return (dp, lax.rem(at["y"], 2) * 4 + at["x"])


def moved(at, axis, step):
    count = 2 if axis == "c" else 4
    there = dict(at)
    there[axis] = lax.rem(at[axis] + step, count)
    return there


def barrier_with(devices):
    sem = pltpu.get_barrier_semaphore()
    for there in devices:
        pl.semaphore_signal(sem, inc=1, device_id=there, device_id_type=MESH)
    pl.semaphore_wait(sem, len(devices))


def seq_peers():
    dp = lax.axis_index("dp")
    seq = lax.axis_index("seq")
    return [(dp, lax.rem(seq + step, SEQN)) for step in range(1, SEQN)]


def everyone(at):
    far_y = moved(at, "y", 3 - 2 * lax.rem(at["y"], 2))
    ring = [device(there) for there in (moved(at, "z", 1), moved(at, "z", 3), far_y)]
    return seq_peers() + ring + [device(moved(at, "c", 1))]


def spread(k):
    return k + lax.div(k, 2) * (1 - 2 * lax.rem(k, 2))


Z_RIGHT, Z_LEFT, Z_FAR, Y_FAR, X_RIGHT, X_LEFT, X_FAR_RIGHT, X_FAR_LEFT, PAIR, STRIP, PEER = (
    0, 4, 8, 12, 16, 20, 24, 28, 32, 40, 48
)


def cut(dims, axis, index, half):
    return tuple(index if d == axis else slice(None) for d in dims) + (half,)


def layer_kernel(
    len_ref, flag_ref, x_ref, w_hbm, cot_ref, o_ref, ig_ref, wg_ref,
    w_all, acc, x_other, xt, kv_ref, s_buf, kt_buf, vt_buf, qt, ct, qr, cr, total, dkv_ref, dproj, dkv_in,
    d00, d01, d02, d10, d11, d12, d20, d21, d22,
    b00, b01, b02, b10, b11, b12, b20, b21, b22,
    load_sem, send_sem, recv_sem, pair_send, pair_recv, kv_send, kv_recv, ring_send, ring_recv,
):
    data = ((d00, d01, d02), (d10, d11, d12), (d20, d21, d22))
    bufs = ((b00, b01, b02), (b10, b11, b12), (b20, b21, b22))
    dp = lax.axis_index("dp")
    seq = lax.axis_index("seq")
    at = place()
    z, x, c = at["z"], at["x"], at["c"]
    half_y = lax.rem(lax.div(dp, 2), 2)
    partner = device(moved(at, "c", 1))
    far_y = device(moved(at, "y", 3 - 2 * lax.rem(at["y"], 2)))
    z_right, z_left = device(moved(at, "z", 1)), device(moved(at, "z", 3))
    x_right, x_left = device(moved(at, "x", 1)), device(moved(at, "x", 3))

    def shard(step, other_y=0, other_c=0):
        zz = lax.rem(z + step, 4)
        yy = lax.rem(half_y + other_y, 2)
        return zz * 4 + yy * 2 + lax.rem(c + other_c, 2)

    def quarter(i):
        return lax.rem(x + i, 4)

    def copy(slot, ref, there):
        return pltpu.make_async_remote_copy(
            src_ref=ref, dst_ref=ref, send_sem=send_sem.at[slot], recv_sem=recv_sem.at[slot],
            device_id=there, device_id_type=MESH,
        )

    def to_z_right(i):
        return copy(Z_RIGHT + i, w_all.at[dp, quarter(i)], z_right)

    def to_z_left(i):
        return copy(Z_LEFT + i, w_all.at[dp, quarter(i)], z_left)

    def to_z_far(i):
        if i < 2:
            return copy(Z_FAR + i, w_all.at[shard(3), quarter(i)], z_right)
        return copy(Z_FAR + i, w_all.at[shard(1), quarter(i)], z_left)

    def to_far_y(k):
        return copy(Y_FAR + k, w_all.at[shard(spread(k)), x], far_y)

    def to_x_right(k):
        return copy(X_RIGHT + k, w_all.at[shard(spread(k), 1), x], x_right)

    def to_x_left(k):
        return copy(X_LEFT + k, w_all.at[shard(spread(k), 1), x], x_left)

    def to_x_far_right(k):
        return copy(X_FAR_RIGHT + k, w_all.at[shard(spread(k), 1), quarter(3), 0], x_right)

    def to_x_far_left(k):
        return copy(X_FAR_LEFT + k, w_all.at[shard(spread(k), 1), quarter(1), 1], x_left)

    def to_pair(k, other_y):
        return copy(PAIR + 4 * other_y + k, w_all.at[shard(spread(k), other_y)], partner)

    def strip(j):
        return pltpu.make_async_remote_copy(
            src_ref=x_ref.at[:, pl.ds(pl.multiple_of(j * 512 + (1 - c) * 256, 256), 256)],
            dst_ref=x_other.at[j],
            send_sem=send_sem.at[STRIP + j], recv_sem=recv_sem.at[STRIP + j],
            device_id=partner, device_id_type=MESH,
        )

    def project(s):
        lanes = pl.ds(pl.multiple_of(s * 256, 256), 256)
        acc[...] += jnp.dot(
            x_ref[:, lanes], w_all[s].reshape(256, COLS), preferred_element_type=F32
        )

    own = pltpu.make_async_copy(w_hbm, w_all.at[dp], load_sem)
    own.start()
    barrier_with(everyone(at))
    own.wait()
    sent = []

    def send(item):
        item.start()
        sent.append(item)

    for i in range(4):
        send(to_z_right(i))
        send(to_z_left(i))
        if i == 0:
            send(to_far_y(0))
    send(to_pair(0, 0))
    for j in range(8):
        send(strip(j))
    acc[...] = jnp.zeros_like(acc)

    def turn_own(j, carry):
        rows = pl.ds(pl.multiple_of(j * 256, 256), 256)
        lanes = pl.ds(pl.multiple_of(j * 512 + c * 256, 256), 256)
        xt[rows, :256] = x_ref[:, lanes].T
        return carry

    lax.fori_loop(0, 8, turn_own, 0)
    to_z_right(0).wait_recv()
    send(to_far_y(2))
    send(to_z_far(0))
    to_z_left(0).wait_recv()
    send(to_far_y(1))
    for k in range(3):
        to_far_y(k).wait_recv()
        send(to_x_right(k))
        send(to_x_left(k))
    to_z_right(1).wait_recv()
    send(to_z_far(1))

    def pass_x(k):
        to_x_right(k).wait_recv()
        send(to_x_far_right(k))
        to_x_left(k).wait_recv()
        send(to_x_far_left(k))

    pass_x(0)
    to_z_far(0).wait_recv()
    send(to_far_y(3))

    for j in range(8):
        strip(j).wait_recv()

    def turn_other(j, carry):
        rows = pl.ds(pl.multiple_of(j * 256, 256), 256)
        xt[rows, 256:] = x_other[j].T
        return carry

    lax.fori_loop(0, 8, turn_other, 0)
    to_z_left(1).wait_recv()
    for i in (2, 3):
        to_z_left(i).wait_recv()
        send(to_z_far(i))
    send(to_pair(1, 0))
    for i in (2, 3):
        to_z_right(i).wait_recv()
    send(to_pair(2, 0))
    pass_x(1)
    to_far_y(3).wait_recv()
    send(to_x_right(3))
    send(to_x_left(3))
    pass_x(2)

    def near(k, carry):
        project(shard(spread(k)))
        return carry

    lax.fori_loop(0, 3, near, 0)
    for i in (1, 2, 3):
        to_z_far(i).wait_recv()
    send(to_pair(3, 0))
    pass_x(3)
    lax.fori_loop(3, 4, near, 0)

    def far(k, carry):
        to_x_far_right(k).wait_recv()
        to_x_far_left(k).wait_recv()
        to_pair(k, 1).start()
        to_pair(k, 0).wait_recv()
        project(shard(spread(k), 0, 1))
        project(shard(spread(k), 1))

        @pl.when(k > 0)
        def _():
            to_pair(k - 1, 1).wait_recv()
            project(shard(spread(k - 1), 1, 1))

        return carry

    lax.fori_loop(0, 4, far, 0)
    to_pair(3, 1).wait_recv()
    project(shard(spread(3), 1, 1))

    kv_ref[WIN - 1] = acc[:, QW:].astype(BF16)

    def to_peer(step):
        return pltpu.make_async_remote_copy(
            src_ref=kv_ref.at[WIN - 1],
            dst_ref=kv_ref.at[WIN - 1 - step],
            send_sem=send_sem.at[PEER + step - 1],
            recv_sem=recv_sem.at[PEER + step - 1],
            device_id=(dp, lax.rem(seq + step, SEQN)),
            device_id_type=MESH,
        )

    for step in range(1, WIN):
        @pl.when(seq + step < SEQN)
        def _(step=step):
            to_peer(step).start()

    row0 = seq * BLK
    lane_pos = row0 + lax.broadcasted_iota(jnp.int32, (1, BLK), 1)
    sub_pos = row0 + lax.broadcasted_iota(jnp.int32, (BLK, HEAD), 0)
    doc_start = jnp.int32(0)
    starts = jnp.zeros((1, BLK), jnp.int32)
    keep = jnp.zeros((BLK, HEAD), jnp.int32)
    for doc in range(NDOC):
        doc_end = doc_start + len_ref[0, doc]
        starts = jnp.where((lane_pos >= doc_start) & (lane_pos < doc_end), doc_start, starts)
        keep = jnp.where((sub_pos >= doc_start) & (sub_pos < doc_end), flag_ref[0, doc], keep)
        doc_start = doc_end
    base = seq - (WIN - 1)
    low = jnp.maximum(WIN - 1 - seq, 0)

    for head in range(HEADS):
        lanes, rows = slice(head * HEAD, (head + 1) * HEAD), slice(head * BLK, (head + 1) * BLK)
        q = acc[:, lanes].astype(BF16)
        cot = jnp.where(keep > 0, cot_ref[:, lanes], jnp.zeros((), BF16))
        qr[rows, :] = q
        cr[rows, :] = cot
        qt[:, rows] = q.T
        ct[:, rows] = cot.T

    def score(back, top):
        j = WIN - 1 - back

        @pl.when(back > 0)
        def _():
            to_peer(back).wait_recv()

        key_pos = (base + j) * BLK + lax.broadcasted_iota(jnp.int32, (BLK, BLK), 0)
        allowed = (key_pos >= starts) & (key_pos <= lane_pos)
        mask = jnp.where(allowed, 0.0, -1e30)
        kt_buf[j] = kv_ref[j, :, :HEAD].T
        vt_buf[j] = kv_ref[j, :, HEAD:].T
        s = jnp.dot(kv_ref[j, :, :HEAD], qt[...], preferred_element_type=F32)
        s = s * (SCALE * LOG2E) + jnp.concatenate([mask] * HEADS, axis=1)
        s_buf[j] = s
        return jnp.maximum(top, jnp.max(s, axis=0, keepdims=True))

    top = lax.fori_loop(0, WIN - low, score, jnp.full((1, HEADS * BLK), -1e30, F32))
    total[...] = jnp.zeros_like(total)

    def weigh(j, mass):
        p = jnp.exp2(s_buf[j] - top)
        s_buf[j] = p
        total[...] += jnp.dot(vt_buf[j], p.astype(BF16), preferred_element_type=F32)
        return mass + jnp.sum(p, axis=0, keepdims=True)

    mass = lax.fori_loop(low, WIN, weigh, jnp.zeros((1, HEADS * BLK), F32))
    inverse = 1.0 / mass
    out = (total[...] * inverse).astype(BF16)
    for head in range(HEADS):
        o_ref[:, head * HEAD : (head + 1) * HEAD] = out[:, head * BLK : (head + 1) * BLK].T
    delta = jnp.sum(ct[...].astype(F32) * out.astype(F32), axis=0, keepdims=True)
    total[...] = jnp.zeros_like(total)

    def back(j, carry):
        p = s_buf[j] * inverse
        dp = jnp.dot(kv_ref[j, :, HEAD:], ct[...], preferred_element_type=F32)
        ds = (p * (dp - delta)).astype(BF16)
        total[...] += jnp.dot(kt_buf[j], ds, preferred_element_type=F32)
        dk = jnp.dot(ds, qr[...], preferred_element_type=F32) * SCALE
        dkv_ref[j, :, :HEAD] = dk.astype(BF16)
        dkv_ref[j, :, HEAD:] = jnp.dot(p.astype(BF16), cr[...], preferred_element_type=F32).astype(BF16)
        return carry

    lax.fori_loop(low, WIN, back, 0)
    for head in range(HEADS):
        dq = (total[:, head * BLK : (head + 1) * BLK] * SCALE).astype(BF16)
        dproj[pl.ds(0, BLK), head * HEAD : (head + 1) * HEAD] = dq.T

    def pair_copy(index, src, columns):
        return pltpu.make_async_remote_copy(
            src_ref=src,
            dst_ref=dproj.at[pl.ds(BLK, BLK), columns],
            send_sem=pair_send.at[index],
            recv_sem=pair_recv.at[index],
            device_id=partner,
            device_id_type=MESH,
        )

    def kv_copy(step):
        return pltpu.make_async_remote_copy(
            src_ref=dkv_ref.at[WIN - 1 - step],
            dst_ref=dkv_in.at[step - 1],
            send_sem=kv_send.at[step - 1],
            recv_sem=kv_recv.at[step - 1],
            device_id=(dp, lax.rem(seq + SEQN - step, SEQN)),
            device_id_type=MESH,
        )

    for step in range(1, WIN):
        @pl.when(seq >= step)
        def _(step=step):
            kv_copy(step).start()
    pair_q = pair_copy(0, dproj.at[pl.ds(0, BLK), pl.ds(0, QW)], pl.ds(0, QW))
    pair_q.start()

    def ring_copy(color, stage, buf, src, there):
        k = (color * 3 + stage) * 6 + buf
        return pltpu.make_async_remote_copy(
            src_ref=src,
            dst_ref=bufs[color][stage].at[buf],
            send_sem=ring_send.at[k],
            recv_sem=ring_recv.at[k],
            device_id=device(there),
            device_id_type=MESH,
        )

    def stage_of(color, stage):
        order = COLORS[color][2]
        dims = [d for d in "zyx" if d in order[stage:]]
        axis = order[stage]
        me = at[axis]
        return (
            dims, axis, me,
            lax.rem(me + 1, 4), lax.rem(me + 2, 4), lax.rem(me + 3, 4),
            moved(at, axis, 1), moved(at, axis, 3),
        )

    started = []

    def open_stage(color, stage):
        dims, axis, me, right, across, left, to_right, to_left = stage_of(color, stage)
        src = data[color][stage]
        for buf, index, half, there in (
            (0, across, 0, to_right),
            (1, across, 1, to_left),
            (3, right, 1, to_right),
            (4, left, 0, to_left),
        ):
            copy = ring_copy(color, stage, buf, src.at[cut(dims, axis, index, half)], there)
            copy.start()
            started.append(copy)

    def pass_on(color, stage):
        dims, axis, me, right, across, left, to_right, to_left = stage_of(color, stage)
        src = data[color][stage]
        for first, buf, index, half, there in ((0, 2, right, 0, to_right), (1, 5, left, 1, to_left)):
            where = cut(dims, axis, index, half)
            ring_copy(color, stage, first, src.at[where], there).wait_recv()
            src[where] = (src[where].astype(F32) + bufs[color][stage][first].astype(F32)).astype(BF16)
            copy = ring_copy(color, stage, buf, src.at[where], there)
            copy.start()
            started.append(copy)

    def close_stage(color, stage):
        dims, axis, me, right, across, left, to_right, to_left = stage_of(color, stage)
        src, got = data[color][stage], bufs[color][stage]
        for half in (0, 1):
            where = cut(dims, axis, me, half)
            summed = src[where].astype(F32)
            for buf in (2 + half, 4 + half):
                ring_copy(color, stage, buf, src.at[where], to_right).wait_recv()
                summed = summed + got[buf].astype(F32)
            if stage < 2:
                data[color][stage + 1][(slice(None),) * (len(dims) - 1) + (half,)] = summed.astype(BF16)
            else:
                first, width, _ = COLORS[color]
                wg_ref[16 * half : 16 * half + 16, first : first + width] = summed

    def multiply(color):
        first, width, _ = COLORS[color]

        def body(z, carry):
            rows = pl.ds(pl.multiple_of(z * 512, 512), 512)
            part = jnp.dot(xt[rows, :], dproj[:, first : first + width], preferred_element_type=F32)
            data[color][0][z] = part.astype(BF16).reshape(4, 4, 2, 16, width)
            return carry

        lax.fori_loop(0, 4, body, 0)

    pair_q.wait_recv()
    for color in (0, 1):
        multiply(color)
        open_stage(color, 0)

    pairs = dkv_ref[WIN - 1].astype(F32)
    for step in range(1, WIN):
        @pl.when(seq + step < SEQN)
        def _(step=step):
            kv_copy(step).wait_recv()

        @pl.when(seq + step >= SEQN)
        def _(step=step):
            dkv_in[step - 1] = jnp.zeros((BLK, 2 * HEAD), BF16)

        pairs = pairs + dkv_in[step - 1].astype(F32)
    dproj[pl.ds(0, BLK), QW:] = pairs.astype(BF16)
    pair_kv = pair_copy(1, dproj.at[pl.ds(0, BLK), pl.ds(QW, 2 * HEAD)], pl.ds(QW, 2 * HEAD))
    pair_kv.start()
    pair_kv.wait_recv()
    multiply(2)
    open_stage(2, 0)

    def grad_chunk(n, carry):
        rows = pl.ds(pl.multiple_of(n * 512, 512), 512)
        ig_ref[:, rows] = lax.dot_general(
            dproj[pl.ds(0, BLK), :], w_all[pl.ds(2 * n, 2)].reshape(512, COLS), NT, preferred_element_type=F32
        ).astype(BF16)
        return carry

    lax.fori_loop(0, 8, grad_chunk, 0)

    for stage in range(3):
        for color in range(3):
            pass_on(color, stage)
        for color in range(3):
            close_stage(color, stage)
            if stage < 2:
                open_stage(color, stage + 1)
    for item in started:
        item.wait_send()
    pair_q.wait_send()
    pair_kv.wait_send()
    for step in range(1, WIN):
        @pl.when(seq >= step)
        def _(step=step):
            kv_copy(step).wait_send()
    for item in sent:
        item.wait_send()

    def finish(k, carry):
        to_pair(k, 1).wait_send()
        return carry

    lax.fori_loop(0, 4, finish, 0)
    for step in range(1, WIN):
        @pl.when(seq + step < SEQN)
        def _(step=step):
            to_peer(step).wait_send()


VM = pl.BlockSpec(memory_space=pltpu.VMEM)
SM = pl.BlockSpec(memory_space=pltpu.SMEM)
ANY = pl.BlockSpec(memory_space=pl.ANY)
DMA = pltpu.SemaphoreType.DMA
LIMIT = 60 * 1024 * 1024


def shape(dims, kind=BF16):
    return jax.ShapeDtypeStruct(dims, kind)


def shards(inputs, weights, cotangent, doc_lengths, kept_flags):
    held, received = [], []
    for _, width, order in COLORS:
        for stage in range(3):
            dims = (4,) * (3 - stage)
            held.append(pltpu.VMEM(dims + (2, 16, width), BF16))
            received.append(pltpu.VMEM((6,) + dims[1:] + (16, width), BF16))
    rows = HEADS * BLK
    attention, inputs_grad, weights_grad = pl.pallas_call(
        layer_kernel,
        out_shape=(shape((BLK, QW)), shape((BLK, D)), shape((32, COLS), F32)),
        in_specs=[SM, SM, VM, ANY, VM],
        out_specs=(VM, VM, VM),
        scratch_shapes=[
            pltpu.VMEM((16, 4, 2, 32, COLS), BF16),
            pltpu.VMEM((BLK, COLS), F32),
            pltpu.VMEM((8, BLK, 256), BF16),
            pltpu.VMEM((2048, 2 * BLK), BF16),
            pltpu.VMEM((WIN, BLK, 2 * HEAD), BF16),
            pltpu.VMEM((WIN, BLK, rows), F32),
            pltpu.VMEM((WIN, HEAD, BLK), BF16),
            pltpu.VMEM((WIN, HEAD, BLK), BF16),
            pltpu.VMEM((HEAD, rows), BF16),
            pltpu.VMEM((HEAD, rows), BF16),
            pltpu.VMEM((rows, HEAD), BF16),
            pltpu.VMEM((rows, HEAD), BF16),
            pltpu.VMEM((HEAD, rows), F32),
            pltpu.VMEM((WIN, BLK, 2 * HEAD), BF16),
            pltpu.VMEM((2 * BLK, COLS), BF16),
            pltpu.VMEM((WIN - 1, BLK, 2 * HEAD), BF16),
        ]
        + held
        + received
        + [DMA, DMA((52,)), DMA((52,)), DMA((2,)), DMA((2,)), DMA((WIN - 1,)), DMA((WIN - 1,)), DMA((54,)), DMA((54,))],
        compiler_params=pltpu.CompilerParams(collective_id=0, has_side_effects=True, vmem_limit_bytes=LIMIT),
        name="layer",
    )(doc_lengths, kept_flags, inputs[0], weights.reshape(4, 2, 32, COLS), cotangent[0])
    return (attention[None], inputs_grad[None], weights_grad)


def solution(mesh):
    in_specs = (
        P("dp", "seq", None),
        P("dp", None),
        P("dp", "seq", None),
        P("dp", None),
        P("dp", None),
    )
    out_specs = (P("dp", "seq", None), P("dp", "seq", None), P(("dp", "seq"), None))
    return jax.shard_map(shards, mesh=mesh, in_specs=in_specs, out_specs=out_specs, check_vma=False)
```

```python
import math

import jax
import jax.numpy as jnp
from jax import lax
from jax.experimental import pallas as pl
from jax.experimental.pallas import tpu as pltpu
from jax.sharding import PartitionSpec as P

MESH = pl.DeviceIdType.MESH
HEAD = 128
HEADS = 8
BLK = 256
WIN = 5
D = 4096
QW = 1024
COLS = 1280
NDOC = 8
SEQN = 8
SCALE = 1.0 / math.sqrt(HEAD)
LOG2E = math.log2(math.e)
F32 = jnp.float32
BF16 = jnp.bfloat16
NT = (((1,), (1,)), ((), ()))
PARTS = (
    (0, 256, "xyz"), (256, 128, "yzx"), (384, 128, "zxy"), (512, 256, "yzx"), (768, 256, "zxy"), (1024, 256, "xyz"),
)
STEPS = (
    "e10 e20 r30 r40 e00 r50 r11 r21 e30 e40 r01 e11 e21 e50 r31 r41 e01 r12 r22 r51 e31 e41 "
    "r02 e12 e22 e51 r32 r42 e02 e32 e42 r52 e52"
).split()


def place():
    dp = lax.axis_index("dp")
    seq = lax.axis_index("seq")
    z = lax.div(dp, 4)
    y = lax.rem(lax.div(dp, 2), 2) * 2 + lax.div(seq, 4)
    return {"z": z, "y": y, "x": lax.rem(seq, 4), "c": lax.rem(dp, 2)}


def device(at):
    dp = at["z"] * 4 + lax.div(at["y"], 2) * 2 + at["c"]
    return (dp, lax.rem(at["y"], 2) * 4 + at["x"])


def moved(at, axis, step):
    count = 2 if axis == "c" else 4
    there = dict(at)
    there[axis] = lax.rem(at[axis] + step, count)
    return there


def barrier_with(devices):
    sem = pltpu.get_barrier_semaphore()
    for there in devices:
        pl.semaphore_signal(sem, inc=1, device_id=there, device_id_type=MESH)
    pl.semaphore_wait(sem, len(devices))


def seq_peers():
    dp = lax.axis_index("dp")
    seq = lax.axis_index("seq")
    return [(dp, lax.rem(seq + step, SEQN)) for step in range(1, SEQN)]


def everyone(at):
    far_y = moved(at, "y", 3 - 2 * lax.rem(at["y"], 2))
    ring = [device(there) for there in (moved(at, "z", 1), moved(at, "z", 3), far_y)]
    return seq_peers() + ring + [device(moved(at, "c", 1))]


def spread(k):
    return k + lax.div(k, 2) * (1 - 2 * lax.rem(k, 2))


(
    Z_RIGHT, Z_LEFT, Z_FAR, Y_FAR, X_RIGHT, X_LEFT, X_FAR_RIGHT, X_FAR_LEFT, PAIR, STRIP, PEER, Y_NEAR_Z, Y_NEAR_X, SLOTS,
) = (0, 4, 8, 12, 16, 20, 24, 28, 32, 40, 48, 52, 56, 60)


def cut(dims, axis, index, half):
    return tuple(index if d == axis else slice(None) for d in dims) + (half,)


def layer_kernel(
    len_ref, flag_ref, x_ref, w_hbm, cot_ref, o_ref, ig_ref, wg_ref,
    w_all, acc, x_other, xt, kv_ref, s_buf, kt_buf, vt_buf, qt, ct, qr, cr, total, dkv_ref, dproj, dkv_in,
    *rest,
):
    count = len(PARTS)
    data = [rest[3 * part : 3 * part + 3] for part in range(count)]
    bufs = [rest[3 * (count + part) : 3 * (count + part) + 3] for part in range(count)]
    load_sem, send_sem, recv_sem, pair_send, pair_recv, kv_send, kv_recv, ring_send, ring_recv = rest[6 * count :]
    dp = lax.axis_index("dp")
    seq = lax.axis_index("seq")
    at = place()
    z, x, c = at["z"], at["x"], at["c"]
    half_y = lax.rem(lax.div(dp, 2), 2)
    partner = device(moved(at, "c", 1))
    far_y = device(moved(at, "y", 3 - 2 * lax.rem(at["y"], 2)))
    z_right, z_left = device(moved(at, "z", 1)), device(moved(at, "z", 3))
    x_right, x_left = device(moved(at, "x", 1)), device(moved(at, "x", 3))
    low_y = lax.rem(at["y"], 2)
    near_y = device(moved(at, "y", 1 + 2 * low_y))

    def shard(step, other_y=0, other_c=0):
        zz = lax.rem(z + step, 4)
        yy = lax.rem(half_y + other_y, 2)
        return zz * 4 + yy * 2 + lax.rem(c + other_c, 2)

    def quarter(i):
        return lax.rem(x + i, 4)

    def copy(slot, ref, there):
        return pltpu.make_async_remote_copy(
            src_ref=ref, dst_ref=ref, send_sem=send_sem.at[slot], recv_sem=recv_sem.at[slot],
            device_id=there, device_id_type=MESH,
        )

    def to_z_right(i):
        return copy(Z_RIGHT + i, w_all.at[dp, quarter(i)], z_right)

    def to_z_left(i):
        return copy(Z_LEFT + i, w_all.at[dp, quarter(i)], z_left)

    def to_z_far(i):
        if i == 0:
            return copy(Z_FAR, w_all.at[shard(3), quarter(0)], z_right)
        there = z_right if i == 1 else z_left
        return copy(Z_FAR + i, w_all.at[shard(3 if i == 1 else 1), quarter(i), :, low_y], there)

    def to_near_z(i):
        return copy(Y_NEAR_Z + i, w_all.at[shard(2), quarter(i), :, low_y], near_y)

    def to_near_x(k):
        return copy(Y_NEAR_X + k, w_all.at[shard(spread(k), 1), quarter(2), :, low_y], near_y)

    def to_far_y(k):
        return copy(Y_FAR + k, w_all.at[shard(spread(k)), x], far_y)

    def to_x_right(k):
        return copy(X_RIGHT + k, w_all.at[shard(spread(k), 1), x], x_right)

    def to_x_left(k):
        return copy(X_LEFT + k, w_all.at[shard(spread(k), 1), x], x_left)

    def to_x_far_right(k):
        return copy(X_FAR_RIGHT + k, w_all.at[shard(spread(k), 1), quarter(3), 0, low_y], x_right)

    def to_x_far_left(k):
        return copy(X_FAR_LEFT + k, w_all.at[shard(spread(k), 1), quarter(1), 1, low_y], x_left)

    def to_pair(k, other_y):
        return copy(PAIR + 4 * other_y + k, w_all.at[shard(spread(k), other_y)], partner)

    def strip(j):
        return pltpu.make_async_remote_copy(
            src_ref=x_ref.at[:, pl.ds(pl.multiple_of(j * 512 + (1 - c) * 256, 256), 256)],
            dst_ref=x_other.at[j],
            send_sem=send_sem.at[STRIP + j], recv_sem=recv_sem.at[STRIP + j],
            device_id=partner, device_id_type=MESH,
        )

    def project(s):
        lanes = pl.ds(pl.multiple_of(s * 256, 256), 256)
        acc[...] += jnp.dot(
            x_ref[:, lanes], w_all[s].reshape(256, COLS), preferred_element_type=F32
        )

    own = pltpu.make_async_copy(w_hbm, w_all.at[dp], load_sem)
    own.start()
    barrier_with(everyone(at))
    own.wait()
    sent = []

    def send(item):
        item.start()
        sent.append(item)

    for i in range(2):
        send(to_z_right(i))
        send(to_z_left(i))
        if i == 0:
            send(to_far_y(0))
    send(to_pair(0, 0))
    for j in range(8):
        send(strip(j))
    acc[...] = jnp.zeros_like(acc)

    def turn_own(j, carry):
        rows = pl.ds(pl.multiple_of(j * 256, 256), 256)
        lanes = pl.ds(pl.multiple_of(j * 512 + c * 256, 256), 256)
        xt[rows, :256] = x_ref[:, lanes].T
        return carry

    lax.fori_loop(0, 8, turn_own, 0)
    to_z_right(0).wait_recv()
    send(to_z_far(0))
    to_z_left(0).wait_recv()
    send(to_far_y(1))
    send(to_far_y(2))
    for i in (2, 3):
        send(to_z_right(i))
        send(to_z_left(i))
    for k in range(3):
        to_far_y(k).wait_recv()
        send(to_x_right(k))
        send(to_x_left(k))
    to_z_right(1).wait_recv()
    send(to_z_far(1))

    def pass_x(k):
        to_x_right(k).wait_recv()
        send(to_x_far_right(k))
        to_x_left(k).wait_recv()
        send(to_x_far_left(k))

    def pass_y(k):
        to_x_far_right(k).wait_recv()
        to_x_far_left(k).wait_recv()
        send(to_near_x(k))

    pass_x(0)
    to_z_far(0).wait_recv()
    send(to_far_y(3))
    for j in range(8):
        strip(j).wait_recv()

    def turn_other(j, carry):
        rows = pl.ds(pl.multiple_of(j * 256, 256), 256)
        xt[rows, 256:] = x_other[j].T
        return carry

    lax.fori_loop(0, 8, turn_other, 0)
    pass_x(1)
    for i in (1, 2):
        to_z_left(i).wait_recv()
    send(to_z_far(2))
    to_z_far(1).wait_recv()
    send(to_near_z(1))
    pass_y(0)
    to_far_y(3).wait_recv()
    send(to_x_right(3))
    send(to_x_left(3))
    to_z_left(3).wait_recv()
    send(to_z_far(3))
    send(to_pair(1, 0))
    for i in (2, 3):
        to_z_right(i).wait_recv()
    send(to_pair(2, 0))
    pass_x(2)
    pass_y(1)

    def near(k, carry):
        project(shard(spread(k)))
        return carry

    lax.fori_loop(0, 3, near, 0)
    for i in (2, 3):
        to_z_far(i).wait_recv()
        send(to_near_z(i))
    pass_x(3)
    pass_y(2)
    for i in (1, 2, 3):
        to_near_z(i).wait_recv()
    send(to_pair(3, 0))
    lax.fori_loop(3, 4, near, 0)
    pass_y(3)

    def far(k, carry):
        to_near_x(k).wait_recv()
        to_pair(k, 1).start()
        to_pair(k, 0).wait_recv()
        project(shard(spread(k), 0, 1))
        project(shard(spread(k), 1))

        @pl.when(k > 0)
        def _():
            to_pair(k - 1, 1).wait_recv()
            project(shard(spread(k - 1), 1, 1))

        return carry

    lax.fori_loop(0, 4, far, 0)
    to_pair(3, 1).wait_recv()
    project(shard(spread(3), 1, 1))

    kv_ref[WIN - 1] = acc[:, QW:].astype(BF16)

    def to_peer(step):
        return pltpu.make_async_remote_copy(
            src_ref=kv_ref.at[WIN - 1],
            dst_ref=kv_ref.at[WIN - 1 - step],
            send_sem=send_sem.at[PEER + step - 1],
            recv_sem=recv_sem.at[PEER + step - 1],
            device_id=(dp, lax.rem(seq + step, SEQN)),
            device_id_type=MESH,
        )

    for step in range(1, WIN):
        @pl.when(seq + step < SEQN)
        def _(step=step):
            to_peer(step).start()

    row0 = seq * BLK
    lane_pos = row0 + lax.broadcasted_iota(jnp.int32, (1, BLK), 1)
    sub_pos = row0 + lax.broadcasted_iota(jnp.int32, (BLK, HEAD), 0)
    doc_start = jnp.int32(0)
    starts = jnp.zeros((1, BLK), jnp.int32)
    keep = jnp.zeros((BLK, HEAD), jnp.int32)
    for doc in range(NDOC):
        doc_end = doc_start + len_ref[0, doc]
        starts = jnp.where((lane_pos >= doc_start) & (lane_pos < doc_end), doc_start, starts)
        keep = jnp.where((sub_pos >= doc_start) & (sub_pos < doc_end), flag_ref[0, doc], keep)
        doc_start = doc_end
    base = seq - (WIN - 1)
    low = jnp.maximum(WIN - 1 - seq, 0)

    for head in range(HEADS):
        lanes, rows = slice(head * HEAD, (head + 1) * HEAD), slice(head * BLK, (head + 1) * BLK)
        q = acc[:, lanes].astype(BF16)
        cot = jnp.where(keep > 0, cot_ref[:, lanes], jnp.zeros((), BF16))
        qr[rows, :] = q
        cr[rows, :] = cot
        qt[:, rows] = q.T
        ct[:, rows] = cot.T

    def score(back, top):
        j = WIN - 1 - back

        @pl.when(back > 0)
        def _():
            to_peer(back).wait_recv()

        key_pos = (base + j) * BLK + lax.broadcasted_iota(jnp.int32, (BLK, BLK), 0)
        allowed = (key_pos >= starts) & (key_pos <= lane_pos)
        mask = jnp.where(allowed, 0.0, -1e30)
        kt_buf[j] = kv_ref[j, :, :HEAD].T
        vt_buf[j] = kv_ref[j, :, HEAD:].T
        s = jnp.dot(kv_ref[j, :, :HEAD], qt[...], preferred_element_type=F32)
        s = s * (SCALE * LOG2E) + jnp.concatenate([mask] * HEADS, axis=1)
        s_buf[j] = s
        return jnp.maximum(top, jnp.max(s, axis=0, keepdims=True))

    top = lax.fori_loop(0, WIN - low, score, jnp.full((1, HEADS * BLK), -1e30, F32))
    total[...] = jnp.zeros_like(total)

    def weigh(j, mass):
        p = jnp.exp2(s_buf[j] - top)
        s_buf[j] = p
        total[...] += jnp.dot(vt_buf[j], p.astype(BF16), preferred_element_type=F32)
        return mass + jnp.sum(p, axis=0, keepdims=True)

    mass = lax.fori_loop(low, WIN, weigh, jnp.zeros((1, HEADS * BLK), F32))
    inverse = 1.0 / mass
    out = (total[...] * inverse).astype(BF16)
    for head in range(HEADS):
        o_ref[:, head * HEAD : (head + 1) * HEAD] = out[:, head * BLK : (head + 1) * BLK].T
    delta = jnp.sum(ct[...].astype(F32) * out.astype(F32), axis=0, keepdims=True)
    total[...] = jnp.zeros_like(total)

    def kv_copy(step):
        return pltpu.make_async_remote_copy(
            src_ref=dkv_ref.at[WIN - 1 - step],
            dst_ref=dkv_in.at[step - 1],
            send_sem=kv_send.at[step - 1],
            recv_sem=kv_recv.at[step - 1],
            device_id=(dp, lax.rem(seq + SEQN - step, SEQN)),
            device_id_type=MESH,
        )

    def back(j, carry):
        p = s_buf[j] * inverse
        dp = jnp.dot(kv_ref[j, :, HEAD:], ct[...], preferred_element_type=F32)
        ds = (p * (dp - delta)).astype(BF16)
        total[...] += jnp.dot(kt_buf[j], ds, preferred_element_type=F32)
        dk = jnp.dot(ds, qr[...], preferred_element_type=F32) * SCALE
        dkv_ref[j, :, :HEAD] = dk.astype(BF16)
        dkv_ref[j, :, HEAD:] = jnp.dot(p.astype(BF16), cr[...], preferred_element_type=F32).astype(BF16)

        @pl.when(j < WIN - 1)
        def _():
            kv_copy(WIN - 1 - j).start()

        return carry

    lax.fori_loop(low, WIN, back, 0)
    for head in range(HEADS):
        dq = (total[:, head * BLK : (head + 1) * BLK] * SCALE).astype(BF16)
        dproj[pl.ds(0, BLK), head * HEAD : (head + 1) * HEAD] = dq.T

    def pair_copy(index, src, columns):
        return pltpu.make_async_remote_copy(
            src_ref=src,
            dst_ref=dproj.at[pl.ds(BLK, BLK), columns],
            send_sem=pair_send.at[index],
            recv_sem=pair_recv.at[index],
            device_id=partner,
            device_id_type=MESH,
        )

    pair_q = pair_copy(0, dproj.at[pl.ds(0, BLK), pl.ds(0, QW)], pl.ds(0, QW))
    pair_q.start()

    def ring_copy(color, stage, buf, src, there):
        k = (color * 3 + stage) * 6 + buf
        return pltpu.make_async_remote_copy(
            src_ref=src,
            dst_ref=bufs[color][stage].at[buf],
            send_sem=ring_send.at[k],
            recv_sem=ring_recv.at[k],
            device_id=device(there),
            device_id_type=MESH,
        )

    def stage_of(color, stage):
        order = PARTS[color][2]
        dims = [d for d in "zyx" if d in order[stage:]]
        axis = order[stage]
        me = at[axis]
        return (
            dims, axis, me,
            lax.rem(me + 1, 4), lax.rem(me + 2, 4), lax.rem(me + 3, 4),
            moved(at, axis, 1), moved(at, axis, 3),
        )

    started = []

    def open_stage(color, stage):
        dims, axis, me, right, across, left, to_right, to_left = stage_of(color, stage)
        src = data[color][stage]
        for buf, index, half, there in (
            (0, across, 0, to_right),
            (1, across, 1, to_left),
            (3, right, 1, to_right),
            (4, left, 0, to_left),
        ):
            copy = ring_copy(color, stage, buf, src.at[cut(dims, axis, index, half)], there)
            copy.start()
            started.append(copy)

    def pass_on(color, stage):
        dims, axis, me, right, across, left, to_right, to_left = stage_of(color, stage)
        src = data[color][stage]
        for first, buf, index, half, there in ((0, 2, right, 0, to_right), (1, 5, left, 1, to_left)):
            where = cut(dims, axis, index, half)
            ring_copy(color, stage, first, src.at[where], there).wait_recv()
            src[where] = (src[where].astype(F32) + bufs[color][stage][first].astype(F32)).astype(BF16)
            copy = ring_copy(color, stage, buf, src.at[where], there)
            copy.start()
            started.append(copy)

    def close_stage(color, stage):
        dims, axis, me, right, across, left, to_right, to_left = stage_of(color, stage)
        src, got = data[color][stage], bufs[color][stage]
        for half in (0, 1):
            where = cut(dims, axis, me, half)
            summed = src[where].astype(F32)
            for buf in (2 + half, 4 + half):
                ring_copy(color, stage, buf, src.at[where], to_right).wait_recv()
                summed = summed + got[buf].astype(F32)
            if stage < 2:
                data[color][stage + 1][(slice(None),) * (len(dims) - 1) + (half,)] = summed.astype(BF16)
            else:
                first, width, _ = PARTS[color]
                wg_ref[16 * half : 16 * half + 16, first : first + width] = summed

    def multiply(color):
        first, width, _ = PARTS[color]

        def body(z, carry):
            rows = pl.ds(pl.multiple_of(z * 512, 512), 512)
            part = jnp.dot(xt[rows, :], dproj[:, first : first + width], preferred_element_type=F32)
            data[color][0][z] = part.astype(BF16).reshape(4, 4, 2, 16, width)
            return carry

        lax.fori_loop(0, 4, body, 0)

    pair_q.wait_recv()
    for color in range(5):
        multiply(color)
        open_stage(color, 0)

    pairs = dkv_ref[WIN - 1].astype(F32)
    for step in range(1, WIN):
        @pl.when(seq + step < SEQN)
        def _(step=step):
            kv_copy(step).wait_recv()

        @pl.when(seq + step >= SEQN)
        def _(step=step):
            dkv_in[step - 1] = jnp.zeros((BLK, 2 * HEAD), BF16)

        pairs = pairs + dkv_in[step - 1].astype(F32)
    dproj[pl.ds(0, BLK), QW:] = pairs.astype(BF16)
    pair_kv = pair_copy(1, dproj.at[pl.ds(0, BLK), pl.ds(QW, 2 * HEAD)], pl.ds(QW, 2 * HEAD))
    pair_kv.start()
    pair_kv.wait_recv()
    multiply(5)
    open_stage(5, 0)
    for color in (1, 2, 0):
        pass_on(color, 0)

    def grad_chunk(n, carry):
        rows = pl.ds(pl.multiple_of(n * 512, 512), 512)
        ig_ref[:, rows] = lax.dot_general(
            dproj[pl.ds(0, BLK), :], w_all[pl.ds(2 * n, 2)].reshape(512, COLS), NT, preferred_element_type=F32
        ).astype(BF16)
        return carry

    lax.fori_loop(0, 8, grad_chunk, 0)

    for step in STEPS:
        color, stage = int(step[1]), int(step[2])
        if step[0] == "r":
            pass_on(color, stage)
        else:
            close_stage(color, stage)
            if stage < 2:
                open_stage(color, stage + 1)
    for item in started:
        item.wait_send()
    pair_q.wait_send()
    pair_kv.wait_send()
    for step in range(1, WIN):
        @pl.when(seq >= step)
        def _(step=step):
            kv_copy(step).wait_send()
    for item in sent:
        item.wait_send()

    def finish(k, carry):
        to_pair(k, 1).wait_send()
        return carry

    lax.fori_loop(0, 4, finish, 0)
    for step in range(1, WIN):
        @pl.when(seq + step < SEQN)
        def _(step=step):
            to_peer(step).wait_send()


VM = pl.BlockSpec(memory_space=pltpu.VMEM)
SM = pl.BlockSpec(memory_space=pltpu.SMEM)
ANY = pl.BlockSpec(memory_space=pl.ANY)
DMA = pltpu.SemaphoreType.DMA
LIMIT = 60 * 1024 * 1024


def shape(dims, kind=BF16):
    return jax.ShapeDtypeStruct(dims, kind)


def shards(inputs, weights, cotangent, doc_lengths, kept_flags):
    held, received = [], []
    for _, width, order in PARTS:
        for stage in range(3):
            dims = (4,) * (3 - stage)
            held.append(pltpu.VMEM(dims + (2, 16, width), BF16))
            received.append(pltpu.VMEM((6,) + dims[1:] + (16, width), BF16))
    rows = HEADS * BLK
    attention, inputs_grad, weights_grad = pl.pallas_call(
        layer_kernel,
        out_shape=(pltpu.VMEM((BLK, QW), BF16), pltpu.VMEM((BLK, D), BF16), pltpu.VMEM((32, COLS), F32)),
        in_specs=[SM, SM, VM, ANY, VM],
        out_specs=(VM, VM, VM),
        scratch_shapes=[
            pltpu.VMEM((16, 4, 2, 2, 16, COLS), BF16),
            pltpu.VMEM((BLK, COLS), F32),
            pltpu.VMEM((8, BLK, 256), BF16),
            pltpu.VMEM((2048, 2 * BLK), BF16),
            pltpu.VMEM((WIN, BLK, 2 * HEAD), BF16),
            pltpu.VMEM((WIN, BLK, rows), F32),
            pltpu.VMEM((WIN, HEAD, BLK), BF16),
            pltpu.VMEM((WIN, HEAD, BLK), BF16),
            pltpu.VMEM((HEAD, rows), BF16),
            pltpu.VMEM((HEAD, rows), BF16),
            pltpu.VMEM((rows, HEAD), BF16),
            pltpu.VMEM((rows, HEAD), BF16),
            pltpu.VMEM((HEAD, rows), F32),
            pltpu.VMEM((WIN, BLK, 2 * HEAD), BF16),
            pltpu.VMEM((2 * BLK, COLS), BF16),
            pltpu.VMEM((WIN - 1, BLK, 2 * HEAD), BF16),
        ]
        + held
        + received
        + [DMA, DMA((SLOTS,)), DMA((SLOTS,)), DMA((2,)), DMA((2,)), DMA((WIN - 1,)), DMA((WIN - 1,)), DMA((18 * len(PARTS),)), DMA((18 * len(PARTS),))],
        compiler_params=pltpu.CompilerParams(collective_id=0, has_side_effects=True, vmem_limit_bytes=LIMIT),
        name="layer",
    )(doc_lengths, kept_flags, inputs[0], weights.reshape(4, 2, 2, 16, COLS), cotangent[0])
    return (attention[None], inputs_grad[None], weights_grad)


def solution(mesh):
    in_specs = (
        P("dp", "seq", None),
        P("dp", None),
        P("dp", "seq", None),
        P("dp", None),
        P("dp", None),
    )
    out_specs = (P("dp", "seq", None), P("dp", "seq", None), P(("dp", "seq"), None))
    return jax.shard_map(shards, mesh=mesh, in_specs=in_specs, out_specs=out_specs, check_vma=False)
```

```python
import math

import jax
import jax.numpy as jnp
from jax import lax
from jax.experimental import pallas as pl
from jax.experimental.pallas import tpu as pltpu
from jax.sharding import PartitionSpec as P

MESH = pl.DeviceIdType.MESH
HEAD = 128
HEADS = 8
BLK = 256
WIN = 5
D = 4096
QW = 1024
COLS = 1280
NDOC = 8
SEQN = 8
SCALE = 1.0 / math.sqrt(HEAD)
LOG2E = math.log2(math.e)
F32 = jnp.float32
BF16 = jnp.bfloat16
NT = (((1,), (1,)), ((), ()))
PARTS = (
    (0, 256, "xyz"), (256, 128, "yzx"), (384, 128, "zxy"), (512, 256, "yzx"), (768, 256, "zxy"), (1024, 256, "xyz"),
)
STEPS = (
    "e10 e20 r30 r40 e00 r50 e11 e21 e30 e40 e01 e12 e22 e50 e31 e41 e02 e51 e32 e42 e52"
).split()


def place():
    dp = lax.axis_index("dp")
    seq = lax.axis_index("seq")
    z = lax.div(dp, 4)
    y = lax.rem(lax.div(dp, 2), 2) * 2 + lax.div(seq, 4)
    return {"z": z, "y": y, "x": lax.rem(seq, 4), "c": lax.rem(dp, 2)}


def device(at):
    dp = at["z"] * 4 + lax.div(at["y"], 2) * 2 + at["c"]
    return (dp, lax.rem(at["y"], 2) * 4 + at["x"])


def moved(at, axis, step):
    count = 2 if axis == "c" else 4
    there = dict(at)
    there[axis] = lax.rem(at[axis] + step, count)
    return there


def barrier_with(devices):
    sem = pltpu.get_barrier_semaphore()
    for there in devices:
        pl.semaphore_signal(sem, inc=1, device_id=there, device_id_type=MESH)
    pl.semaphore_wait(sem, len(devices))


def seq_peers():
    dp = lax.axis_index("dp")
    seq = lax.axis_index("seq")
    return [(dp, lax.rem(seq + step, SEQN)) for step in range(1, SEQN)]


def everyone(at):
    far_y = moved(at, "y", 3 - 2 * lax.rem(at["y"], 2))
    ring = [device(there) for there in (moved(at, "z", 1), moved(at, "z", 2), moved(at, "z", 3), far_y, moved(at, "y", 2))]
    return seq_peers() + ring + [device(moved(at, "c", 1))]


def spread(k):
    return k + lax.div(k, 2) * (1 - 2 * lax.rem(k, 2))


Z_RIGHT, Z_LEFT, Z_FAR, Y_FAR, X_RIGHT, X_LEFT, X_FAR_RIGHT, X_FAR_LEFT, PAIR, STRIP, PEER, SLOTS = (
    0, 4, 8, 12, 16, 20, 24, 28, 32, 40, 48, 52
)


def whole(dims, axis, index):
    return tuple(index if d == axis else slice(None) for d in dims)


def cut(dims, axis, index, half):
    return tuple(index if d == axis else slice(None) for d in dims) + (half,)


def layer_kernel(
    len_ref, flag_ref, x_ref, w_hbm, cot_ref, o_ref, ig_ref, wg_ref,
    w_all, acc, x_other, xt, kv_ref, s_buf, kt_buf, vt_buf, qt, ct, qr, cr, total, dkv_ref, dproj, dkv_in,
    *rest,
):
    count = len(PARTS)
    data = [rest[3 * part : 3 * part + 3] for part in range(count)]
    bufs = [rest[3 * (count + part) : 3 * (count + part) + 3] for part in range(count)]
    load_sem, send_sem, recv_sem, pair_send, pair_recv, kv_send, kv_recv, ring_send, ring_recv = rest[6 * count :]
    dp = lax.axis_index("dp")
    seq = lax.axis_index("seq")
    at = place()
    z, x, c = at["z"], at["x"], at["c"]
    half_y = lax.rem(lax.div(dp, 2), 2)
    partner = device(moved(at, "c", 1))
    far_y = device(moved(at, "y", 3 - 2 * lax.rem(at["y"], 2)))
    z_right, z_left = device(moved(at, "z", 1)), device(moved(at, "z", 3))
    x_right, x_left = device(moved(at, "x", 1)), device(moved(at, "x", 3))

    def shard(step, other_y=0, other_c=0):
        zz = lax.rem(z + step, 4)
        yy = lax.rem(half_y + other_y, 2)
        return zz * 4 + yy * 2 + lax.rem(c + other_c, 2)

    def quarter(i):
        return lax.rem(x + i, 4)

    def copy(slot, ref, there):
        return pltpu.make_async_remote_copy(
            src_ref=ref, dst_ref=ref, send_sem=send_sem.at[slot], recv_sem=recv_sem.at[slot],
            device_id=there, device_id_type=MESH,
        )

    def to_z_right(i):
        return copy(Z_RIGHT + i, w_all.at[dp, quarter(i)], z_right)

    def to_z_left(i):
        return copy(Z_LEFT + i, w_all.at[dp, quarter(i)], z_left)

    def to_z_far(i):
        if i < 2:
            return copy(Z_FAR + i, w_all.at[shard(3), quarter(i)], z_right)
        return copy(Z_FAR + i, w_all.at[shard(1), quarter(i)], z_left)

    def to_far_y(k):
        return copy(Y_FAR + k, w_all.at[shard(spread(k)), x], far_y)

    def to_x_right(k):
        return copy(X_RIGHT + k, w_all.at[shard(spread(k), 1), x], x_right)

    def to_x_left(k):
        return copy(X_LEFT + k, w_all.at[shard(spread(k), 1), x], x_left)

    def to_x_far_right(k):
        return copy(X_FAR_RIGHT + k, w_all.at[shard(spread(k), 1), quarter(3), 0], x_right)

    def to_x_far_left(k):
        return copy(X_FAR_LEFT + k, w_all.at[shard(spread(k), 1), quarter(1), 1], x_left)

    def to_pair(k, other_y):
        return copy(PAIR + 4 * other_y + k, w_all.at[shard(spread(k), other_y)], partner)

    def strip(j):
        return pltpu.make_async_remote_copy(
            src_ref=x_ref.at[:, pl.ds(pl.multiple_of(j * 512 + (1 - c) * 256, 256), 256)],
            dst_ref=x_other.at[j],
            send_sem=send_sem.at[STRIP + j], recv_sem=recv_sem.at[STRIP + j],
            device_id=partner, device_id_type=MESH,
        )

    def project(s):
        lanes = pl.ds(pl.multiple_of(s * 256, 256), 256)
        acc[...] += jnp.dot(
            x_ref[:, lanes], w_all[s].reshape(256, COLS), preferred_element_type=F32
        )

    own = pltpu.make_async_copy(w_hbm, w_all.at[dp], load_sem)
    own.start()
    barrier_with(everyone(at))
    own.wait()
    sent = []

    def send(item):
        item.start()
        sent.append(item)

    for i in range(2):
        send(to_z_right(i))
        send(to_z_left(i))
        if i == 0:
            send(to_far_y(0))
    send(to_pair(0, 0))
    for j in range(8):
        send(strip(j))
    acc[...] = jnp.zeros_like(acc)

    def turn_own(j, carry):
        rows = pl.ds(pl.multiple_of(j * 256, 256), 256)
        lanes = pl.ds(pl.multiple_of(j * 512 + c * 256, 256), 256)
        xt[rows, :256] = x_ref[:, lanes].T
        return carry

    lax.fori_loop(0, 8, turn_own, 0)
    to_z_right(0).wait_recv()
    send(to_z_far(0))
    to_z_left(0).wait_recv()
    send(to_far_y(1))
    send(to_far_y(2))
    for i in (2, 3):
        send(to_z_right(i))
        send(to_z_left(i))

    def to_x(k):
        to_far_y(k).wait_recv()
        send(to_x_right(k))
        send(to_x_left(k))

    def pass_x(k):
        to_x_right(k).wait_recv()
        send(to_x_far_right(k))
        to_x_left(k).wait_recv()
        send(to_x_far_left(k))

    def far_done(k):
        to_x_far_right(k).wait_recv()
        to_x_far_left(k).wait_recv()
        send(to_pair(k, 1))

    def near_own(k, carry):
        project(shard(spread(k)))
        return carry

    def near_pair(k, carry):
        to_pair(k, 0).wait_recv()
        project(shard(spread(k), 0, 1))
        return carry

    def far_own(k, carry):
        project(shard(spread(k), 1))
        return carry

    def far_pair(k, carry):
        to_pair(k, 1).wait_recv()
        project(shard(spread(k), 1, 1))
        return carry

    def turn_other(j, carry):
        rows = pl.ds(pl.multiple_of(j * 256, 256), 256)
        strip(j).wait_recv()
        xt[rows, 256:] = x_other[j].T
        return carry

    to_x(0)
    lax.fori_loop(0, 8, turn_other, 0)
    to_z_right(1).wait_recv()
    send(to_z_far(1))
    to_x(1)
    pass_x(0)
    to_z_far(0).wait_recv()
    send(to_far_y(3))
    for i in (1, 2):
        to_z_left(i).wait_recv()
    send(to_z_far(2))
    to_x(2)
    to_z_left(3).wait_recv()
    send(to_z_far(3))
    send(to_pair(1, 0))
    pass_x(1)
    to_x(3)
    for i in (2, 3):
        to_z_right(i).wait_recv()
    send(to_pair(2, 0))
    far_done(0)
    lax.fori_loop(0, 2, near_own, 0)
    pass_x(2)
    lax.fori_loop(0, 2, near_pair, 0)
    for i in (1, 2, 3):
        to_z_far(i).wait_recv()
    send(to_pair(3, 0))
    far_done(1)
    lax.fori_loop(2, 4, near_own, 0)
    pass_x(3)
    far_done(2)
    lax.fori_loop(2, 4, near_pair, 0)
    lax.fori_loop(0, 3, far_own, 0)
    far_done(3)
    lax.fori_loop(0, 3, far_pair, 0)
    lax.fori_loop(3, 4, far_own, 0)
    lax.fori_loop(3, 4, far_pair, 0)

    kv_ref[WIN - 1] = acc[:, QW:].astype(BF16)

    def to_peer(step):
        return pltpu.make_async_remote_copy(
            src_ref=kv_ref.at[WIN - 1],
            dst_ref=kv_ref.at[WIN - 1 - step],
            send_sem=send_sem.at[PEER + step - 1],
            recv_sem=recv_sem.at[PEER + step - 1],
            device_id=(dp, lax.rem(seq + step, SEQN)),
            device_id_type=MESH,
        )

    for step in range(1, WIN):
        @pl.when(seq + step < SEQN)
        def _(step=step):
            to_peer(step).start()

    row0 = seq * BLK
    lane_pos = row0 + lax.broadcasted_iota(jnp.int32, (1, BLK), 1)
    sub_pos = row0 + lax.broadcasted_iota(jnp.int32, (BLK, HEAD), 0)
    doc_start = jnp.int32(0)
    starts = jnp.zeros((1, BLK), jnp.int32)
    keep = jnp.zeros((BLK, HEAD), jnp.int32)
    for doc in range(NDOC):
        doc_end = doc_start + len_ref[0, doc]
        starts = jnp.where((lane_pos >= doc_start) & (lane_pos < doc_end), doc_start, starts)
        keep = jnp.where((sub_pos >= doc_start) & (sub_pos < doc_end), flag_ref[0, doc], keep)
        doc_start = doc_end
    base = seq - (WIN - 1)
    low = jnp.maximum(WIN - 1 - seq, 0)

    for head in range(HEADS):
        lanes, rows = slice(head * HEAD, (head + 1) * HEAD), slice(head * BLK, (head + 1) * BLK)
        q = acc[:, lanes].astype(BF16)
        cot = jnp.where(keep > 0, cot_ref[:, lanes], jnp.zeros((), BF16))
        qr[rows, :] = q
        cr[rows, :] = cot
        qt[:, rows] = q.T
        ct[:, rows] = cot.T

    def score(back, top):
        j = WIN - 1 - back

        @pl.when(back > 0)
        def _():
            to_peer(back).wait_recv()

        key_pos = (base + j) * BLK + lax.broadcasted_iota(jnp.int32, (BLK, BLK), 0)
        allowed = (key_pos >= starts) & (key_pos <= lane_pos)
        mask = jnp.where(allowed, 0.0, -1e30)
        kt_buf[j] = kv_ref[j, :, :HEAD].T
        vt_buf[j] = kv_ref[j, :, HEAD:].T
        s = jnp.dot(kv_ref[j, :, :HEAD], qt[...], preferred_element_type=F32)
        s = s * (SCALE * LOG2E) + jnp.concatenate([mask] * HEADS, axis=1)
        s_buf[j] = s
        return jnp.maximum(top, jnp.max(s, axis=0, keepdims=True))

    top = lax.fori_loop(0, WIN - low, score, jnp.full((1, HEADS * BLK), -1e30, F32))
    total[...] = jnp.zeros_like(total)

    def weigh(j, mass):
        p = jnp.exp2(s_buf[j] - top)
        s_buf[j] = p
        total[...] += jnp.dot(vt_buf[j], p.astype(BF16), preferred_element_type=F32)
        return mass + jnp.sum(p, axis=0, keepdims=True)

    mass = lax.fori_loop(low, WIN, weigh, jnp.zeros((1, HEADS * BLK), F32))
    inverse = 1.0 / mass
    out = (total[...] * inverse).astype(BF16)
    for head in range(HEADS):
        o_ref[:, head * HEAD : (head + 1) * HEAD] = out[:, head * BLK : (head + 1) * BLK].T
    delta = jnp.sum(ct[...].astype(F32) * out.astype(F32), axis=0, keepdims=True)
    total[...] = jnp.zeros_like(total)

    def kv_copy(step):
        return pltpu.make_async_remote_copy(
            src_ref=dkv_ref.at[WIN - 1 - step],
            dst_ref=dkv_in.at[step - 1],
            send_sem=kv_send.at[step - 1],
            recv_sem=kv_recv.at[step - 1],
            device_id=(dp, lax.rem(seq + SEQN - step, SEQN)),
            device_id_type=MESH,
        )

    def back(j, carry):
        p = s_buf[j] * inverse
        dp = jnp.dot(kv_ref[j, :, HEAD:], ct[...], preferred_element_type=F32)
        ds = (p * (dp - delta)).astype(BF16)
        total[...] += jnp.dot(kt_buf[j], ds, preferred_element_type=F32)
        dk = jnp.dot(ds, qr[...], preferred_element_type=F32) * SCALE
        dkv_ref[j, :, :HEAD] = dk.astype(BF16)
        dkv_ref[j, :, HEAD:] = jnp.dot(p.astype(BF16), cr[...], preferred_element_type=F32).astype(BF16)

        @pl.when(j < WIN - 1)
        def _():
            kv_copy(WIN - 1 - j).start()

        return carry

    lax.fori_loop(low, WIN, back, 0)
    for head in range(HEADS):
        dq = (total[:, head * BLK : (head + 1) * BLK] * SCALE).astype(BF16)
        dproj[pl.ds(0, BLK), head * HEAD : (head + 1) * HEAD] = dq.T

    def pair_copy(index, src, columns):
        return pltpu.make_async_remote_copy(
            src_ref=src,
            dst_ref=dproj.at[pl.ds(BLK, BLK), columns],
            send_sem=pair_send.at[index],
            recv_sem=pair_recv.at[index],
            device_id=partner,
            device_id_type=MESH,
        )

    pair_q = pair_copy(0, dproj.at[pl.ds(0, BLK), pl.ds(0, QW)], pl.ds(0, QW))
    pair_q.start()

    def ring_copy(color, stage, buf, src, there):
        k = (color * 3 + stage) * 6 + buf
        return pltpu.make_async_remote_copy(
            src_ref=src,
            dst_ref=bufs[color][stage].at[buf],
            send_sem=ring_send.at[k],
            recv_sem=ring_recv.at[k],
            device_id=device(there),
            device_id_type=MESH,
        )

    def stage_of(color, stage):
        order = PARTS[color][2]
        dims = [d for d in "zyx" if d in order[stage:]]
        axis = order[stage]
        me = at[axis]
        return (
            dims, axis, me,
            lax.rem(me + 1, 4), lax.rem(me + 2, 4), lax.rem(me + 3, 4),
            moved(at, axis, 1), moved(at, axis, 3),
        )

    started = []

    def open_stage(color, stage):
        dims, axis, me, right, across, left, to_right, to_left = stage_of(color, stage)
        src = data[color][stage]
        if stage == 0:
            pieces = (
                (0, cut(dims, axis, across, 0), to_right),
                (1, cut(dims, axis, across, 1), to_left),
                (3, cut(dims, axis, right, 1), to_right),
                (4, cut(dims, axis, left, 0), to_left),
            )
        else:
            pieces = (
                (2, whole(dims, axis, across), moved(at, axis, 2)),
                (0, whole(dims, axis, right), to_right),
                (1, whole(dims, axis, left), to_left),
            )
        for buf, where, there in pieces:
            copy = ring_copy(color, stage, buf, src.at[where], there)
            copy.start()
            started.append(copy)

    def pass_on(color):
        dims, axis, me, right, across, left, to_right, to_left = stage_of(color, 0)
        src = data[color][0]
        for first, buf, index, half, there in ((0, 2, right, 0, to_right), (1, 5, left, 1, to_left)):
            where = cut(dims, axis, index, half)
            ring_copy(color, 0, first, src.at[where], there).wait_recv()
            src[where] = (src[where].astype(F32) + bufs[color][0][first].astype(F32)).astype(BF16)
            copy = ring_copy(color, 0, buf, src.at[where], there)
            copy.start()
            started.append(copy)

    def close_stage(color, stage):
        dims, axis, me, right, across, left, to_right, to_left = stage_of(color, stage)
        src, got = data[color][stage], bufs[color][stage]
        if stage == 0:
            for half in (0, 1):
                where = cut(dims, axis, me, half)
                summed = src[where].astype(F32)
                for buf in (2 + half, 4 + half):
                    ring_copy(color, 0, buf, src.at[where], to_right).wait_recv()
                    summed = summed + got[buf].astype(F32)
                data[color][1][(slice(None),) * (len(dims) - 1) + (half,)] = summed.astype(BF16)
            return
        where = whole(dims, axis, me)
        summed = src[where].astype(F32)
        for buf in range(3):
            ring_copy(color, stage, buf, src.at[where], to_right).wait_recv()
            summed = summed + got[buf].astype(F32)
        if stage == 1:
            data[color][2][...] = summed.astype(BF16)
        else:
            first, width, _ = PARTS[color]
            wg_ref[:, first : first + width] = summed.reshape(32, width)

    def multiply(color):
        first, width, _ = PARTS[color]

        def body(z, carry):
            rows = pl.ds(pl.multiple_of(z * 512, 512), 512)
            part = jnp.dot(xt[rows, :], dproj[:, first : first + width], preferred_element_type=F32)
            data[color][0][z] = part.astype(BF16).reshape(4, 4, 2, 16, width)
            return carry

        lax.fori_loop(0, 4, body, 0)

    pair_q.wait_recv()
    for color in range(5):
        multiply(color)
        open_stage(color, 0)

    pairs = dkv_ref[WIN - 1].astype(F32)
    for step in range(1, WIN):
        @pl.when(seq + step < SEQN)
        def _(step=step):
            kv_copy(step).wait_recv()

        @pl.when(seq + step >= SEQN)
        def _(step=step):
            dkv_in[step - 1] = jnp.zeros((BLK, 2 * HEAD), BF16)

        pairs = pairs + dkv_in[step - 1].astype(F32)
    dproj[pl.ds(0, BLK), QW:] = pairs.astype(BF16)
    pair_kv = pair_copy(1, dproj.at[pl.ds(0, BLK), pl.ds(QW, 2 * HEAD)], pl.ds(QW, 2 * HEAD))
    pair_kv.start()
    pair_kv.wait_recv()
    multiply(5)
    open_stage(5, 0)
    for color in (1, 2, 0):
        pass_on(color)

    def grad_chunk(n, carry):
        rows = pl.ds(pl.multiple_of(n * 512, 512), 512)
        ig_ref[:, rows] = lax.dot_general(
            dproj[pl.ds(0, BLK), :], w_all[pl.ds(2 * n, 2)].reshape(512, COLS), NT, preferred_element_type=F32
        ).astype(BF16)
        return carry

    lax.fori_loop(0, 8, grad_chunk, 0)

    for step in STEPS:
        color, stage = int(step[1]), int(step[2])
        if step[0] == "r":
            pass_on(color)
        else:
            close_stage(color, stage)
            if stage < 2:
                open_stage(color, stage + 1)
    for item in started:
        item.wait_send()
    pair_q.wait_send()
    pair_kv.wait_send()
    for step in range(1, WIN):
        @pl.when(seq >= step)
        def _(step=step):
            kv_copy(step).wait_send()
    for item in sent:
        item.wait_send()

    for step in range(1, WIN):
        @pl.when(seq + step < SEQN)
        def _(step=step):
            to_peer(step).wait_send()


VM = pl.BlockSpec(memory_space=pltpu.VMEM)
SM = pl.BlockSpec(memory_space=pltpu.SMEM)
ANY = pl.BlockSpec(memory_space=pl.ANY)
DMA = pltpu.SemaphoreType.DMA
LIMIT = 60 * 1024 * 1024


def shape(dims, kind=BF16):
    return jax.ShapeDtypeStruct(dims, kind)


def shards(inputs, weights, cotangent, doc_lengths, kept_flags):
    held, received = [], []
    for _, width, order in PARTS:
        for stage in range(3):
            dims = (4,) * (3 - stage)
            held.append(pltpu.VMEM(dims + (2, 16, width), BF16))
            received.append(pltpu.VMEM(((6,) + dims[1:] if stage == 0 else (3,) + dims[1:] + (2,)) + (16, width), BF16))
    rows = HEADS * BLK
    attention, inputs_grad, weights_grad = pl.pallas_call(
        layer_kernel,
        out_shape=(pltpu.VMEM((BLK, QW), BF16), pltpu.VMEM((BLK, D), BF16), pltpu.VMEM((32, COLS), F32)),
        in_specs=[SM, SM, VM, ANY, VM],
        out_specs=(VM, VM, VM),
        scratch_shapes=[
            pltpu.VMEM((16, 4, 2, 32, COLS), BF16),
            pltpu.VMEM((BLK, COLS), F32),
            pltpu.VMEM((8, BLK, 256), BF16),
            pltpu.VMEM((2048, 2 * BLK), BF16),
            pltpu.VMEM((WIN, BLK, 2 * HEAD), BF16),
            pltpu.VMEM((WIN, BLK, rows), F32),
            pltpu.VMEM((WIN, HEAD, BLK), BF16),
            pltpu.VMEM((WIN, HEAD, BLK), BF16),
            pltpu.VMEM((HEAD, rows), BF16),
            pltpu.VMEM((HEAD, rows), BF16),
            pltpu.VMEM((rows, HEAD), BF16),
            pltpu.VMEM((rows, HEAD), BF16),
            pltpu.VMEM((HEAD, rows), F32),
            pltpu.VMEM((WIN, BLK, 2 * HEAD), BF16),
            pltpu.VMEM((2 * BLK, COLS), BF16),
            pltpu.VMEM((WIN - 1, BLK, 2 * HEAD), BF16),
        ]
        + held
        + received
        + [DMA, DMA((SLOTS,)), DMA((SLOTS,)), DMA((2,)), DMA((2,)), DMA((WIN - 1,)), DMA((WIN - 1,)), DMA((18 * len(PARTS),)), DMA((18 * len(PARTS),))],
        compiler_params=pltpu.CompilerParams(collective_id=0, has_side_effects=True, vmem_limit_bytes=LIMIT),
        name="layer",
    )(doc_lengths, kept_flags, inputs[0], weights.reshape(4, 2, 32, COLS), cotangent[0])
    return (attention[None], inputs_grad[None], weights_grad)


def solution(mesh):
    in_specs = (
        P("dp", "seq", None),
        P("dp", None),
        P("dp", "seq", None),
        P("dp", None),
        P("dp", None),
    )
    out_specs = (P("dp", "seq", None), P("dp", "seq", None), P(("dp", "seq"), None))
    return jax.shard_map(shards, mesh=mesh, in_specs=in_specs, out_specs=out_specs, check_vma=False)
```

```python
import math

import jax
import jax.numpy as jnp
from jax import lax
from jax.experimental import pallas as pl
from jax.experimental.pallas import tpu as pltpu
from jax.sharding import PartitionSpec as P

MESH = pl.DeviceIdType.MESH
HEAD = 128
HEADS = 8
BLK = 256
WIN = 5
D = 4096
QW = 1024
COLS = 1280
NDOC = 8
SEQN = 8
SCALE = 1.0 / math.sqrt(HEAD)
LOG2E = math.log2(math.e)
F32 = jnp.float32
BF16 = jnp.bfloat16
NT = (((1,), (1,)), ((), ()))
PARTS = (
    (0, 256, "xyz"), (256, 256, "yzx"), (512, 256, "zxy"), (768, 128, "xyz"), (896, 128, "yzx"), (1024, 128, "zxy"), (1152, 128, "xyz"),
)
STEPS = (
    "r30 r40 e00 e10 e20 r50 r60 e30 e40 e01 e11 e21 e50 e60 e31 e41 e02 e12 e22 e51 e61 e32 e42 e52 e62"
).split()


def place():
    dp = lax.axis_index("dp")
    seq = lax.axis_index("seq")
    z = lax.div(dp, 4)
    y = lax.rem(lax.div(dp, 2), 2) * 2 + lax.div(seq, 4)
    return {"z": z, "y": y, "x": lax.rem(seq, 4), "c": lax.rem(dp, 2)}


def device(at):
    dp = at["z"] * 4 + lax.div(at["y"], 2) * 2 + at["c"]
    return (dp, lax.rem(at["y"], 2) * 4 + at["x"])


def moved(at, axis, step):
    count = 2 if axis == "c" else 4
    there = dict(at)
    there[axis] = lax.rem(at[axis] + step, count)
    return there


def barrier_with(devices):
    sem = pltpu.get_barrier_semaphore()
    for there in devices:
        pl.semaphore_signal(sem, inc=1, device_id=there, device_id_type=MESH)
    pl.semaphore_wait(sem, len(devices))


def seq_peers():
    dp = lax.axis_index("dp")
    seq = lax.axis_index("seq")
    return [(dp, lax.rem(seq + step, SEQN)) for step in range(1, SEQN)]


def everyone(at):
    far_y = moved(at, "y", 3 - 2 * lax.rem(at["y"], 2))
    ring = [device(there) for there in (moved(at, "z", 1), moved(at, "z", 2), moved(at, "z", 3), far_y, moved(at, "y", 2))]
    return seq_peers() + ring + [device(moved(at, "c", 1))]


def spread(k):
    return k + lax.div(k, 2) * (1 - 2 * lax.rem(k, 2))


Z_RIGHT, Z_LEFT, Z_FAR, Y_FAR, X_RIGHT, X_LEFT, X_FAR_RIGHT, X_FAR_LEFT, PAIR, STRIP, PEER, SLOTS = (
    0, 4, 8, 12, 16, 20, 24, 28, 32, 40, 48, 52
)


def whole(dims, axis, index):
    return tuple(index if d == axis else slice(None) for d in dims)


def cut(dims, axis, index, half):
    return tuple(index if d == axis else slice(None) for d in dims) + (half,)


def layer_kernel(
    len_ref, flag_ref, x_ref, w_hbm, cot_ref, o_ref, ig_ref, wg_ref,
    w_all, acc, x_other, xt, kv_ref, s_buf, kt_buf, vt_buf, qt, ct, qr, cr, total, dkv_ref, dproj, dkv_in,
    *rest,
):
    count = len(PARTS)
    data = [rest[3 * part : 3 * part + 3] for part in range(count)]
    bufs = [rest[3 * (count + part) : 3 * (count + part) + 3] for part in range(count)]
    load_sem, send_sem, recv_sem, pair_send, pair_recv, kv_send, kv_recv, ring_send, ring_recv = rest[6 * count :]
    dp = lax.axis_index("dp")
    seq = lax.axis_index("seq")
    at = place()
    z, x, c = at["z"], at["x"], at["c"]
    half_y = lax.rem(lax.div(dp, 2), 2)
    partner = device(moved(at, "c", 1))
    far_y = device(moved(at, "y", 3 - 2 * lax.rem(at["y"], 2)))
    z_right, z_left = device(moved(at, "z", 1)), device(moved(at, "z", 3))
    x_right, x_left = device(moved(at, "x", 1)), device(moved(at, "x", 3))

    def shard(step, other_y=0, other_c=0):
        zz = lax.rem(z + step, 4)
        yy = lax.rem(half_y + other_y, 2)
        return zz * 4 + yy * 2 + lax.rem(c + other_c, 2)

    def quarter(i):
        return lax.rem(x + i, 4)

    def copy(slot, ref, there):
        return pltpu.make_async_remote_copy(
            src_ref=ref, dst_ref=ref, send_sem=send_sem.at[slot], recv_sem=recv_sem.at[slot],
            device_id=there, device_id_type=MESH,
        )

    def to_z_right(i):
        return copy(Z_RIGHT + i, w_all.at[dp, quarter(i)], z_right)

    def to_z_left(i):
        return copy(Z_LEFT + i, w_all.at[dp, quarter(i)], z_left)

    def to_z_far(i):
        if i < 2:
            return copy(Z_FAR + i, w_all.at[shard(3), quarter(i)], z_right)
        return copy(Z_FAR + i, w_all.at[shard(1), quarter(i)], z_left)

    def to_far_y(k):
        return copy(Y_FAR + k, w_all.at[shard(spread(k)), x], far_y)

    def to_x_right(k):
        return copy(X_RIGHT + k, w_all.at[shard(spread(k), 1), x], x_right)

    def to_x_left(k):
        return copy(X_LEFT + k, w_all.at[shard(spread(k), 1), x], x_left)

    def to_x_far_right(k):
        return copy(X_FAR_RIGHT + k, w_all.at[shard(spread(k), 1), quarter(3), 0], x_right)

    def to_x_far_left(k):
        return copy(X_FAR_LEFT + k, w_all.at[shard(spread(k), 1), quarter(1), 1], x_left)

    def to_pair(k, other_y):
        return copy(PAIR + 4 * other_y + k, w_all.at[shard(spread(k), other_y)], partner)

    def strip(j):
        return pltpu.make_async_remote_copy(
            src_ref=x_ref.at[:, pl.ds(pl.multiple_of(j * 512 + (1 - c) * 256, 256), 256)],
            dst_ref=x_other.at[j],
            send_sem=send_sem.at[STRIP + j], recv_sem=recv_sem.at[STRIP + j],
            device_id=partner, device_id_type=MESH,
        )

    def project(s):
        lanes = pl.ds(pl.multiple_of(s * 256, 256), 256)
        acc[...] += jnp.dot(
            x_ref[:, lanes], w_all[s].reshape(256, COLS), preferred_element_type=F32
        )

    own = pltpu.make_async_copy(w_hbm, w_all.at[dp], load_sem)
    own.start()
    barrier_with(everyone(at))
    own.wait()
    sent = []

    def send(item):
        item.start()
        sent.append(item)

    for i in range(2):
        send(to_z_right(i))
        send(to_z_left(i))
        if i == 0:
            send(to_far_y(0))
    send(to_pair(0, 0))
    for j in range(8):
        send(strip(j))
    acc[...] = jnp.zeros_like(acc)

    def turn_own(j, carry):
        rows = pl.ds(pl.multiple_of(j * 256, 256), 256)
        lanes = pl.ds(pl.multiple_of(j * 512 + c * 256, 256), 256)
        xt[rows, :256] = x_ref[:, lanes].T
        return carry

    lax.fori_loop(0, 8, turn_own, 0)
    to_z_right(0).wait_recv()
    send(to_z_far(0))
    to_z_left(0).wait_recv()
    send(to_far_y(1))
    send(to_far_y(2))
    for i in (2, 3):
        send(to_z_right(i))
        send(to_z_left(i))

    def to_x(k):
        to_far_y(k).wait_recv()
        send(to_x_right(k))
        send(to_x_left(k))

    def pass_x(k):
        to_x_right(k).wait_recv()
        send(to_x_far_right(k))
        to_x_left(k).wait_recv()
        send(to_x_far_left(k))

    def far_done(k):
        to_x_far_right(k).wait_recv()
        to_x_far_left(k).wait_recv()
        send(to_pair(k, 1))

    def near_own(k, carry):
        project(shard(spread(k)))
        return carry

    def near_pair(k, carry):
        to_pair(k, 0).wait_recv()
        project(shard(spread(k), 0, 1))
        return carry

    def far_own(k, carry):
        project(shard(spread(k), 1))
        return carry

    def far_pair(k, carry):
        to_pair(k, 1).wait_recv()
        project(shard(spread(k), 1, 1))
        return carry

    def turn_other(j, carry):
        rows = pl.ds(pl.multiple_of(j * 256, 256), 256)
        strip(j).wait_recv()
        xt[rows, 256:] = x_other[j].T
        return carry

    to_x(0)
    lax.fori_loop(0, 8, turn_other, 0)
    to_z_right(1).wait_recv()
    send(to_z_far(1))
    to_x(1)
    pass_x(0)
    to_z_far(0).wait_recv()
    send(to_far_y(3))
    for i in (1, 2):
        to_z_left(i).wait_recv()
    send(to_z_far(2))
    to_x(2)
    to_z_left(3).wait_recv()
    send(to_z_far(3))
    send(to_pair(1, 0))
    pass_x(1)
    to_x(3)
    for i in (2, 3):
        to_z_right(i).wait_recv()
    send(to_pair(2, 0))
    far_done(0)
    lax.fori_loop(0, 2, near_own, 0)
    pass_x(2)
    lax.fori_loop(0, 2, near_pair, 0)
    for i in (1, 2, 3):
        to_z_far(i).wait_recv()
    send(to_pair(3, 0))
    far_done(1)
    lax.fori_loop(2, 4, near_own, 0)
    pass_x(3)
    far_done(2)
    lax.fori_loop(2, 4, near_pair, 0)
    lax.fori_loop(0, 3, far_own, 0)
    far_done(3)
    lax.fori_loop(0, 3, far_pair, 0)
    lax.fori_loop(3, 4, far_own, 0)
    lax.fori_loop(3, 4, far_pair, 0)

    kv_ref[WIN - 1] = acc[:, QW:].astype(BF16)

    def to_peer(step):
        return pltpu.make_async_remote_copy(
            src_ref=kv_ref.at[WIN - 1],
            dst_ref=kv_ref.at[WIN - 1 - step],
            send_sem=send_sem.at[PEER + step - 1],
            recv_sem=recv_sem.at[PEER + step - 1],
            device_id=(dp, lax.rem(seq + step, SEQN)),
            device_id_type=MESH,
        )

    for step in range(1, WIN):
        @pl.when(seq + step < SEQN)
        def _(step=step):
            to_peer(step).start()

    row0 = seq * BLK
    lane_pos = row0 + lax.broadcasted_iota(jnp.int32, (1, BLK), 1)
    sub_pos = row0 + lax.broadcasted_iota(jnp.int32, (BLK, HEAD), 0)
    doc_start = jnp.int32(0)
    starts = jnp.zeros((1, BLK), jnp.int32)
    keep = jnp.zeros((BLK, HEAD), jnp.int32)
    for doc in range(NDOC):
        doc_end = doc_start + len_ref[0, doc]
        starts = jnp.where((lane_pos >= doc_start) & (lane_pos < doc_end), doc_start, starts)
        keep = jnp.where((sub_pos >= doc_start) & (sub_pos < doc_end), flag_ref[0, doc], keep)
        doc_start = doc_end
    base = seq - (WIN - 1)
    low = jnp.maximum(WIN - 1 - seq, 0)

    for head in range(HEADS):
        lanes, rows = slice(head * HEAD, (head + 1) * HEAD), slice(head * BLK, (head + 1) * BLK)
        q = acc[:, lanes].astype(BF16)
        cot = jnp.where(keep > 0, cot_ref[:, lanes], jnp.zeros((), BF16))
        qr[rows, :] = q
        cr[rows, :] = cot
        qt[:, rows] = q.T
        ct[:, rows] = cot.T

    def score(back, top):
        j = WIN - 1 - back

        @pl.when(back > 0)
        def _():
            to_peer(back).wait_recv()

        key_pos = (base + j) * BLK + lax.broadcasted_iota(jnp.int32, (BLK, BLK), 0)
        allowed = (key_pos >= starts) & (key_pos <= lane_pos)
        mask = jnp.where(allowed, 0.0, -1e30)
        kt_buf[j] = kv_ref[j, :, :HEAD].T
        vt_buf[j] = kv_ref[j, :, HEAD:].T
        s = jnp.dot(kv_ref[j, :, :HEAD], qt[...], preferred_element_type=F32)
        s = s * (SCALE * LOG2E) + jnp.concatenate([mask] * HEADS, axis=1)
        s_buf[j] = s
        return jnp.maximum(top, jnp.max(s, axis=0, keepdims=True))

    top = lax.fori_loop(0, WIN - low, score, jnp.full((1, HEADS * BLK), -1e30, F32))
    total[...] = jnp.zeros_like(total)

    def weigh(j, mass):
        p = jnp.exp2(s_buf[j] - top)
        s_buf[j] = p
        total[...] += jnp.dot(vt_buf[j], p.astype(BF16), preferred_element_type=F32)
        return mass + jnp.sum(p, axis=0, keepdims=True)

    mass = lax.fori_loop(low, WIN, weigh, jnp.zeros((1, HEADS * BLK), F32))
    inverse = 1.0 / mass
    out = (total[...] * inverse).astype(BF16)
    for head in range(HEADS):
        o_ref[:, head * HEAD : (head + 1) * HEAD] = out[:, head * BLK : (head + 1) * BLK].T
    delta = jnp.sum(ct[...].astype(F32) * out.astype(F32), axis=0, keepdims=True)
    total[...] = jnp.zeros_like(total)

    def kv_copy(step):
        return pltpu.make_async_remote_copy(
            src_ref=dkv_ref.at[WIN - 1 - step],
            dst_ref=dkv_in.at[step - 1],
            send_sem=kv_send.at[step - 1],
            recv_sem=kv_recv.at[step - 1],
            device_id=(dp, lax.rem(seq + SEQN - step, SEQN)),
            device_id_type=MESH,
        )

    def back(j, carry):
        p = s_buf[j] * inverse
        dp = jnp.dot(kv_ref[j, :, HEAD:], ct[...], preferred_element_type=F32)
        ds = (p * (dp - delta)).astype(BF16)
        total[...] += jnp.dot(kt_buf[j], ds, preferred_element_type=F32)
        dk = jnp.dot(ds, qr[...], preferred_element_type=F32) * SCALE
        dkv_ref[j, :, :HEAD] = dk.astype(BF16)
        dkv_ref[j, :, HEAD:] = jnp.dot(p.astype(BF16), cr[...], preferred_element_type=F32).astype(BF16)

        @pl.when(j < WIN - 1)
        def _():
            kv_copy(WIN - 1 - j).start()

        return carry

    lax.fori_loop(low, WIN, back, 0)
    def pair_copy(index, src, columns):
        return pltpu.make_async_remote_copy(
            src_ref=src,
            dst_ref=dproj.at[pl.ds(BLK, BLK), columns],
            send_sem=pair_send.at[index],
            recv_sem=pair_recv.at[index],
            device_id=partner,
            device_id_type=MESH,
        )

    pair_q = []
    for head in range(HEADS):
        dq = (total[:, head * BLK : (head + 1) * BLK] * SCALE).astype(BF16)
        dproj[pl.ds(0, BLK), head * HEAD : (head + 1) * HEAD] = dq.T
        if head % 4 == 3:
            columns = pl.ds((head - 3) * HEAD, 4 * HEAD)
            pair_q.append(pair_copy(head // 4, dproj.at[pl.ds(0, BLK), columns], columns))
            pair_q[-1].start()

    def ring_copy(color, stage, buf, src, there):
        k = (color * 3 + stage) * 6 + buf
        return pltpu.make_async_remote_copy(
            src_ref=src,
            dst_ref=bufs[color][stage].at[buf],
            send_sem=ring_send.at[k],
            recv_sem=ring_recv.at[k],
            device_id=device(there),
            device_id_type=MESH,
        )

    def stage_of(color, stage):
        order = PARTS[color][2]
        dims = [d for d in "zyx" if d in order[stage:]]
        axis = order[stage]
        me = at[axis]
        return (
            dims, axis, me,
            lax.rem(me + 1, 4), lax.rem(me + 2, 4), lax.rem(me + 3, 4),
            moved(at, axis, 1), moved(at, axis, 3),
        )

    started = []

    def open_stage(color, stage):
        dims, axis, me, right, across, left, to_right, to_left = stage_of(color, stage)
        src = data[color][stage]
        if stage == 0:
            pieces = (
                (0, cut(dims, axis, across, 0), to_right),
                (1, cut(dims, axis, across, 1), to_left),
                (3, cut(dims, axis, right, 1), to_right),
                (4, cut(dims, axis, left, 0), to_left),
            )
        else:
            pieces = (
                (2, whole(dims, axis, across), moved(at, axis, 2)),
                (0, whole(dims, axis, right), to_right),
                (1, whole(dims, axis, left), to_left),
            )
        for buf, where, there in pieces:
            copy = ring_copy(color, stage, buf, src.at[where], there)
            copy.start()
            started.append(copy)

    def pass_on(color):
        dims, axis, me, right, across, left, to_right, to_left = stage_of(color, 0)
        src = data[color][0]
        for first, buf, index, half, there in ((0, 2, right, 0, to_right), (1, 5, left, 1, to_left)):
            where = cut(dims, axis, index, half)
            ring_copy(color, 0, first, src.at[where], there).wait_recv()
            src[where] = (src[where].astype(F32) + bufs[color][0][first].astype(F32)).astype(BF16)
            copy = ring_copy(color, 0, buf, src.at[where], there)
            copy.start()
            started.append(copy)

    def close_stage(color, stage):
        dims, axis, me, right, across, left, to_right, to_left = stage_of(color, stage)
        src, got = data[color][stage], bufs[color][stage]
        if stage == 0:
            for half in (0, 1):
                where = cut(dims, axis, me, half)
                summed = src[where].astype(F32)
                for buf in (2 + half, 4 + half):
                    ring_copy(color, 0, buf, src.at[where], to_right).wait_recv()
                    summed = summed + got[buf].astype(F32)
                data[color][1][(slice(None),) * (len(dims) - 1) + (half,)] = summed.astype(BF16)
            return
        where = whole(dims, axis, me)
        summed = src[where].astype(F32)
        for buf in range(3):
            ring_copy(color, stage, buf, src.at[where], to_right).wait_recv()
            summed = summed + got[buf].astype(F32)
        if stage == 1:
            data[color][2][...] = summed.astype(BF16)
        else:
            first, width, _ = PARTS[color]
            wg_ref[:, first : first + width] = summed.reshape(32, width)

    def multiply(color):
        first, width, _ = PARTS[color]

        def body(z, carry):
            rows = pl.ds(pl.multiple_of(z * 512, 512), 512)
            part = jnp.dot(xt[rows, :], dproj[:, first : first + width], preferred_element_type=F32)
            data[color][0][z] = part.astype(BF16).reshape(4, 4, 2, 16, width)
            return carry

        lax.fori_loop(0, 4, body, 0)

    for color in (0, 1, 2, 3, 4):
        if color in (0, 2):
            pair_q[color // 2].wait_recv()
        multiply(color)
        open_stage(color, 0)

    pairs = dkv_ref[WIN - 1].astype(F32)
    for step in range(1, WIN):
        @pl.when(seq + step < SEQN)
        def _(step=step):
            kv_copy(step).wait_recv()

        @pl.when(seq + step >= SEQN)
        def _(step=step):
            dkv_in[step - 1] = jnp.zeros((BLK, 2 * HEAD), BF16)

        pairs = pairs + dkv_in[step - 1].astype(F32)
    dproj[pl.ds(0, BLK), QW:] = pairs.astype(BF16)
    pair_kv = pair_copy(2, dproj.at[pl.ds(0, BLK), pl.ds(QW, 2 * HEAD)], pl.ds(QW, 2 * HEAD))
    pair_kv.start()
    pair_kv.wait_recv()
    for color in (5, 6):
        multiply(color)
        open_stage(color, 0)
    for color in (0, 1, 2):
        pass_on(color)

    def grad_chunk(n, carry):
        rows = pl.ds(pl.multiple_of(n * 512, 512), 512)
        ig_ref[:, rows] = lax.dot_general(
            dproj[pl.ds(0, BLK), :], w_all[pl.ds(2 * n, 2)].reshape(512, COLS), NT, preferred_element_type=F32
        ).astype(BF16)
        return carry

    lax.fori_loop(0, 8, grad_chunk, 0)

    for step in STEPS:
        color, stage = int(step[1]), int(step[2])
        if step[0] == "r":
            pass_on(color)
        else:
            close_stage(color, stage)
            if stage < 2:
                open_stage(color, stage + 1)
    for item in started:
        item.wait_send()
    for item in pair_q:
        item.wait_send()
    pair_kv.wait_send()
    for step in range(1, WIN):
        @pl.when(seq >= step)
        def _(step=step):
            kv_copy(step).wait_send()
    for item in sent:
        item.wait_send()

    for step in range(1, WIN):
        @pl.when(seq + step < SEQN)
        def _(step=step):
            to_peer(step).wait_send()


VM = pl.BlockSpec(memory_space=pltpu.VMEM)
SM = pl.BlockSpec(memory_space=pltpu.SMEM)
ANY = pl.BlockSpec(memory_space=pl.ANY)
DMA = pltpu.SemaphoreType.DMA
LIMIT = 60 * 1024 * 1024


def shape(dims, kind=BF16):
    return jax.ShapeDtypeStruct(dims, kind)


def shards(inputs, weights, cotangent, doc_lengths, kept_flags):
    held, received = [], []
    for _, width, order in PARTS:
        for stage in range(3):
            dims = (4,) * (3 - stage)
            held.append(pltpu.VMEM(dims + (2, 16, width), BF16))
            received.append(pltpu.VMEM(((6,) + dims[1:] if stage == 0 else (3,) + dims[1:] + (2,)) + (16, width), BF16))
    rows = HEADS * BLK
    attention, inputs_grad, weights_grad = pl.pallas_call(
        layer_kernel,
        out_shape=(pltpu.VMEM((BLK, QW), BF16), pltpu.VMEM((BLK, D), BF16), pltpu.VMEM((32, COLS), F32)),
        in_specs=[SM, SM, VM, ANY, VM],
        out_specs=(VM, VM, VM),
        scratch_shapes=[
            pltpu.VMEM((16, 4, 2, 32, COLS), BF16),
            pltpu.VMEM((BLK, COLS), F32),
            pltpu.VMEM((8, BLK, 256), BF16),
            pltpu.VMEM((2048, 2 * BLK), BF16),
            pltpu.VMEM((WIN, BLK, 2 * HEAD), BF16),
            pltpu.VMEM((WIN, BLK, rows), F32),
            pltpu.VMEM((WIN, HEAD, BLK), BF16),
            pltpu.VMEM((WIN, HEAD, BLK), BF16),
            pltpu.VMEM((HEAD, rows), BF16),
            pltpu.VMEM((HEAD, rows), BF16),
            pltpu.VMEM((rows, HEAD), BF16),
            pltpu.VMEM((rows, HEAD), BF16),
            pltpu.VMEM((HEAD, rows), F32),
            pltpu.VMEM((WIN, BLK, 2 * HEAD), BF16),
            pltpu.VMEM((2 * BLK, COLS), BF16),
            pltpu.VMEM((WIN - 1, BLK, 2 * HEAD), BF16),
        ]
        + held
        + received
        + [DMA, DMA((SLOTS,)), DMA((SLOTS,)), DMA((3,)), DMA((3,)), DMA((WIN - 1,)), DMA((WIN - 1,)), DMA((18 * len(PARTS),)), DMA((18 * len(PARTS),))],
        compiler_params=pltpu.CompilerParams(collective_id=0, has_side_effects=True, vmem_limit_bytes=LIMIT),
        name="layer",
    )(doc_lengths, kept_flags, inputs[0], weights.reshape(4, 2, 32, COLS), cotangent[0])
    return (attention[None], inputs_grad[None], weights_grad)


def solution(mesh):
    in_specs = (
        P("dp", "seq", None),
        P("dp", None),
        P("dp", "seq", None),
        P("dp", None),
        P("dp", None),
    )
    out_specs = (P("dp", "seq", None), P("dp", "seq", None), P(("dp", "seq"), None))
    return jax.shard_map(shards, mesh=mesh, in_specs=in_specs, out_specs=out_specs, check_vma=False)
```

```python
import math

import jax
import jax.numpy as jnp
from jax import lax
from jax.experimental import pallas as pl
from jax.experimental.pallas import tpu as pltpu
from jax.sharding import PartitionSpec as P

MESH = pl.DeviceIdType.MESH
HEAD = 128
HEADS = 8
BLK = 256
WIN = 5
D = 4096
QW = 1024
COLS = 1280
NDOC = 8
SEQN = 8
SCALE = 1.0 / math.sqrt(HEAD)
LOG2E = math.log2(math.e)
F32 = jnp.float32
BF16 = jnp.bfloat16
NT = (((1,), (1,)), ((), ()))
PARTS = (
    (0, 256, "xyz"), (256, 256, "yzx"), (512, 256, "zxy"), (768, 128, "xyz"), (896, 128, "yzx"), (1024, 128, "zxy"), (1152, 128, "xyz"),
)
STEPS = (
    "r30 r40 e00 e10 e20 r50 r60 e30 e40 e01 e11 e21 e50 e60 e31 e41 e02 e12 e22 e51 e61 e32 e42 e52 e62"
).split()


def place():
    dp = lax.axis_index("dp")
    seq = lax.axis_index("seq")
    z = lax.div(dp, 4)
    y = lax.rem(lax.div(dp, 2), 2) * 2 + lax.div(seq, 4)
    return {"z": z, "y": y, "x": lax.rem(seq, 4), "c": lax.rem(dp, 2)}


def device(at):
    dp = at["z"] * 4 + lax.div(at["y"], 2) * 2 + at["c"]
    return (dp, lax.rem(at["y"], 2) * 4 + at["x"])


def moved(at, axis, step):
    count = 2 if axis == "c" else 4
    there = dict(at)
    there[axis] = lax.rem(at[axis] + step, count)
    return there


def barrier_with(devices):
    sem = pltpu.get_barrier_semaphore()
    for there in devices:
        pl.semaphore_signal(sem, inc=1, device_id=there, device_id_type=MESH)
    pl.semaphore_wait(sem, len(devices))


def seq_peers():
    dp = lax.axis_index("dp")
    seq = lax.axis_index("seq")
    return [(dp, lax.rem(seq + step, SEQN)) for step in range(1, SEQN)]


def everyone(at):
    far_y = moved(at, "y", 3 - 2 * lax.rem(at["y"], 2))
    ring = [device(there) for there in (moved(at, "z", 1), moved(at, "z", 2), moved(at, "z", 3), far_y, moved(at, "y", 2))]
    return seq_peers() + ring + [device(moved(at, "c", 1))]


def spread(k):
    return k + lax.div(k, 2) * (1 - 2 * lax.rem(k, 2))


Z_RIGHT, Z_LEFT, Z_FAR, Y_FAR, X_RIGHT, X_LEFT, X_FAR_RIGHT, X_FAR_LEFT, PAIR, STRIP, PEER, SLOTS = (
    0, 4, 8, 12, 16, 20, 24, 28, 32, 40, 48, 52
)


def whole(dims, axis, index):
    return tuple(index if d == axis else slice(None) for d in dims)


def cut(dims, axis, index, half):
    return tuple(index if d == axis else slice(None) for d in dims) + (half,)


def layer_kernel(
    len_ref, flag_ref, x_hbm, w_hbm, cot_hbm, o_ref, ig_ref, wg_ref,
    x_ref, cot_ref, w_all, acc, x_other, xt, kv_ref, s_buf, kt_buf, vt_buf, qt, ct, qr, cr, total, dkv_ref, dproj, dkv_in,
    *rest,
):
    count = len(PARTS)
    data = [rest[3 * part : 3 * part + 3] for part in range(count)]
    bufs = [rest[3 * (count + part) : 3 * (count + part) + 3] for part in range(count)]
    load_sem, send_sem, recv_sem, pair_send, pair_recv, kv_send, kv_recv, ring_send, ring_recv = rest[6 * count :]
    dp = lax.axis_index("dp")
    seq = lax.axis_index("seq")
    at = place()
    z, x, c = at["z"], at["x"], at["c"]
    half_y = lax.rem(lax.div(dp, 2), 2)
    partner = device(moved(at, "c", 1))
    far_y = device(moved(at, "y", 3 - 2 * lax.rem(at["y"], 2)))
    z_right, z_left = device(moved(at, "z", 1)), device(moved(at, "z", 3))
    x_right, x_left = device(moved(at, "x", 1)), device(moved(at, "x", 3))

    def shard(step, other_y=0, other_c=0):
        zz = lax.rem(z + step, 4)
        yy = lax.rem(half_y + other_y, 2)
        return zz * 4 + yy * 2 + lax.rem(c + other_c, 2)

    def quarter(i):
        return lax.rem(x + i, 4)

    def copy(slot, ref, there):
        return pltpu.make_async_remote_copy(
            src_ref=ref, dst_ref=ref, send_sem=send_sem.at[slot], recv_sem=recv_sem.at[slot],
            device_id=there, device_id_type=MESH,
        )

    def to_z_right(i):
        return copy(Z_RIGHT + i, w_all.at[dp, quarter(i)], z_right)

    def to_z_left(i):
        return copy(Z_LEFT + i, w_all.at[dp, quarter(i)], z_left)

    def to_z_far(i):
        if i < 2:
            return copy(Z_FAR + i, w_all.at[shard(3), quarter(i)], z_right)
        return copy(Z_FAR + i, w_all.at[shard(1), quarter(i)], z_left)

    def to_far_y(k):
        return copy(Y_FAR + k, w_all.at[shard(spread(k)), x], far_y)

    def to_x_right(k):
        return copy(X_RIGHT + k, w_all.at[shard(spread(k), 1), x], x_right)

    def to_x_left(k):
        return copy(X_LEFT + k, w_all.at[shard(spread(k), 1), x], x_left)

    def to_x_far_right(k):
        return copy(X_FAR_RIGHT + k, w_all.at[shard(spread(k), 1), quarter(3), 0], x_right)

    def to_x_far_left(k):
        return copy(X_FAR_LEFT + k, w_all.at[shard(spread(k), 1), quarter(1), 1], x_left)

    def to_pair(k, other_y):
        return copy(PAIR + 4 * other_y + k, w_all.at[shard(spread(k), other_y)], partner)

    def strip(j):
        return pltpu.make_async_remote_copy(
            src_ref=x_ref.at[:, pl.ds(pl.multiple_of(j * 512 + (1 - c) * 256, 256), 256)],
            dst_ref=x_other.at[j],
            send_sem=send_sem.at[STRIP + j], recv_sem=recv_sem.at[STRIP + j],
            device_id=partner, device_id_type=MESH,
        )

    def project(s):
        lanes = pl.ds(pl.multiple_of(s * 256, 256), 256)
        acc[...] += jnp.dot(
            x_ref[:, lanes], w_all[s].reshape(256, COLS), preferred_element_type=F32
        )

    own = pltpu.make_async_copy(w_hbm, w_all.at[dp], load_sem.at[0])
    own.start()
    load_x = pltpu.make_async_copy(x_hbm, x_ref, load_sem.at[1])
    load_x.start()
    load_cot = pltpu.make_async_copy(cot_hbm, cot_ref, load_sem.at[2])
    load_cot.start()
    barrier_with(everyone(at))
    own.wait()
    sent = []

    def send(item):
        item.start()
        sent.append(item)

    for i in range(2):
        send(to_z_right(i))
        send(to_z_left(i))
        if i == 0:
            send(to_far_y(0))
    send(to_pair(0, 0))
    load_x.wait()
    for j in range(8):
        send(strip(j))
    acc[...] = jnp.zeros_like(acc)

    def turn_own(j, carry):
        rows = pl.ds(pl.multiple_of(j * 256, 256), 256)
        lanes = pl.ds(pl.multiple_of(j * 512 + c * 256, 256), 256)
        xt[rows, :256] = x_ref[:, lanes].T
        return carry

    lax.fori_loop(0, 8, turn_own, 0)
    to_z_right(0).wait_recv()
    send(to_z_far(0))
    to_z_left(0).wait_recv()
    send(to_far_y(1))
    send(to_far_y(2))
    for i in (2, 3):
        send(to_z_right(i))
        send(to_z_left(i))

    def to_x(k):
        to_far_y(k).wait_recv()
        send(to_x_right(k))
        send(to_x_left(k))

    def pass_x(k):
        to_x_right(k).wait_recv()
        send(to_x_far_right(k))
        to_x_left(k).wait_recv()
        send(to_x_far_left(k))

    def far_done(k):
        to_x_far_right(k).wait_recv()
        to_x_far_left(k).wait_recv()
        send(to_pair(k, 1))

    def near_own(k, carry):
        project(shard(spread(k)))
        return carry

    def near_pair(k, carry):
        to_pair(k, 0).wait_recv()
        project(shard(spread(k), 0, 1))
        return carry

    def far_own(k, carry):
        project(shard(spread(k), 1))
        return carry

    def far_pair(k, carry):
        to_pair(k, 1).wait_recv()
        project(shard(spread(k), 1, 1))
        return carry

    def turn_other(j, carry):
        rows = pl.ds(pl.multiple_of(j * 256, 256), 256)
        strip(j).wait_recv()
        xt[rows, 256:] = x_other[j].T
        return carry

    to_x(0)
    lax.fori_loop(0, 8, turn_other, 0)
    to_z_right(1).wait_recv()
    send(to_z_far(1))
    to_x(1)
    pass_x(0)
    to_z_far(0).wait_recv()
    send(to_far_y(3))
    for i in (1, 2):
        to_z_left(i).wait_recv()
    send(to_z_far(2))
    to_x(2)
    to_z_left(3).wait_recv()
    send(to_z_far(3))
    send(to_pair(1, 0))
    pass_x(1)
    to_x(3)
    for i in (2, 3):
        to_z_right(i).wait_recv()
    send(to_pair(2, 0))
    far_done(0)
    lax.fori_loop(0, 2, near_own, 0)
    pass_x(2)
    lax.fori_loop(0, 2, near_pair, 0)
    for i in (1, 2, 3):
        to_z_far(i).wait_recv()
    send(to_pair(3, 0))
    far_done(1)
    lax.fori_loop(2, 4, near_own, 0)
    pass_x(3)
    far_done(2)
    lax.fori_loop(2, 4, near_pair, 0)
    lax.fori_loop(0, 3, far_own, 0)
    far_done(3)
    lax.fori_loop(0, 3, far_pair, 0)
    lax.fori_loop(3, 4, far_own, 0)
    lax.fori_loop(3, 4, far_pair, 0)

    kv_ref[WIN - 1] = acc[:, QW:].astype(BF16)

    def to_peer(step):
        return pltpu.make_async_remote_copy(
            src_ref=kv_ref.at[WIN - 1],
            dst_ref=kv_ref.at[WIN - 1 - step],
            send_sem=send_sem.at[PEER + step - 1],
            recv_sem=recv_sem.at[PEER + step - 1],
            device_id=(dp, lax.rem(seq + step, SEQN)),
            device_id_type=MESH,
        )

    for step in range(1, WIN):
        @pl.when(seq + step < SEQN)
        def _(step=step):
            to_peer(step).start()

    row0 = seq * BLK
    lane_pos = row0 + lax.broadcasted_iota(jnp.int32, (1, BLK), 1)
    sub_pos = row0 + lax.broadcasted_iota(jnp.int32, (BLK, HEAD), 0)
    doc_start = jnp.int32(0)
    starts = jnp.zeros((1, BLK), jnp.int32)
    keep = jnp.zeros((BLK, HEAD), jnp.int32)
    for doc in range(NDOC):
        doc_end = doc_start + len_ref[0, doc]
        starts = jnp.where((lane_pos >= doc_start) & (lane_pos < doc_end), doc_start, starts)
        keep = jnp.where((sub_pos >= doc_start) & (sub_pos < doc_end), flag_ref[0, doc], keep)
        doc_start = doc_end
    base = seq - (WIN - 1)
    low = jnp.maximum(WIN - 1 - seq, 0)

    load_cot.wait()
    for head in range(HEADS):
        lanes, rows = slice(head * HEAD, (head + 1) * HEAD), slice(head * BLK, (head + 1) * BLK)
        q = acc[:, lanes].astype(BF16)
        cot = jnp.where(keep > 0, cot_ref[:, lanes], jnp.zeros((), BF16))
        qr[rows, :] = q
        cr[rows, :] = cot
        qt[:, rows] = q.T
        ct[:, rows] = cot.T

    def score(back, top):
        j = WIN - 1 - back

        @pl.when(back > 0)
        def _():
            to_peer(back).wait_recv()

        key_pos = (base + j) * BLK + lax.broadcasted_iota(jnp.int32, (BLK, BLK), 0)
        allowed = (key_pos >= starts) & (key_pos <= lane_pos)
        mask = jnp.where(allowed, 0.0, -1e30)
        kt_buf[j] = kv_ref[j, :, :HEAD].T
        vt_buf[j] = kv_ref[j, :, HEAD:].T
        s = jnp.dot(kv_ref[j, :, :HEAD], qt[...], preferred_element_type=F32)
        s = s * (SCALE * LOG2E) + jnp.concatenate([mask] * HEADS, axis=1)
        s_buf[j] = s
        return jnp.maximum(top, jnp.max(s, axis=0, keepdims=True))

    top = lax.fori_loop(0, WIN - low, score, jnp.full((1, HEADS * BLK), -1e30, F32))
    total[...] = jnp.zeros_like(total)

    def weigh(j, mass):
        p = jnp.exp2(s_buf[j] - top)
        s_buf[j] = p
        total[...] += jnp.dot(vt_buf[j], p.astype(BF16), preferred_element_type=F32)
        return mass + jnp.sum(p, axis=0, keepdims=True)

    mass = lax.fori_loop(low, WIN, weigh, jnp.zeros((1, HEADS * BLK), F32))
    inverse = 1.0 / mass
    out = (total[...] * inverse).astype(BF16)
    for head in range(HEADS):
        o_ref[:, head * HEAD : (head + 1) * HEAD] = out[:, head * BLK : (head + 1) * BLK].T
    delta = jnp.sum(ct[...].astype(F32) * out.astype(F32), axis=0, keepdims=True)
    total[...] = jnp.zeros_like(total)

    def kv_copy(step):
        return pltpu.make_async_remote_copy(
            src_ref=dkv_ref.at[WIN - 1 - step],
            dst_ref=dkv_in.at[step - 1],
            send_sem=kv_send.at[step - 1],
            recv_sem=kv_recv.at[step - 1],
            device_id=(dp, lax.rem(seq + SEQN - step, SEQN)),
            device_id_type=MESH,
        )

    def back(j, carry):
        p = s_buf[j] * inverse
        dp = jnp.dot(kv_ref[j, :, HEAD:], ct[...], preferred_element_type=F32)
        ds = (p * (dp - delta)).astype(BF16)
        total[...] += jnp.dot(kt_buf[j], ds, preferred_element_type=F32)
        dk = jnp.dot(ds, qr[...], preferred_element_type=F32) * SCALE
        dkv_ref[j, :, :HEAD] = dk.astype(BF16)
        dkv_ref[j, :, HEAD:] = jnp.dot(p.astype(BF16), cr[...], preferred_element_type=F32).astype(BF16)

        @pl.when(j < WIN - 1)
        def _():
            kv_copy(WIN - 1 - j).start()

        return carry

    lax.fori_loop(low, WIN, back, 0)
    def pair_copy(index, src, columns):
        return pltpu.make_async_remote_copy(
            src_ref=src,
            dst_ref=dproj.at[pl.ds(BLK, BLK), columns],
            send_sem=pair_send.at[index],
            recv_sem=pair_recv.at[index],
            device_id=partner,
            device_id_type=MESH,
        )

    pair_q = []
    for head in range(HEADS):
        dq = (total[:, head * BLK : (head + 1) * BLK] * SCALE).astype(BF16)
        dproj[pl.ds(0, BLK), head * HEAD : (head + 1) * HEAD] = dq.T
        if head % 4 == 3:
            columns = pl.ds((head - 3) * HEAD, 4 * HEAD)
            pair_q.append(pair_copy(head // 4, dproj.at[pl.ds(0, BLK), columns], columns))
            pair_q[-1].start()

    def ring_copy(color, stage, buf, src, there):
        k = (color * 3 + stage) * 6 + buf
        return pltpu.make_async_remote_copy(
            src_ref=src,
            dst_ref=bufs[color][stage].at[buf],
            send_sem=ring_send.at[k],
            recv_sem=ring_recv.at[k],
            device_id=device(there),
            device_id_type=MESH,
        )

    def stage_of(color, stage):
        order = PARTS[color][2]
        dims = [d for d in "zyx" if d in order[stage:]]
        axis = order[stage]
        me = at[axis]
        return (
            dims, axis, me,
            lax.rem(me + 1, 4), lax.rem(me + 2, 4), lax.rem(me + 3, 4),
            moved(at, axis, 1), moved(at, axis, 3),
        )

    started = []

    def open_stage(color, stage):
        dims, axis, me, right, across, left, to_right, to_left = stage_of(color, stage)
        src = data[color][stage]
        if stage == 0:
            pieces = (
                (0, cut(dims, axis, across, 0), to_right),
                (1, cut(dims, axis, across, 1), to_left),
                (3, cut(dims, axis, right, 1), to_right),
                (4, cut(dims, axis, left, 0), to_left),
            )
        else:
            pieces = (
                (2, whole(dims, axis, across), moved(at, axis, 2)),
                (0, whole(dims, axis, right), to_right),
                (1, whole(dims, axis, left), to_left),
            )
        for buf, where, there in pieces:
            copy = ring_copy(color, stage, buf, src.at[where], there)
            copy.start()
            started.append(copy)

    def pass_on(color):
        dims, axis, me, right, across, left, to_right, to_left = stage_of(color, 0)
        src = data[color][0]
        for first, buf, index, half, there in ((0, 2, right, 0, to_right), (1, 5, left, 1, to_left)):
            where = cut(dims, axis, index, half)
            ring_copy(color, 0, first, src.at[where], there).wait_recv()
            src[where] = (src[where].astype(F32) + bufs[color][0][first].astype(F32)).astype(BF16)
            copy = ring_copy(color, 0, buf, src.at[where], there)
            copy.start()
            started.append(copy)

    def close_stage(color, stage):
        dims, axis, me, right, across, left, to_right, to_left = stage_of(color, stage)
        src, got = data[color][stage], bufs[color][stage]
        if stage == 0:
            for half in (0, 1):
                where = cut(dims, axis, me, half)
                summed = src[where].astype(F32)
                for buf in (2 + half, 4 + half):
                    ring_copy(color, 0, buf, src.at[where], to_right).wait_recv()
                    summed = summed + got[buf].astype(F32)
                data[color][1][(slice(None),) * (len(dims) - 1) + (half,)] = summed.astype(BF16)
            return
        where = whole(dims, axis, me)
        summed = src[where].astype(F32)
        for buf in range(3):
            ring_copy(color, stage, buf, src.at[where], to_right).wait_recv()
            summed = summed + got[buf].astype(F32)
        if stage == 1:
            data[color][2][...] = summed.astype(BF16)
        else:
            first, width, _ = PARTS[color]
            wg_ref[:, first : first + width] = summed.reshape(32, width)

    def multiply(color):
        first, width, _ = PARTS[color]

        def body(z, carry):
            rows = pl.ds(pl.multiple_of(z * 512, 512), 512)
            part = jnp.dot(xt[rows, :], dproj[:, first : first + width], preferred_element_type=F32)
            data[color][0][z] = part.astype(BF16).reshape(4, 4, 2, 16, width)
            return carry

        lax.fori_loop(0, 4, body, 0)

    for color in (0, 1, 2, 3, 4):
        if color in (0, 2):
            pair_q[color // 2].wait_recv()
        multiply(color)
        open_stage(color, 0)

    pairs = dkv_ref[WIN - 1].astype(F32)
    for step in range(1, WIN):
        @pl.when(seq + step < SEQN)
        def _(step=step):
            kv_copy(step).wait_recv()

        @pl.when(seq + step >= SEQN)
        def _(step=step):
            dkv_in[step - 1] = jnp.zeros((BLK, 2 * HEAD), BF16)

        pairs = pairs + dkv_in[step - 1].astype(F32)
    dproj[pl.ds(0, BLK), QW:] = pairs.astype(BF16)
    pair_kv = pair_copy(2, dproj.at[pl.ds(0, BLK), pl.ds(QW, 2 * HEAD)], pl.ds(QW, 2 * HEAD))
    pair_kv.start()
    pair_kv.wait_recv()
    for color in (5, 6):
        multiply(color)
        open_stage(color, 0)
    for color in (0, 1, 2):
        pass_on(color)

    def grad_chunk(n, carry):
        rows = pl.ds(pl.multiple_of(n * 512, 512), 512)
        ig_ref[:, rows] = lax.dot_general(
            dproj[pl.ds(0, BLK), :], w_all[pl.ds(2 * n, 2)].reshape(512, COLS), NT, preferred_element_type=F32
        ).astype(BF16)
        return carry

    lax.fori_loop(0, 8, grad_chunk, 0)

    for step in STEPS:
        color, stage = int(step[1]), int(step[2])
        if step[0] == "r":
            pass_on(color)
        else:
            close_stage(color, stage)
            if stage < 2:
                open_stage(color, stage + 1)
    for item in started:
        item.wait_send()
    for item in pair_q:
        item.wait_send()
    pair_kv.wait_send()
    for step in range(1, WIN):
        @pl.when(seq >= step)
        def _(step=step):
            kv_copy(step).wait_send()
    for item in sent:
        item.wait_send()

    for step in range(1, WIN):
        @pl.when(seq + step < SEQN)
        def _(step=step):
            to_peer(step).wait_send()


VM = pl.BlockSpec(memory_space=pltpu.VMEM)
SM = pl.BlockSpec(memory_space=pltpu.SMEM)
ANY = pl.BlockSpec(memory_space=pl.ANY)
DMA = pltpu.SemaphoreType.DMA
LIMIT = 60 * 1024 * 1024


def shape(dims, kind=BF16):
    return jax.ShapeDtypeStruct(dims, kind)


def shards(inputs, weights, cotangent, doc_lengths, kept_flags):
    held, received = [], []
    for _, width, order in PARTS:
        for stage in range(3):
            dims = (4,) * (3 - stage)
            held.append(pltpu.VMEM(dims + (2, 16, width), BF16))
            received.append(pltpu.VMEM(((6,) + dims[1:] if stage == 0 else (3,) + dims[1:] + (2,)) + (16, width), BF16))
    rows = HEADS * BLK
    attention, inputs_grad, weights_grad = pl.pallas_call(
        layer_kernel,
        out_shape=(pltpu.VMEM((BLK, QW), BF16), pltpu.VMEM((BLK, D), BF16), pltpu.VMEM((32, COLS), F32)),
        in_specs=[SM, SM, ANY, ANY, ANY],
        out_specs=(VM, VM, VM),
        scratch_shapes=[
            pltpu.VMEM((BLK, D), BF16),
            pltpu.VMEM((BLK, QW), BF16),
            pltpu.VMEM((16, 4, 2, 32, COLS), BF16),
            pltpu.VMEM((BLK, COLS), F32),
            pltpu.VMEM((8, BLK, 256), BF16),
            pltpu.VMEM((2048, 2 * BLK), BF16),
            pltpu.VMEM((WIN, BLK, 2 * HEAD), BF16),
            pltpu.VMEM((WIN, BLK, rows), F32),
            pltpu.VMEM((WIN, HEAD, BLK), BF16),
            pltpu.VMEM((WIN, HEAD, BLK), BF16),
            pltpu.VMEM((HEAD, rows), BF16),
            pltpu.VMEM((HEAD, rows), BF16),
            pltpu.VMEM((rows, HEAD), BF16),
            pltpu.VMEM((rows, HEAD), BF16),
            pltpu.VMEM((HEAD, rows), F32),
            pltpu.VMEM((WIN, BLK, 2 * HEAD), BF16),
            pltpu.VMEM((2 * BLK, COLS), BF16),
            pltpu.VMEM((WIN - 1, BLK, 2 * HEAD), BF16),
        ]
        + held
        + received
        + [DMA((3,)), DMA((SLOTS,)), DMA((SLOTS,)), DMA((3,)), DMA((3,)), DMA((WIN - 1,)), DMA((WIN - 1,)), DMA((18 * len(PARTS),)), DMA((18 * len(PARTS),))],
        compiler_params=pltpu.CompilerParams(collective_id=0, has_side_effects=True, vmem_limit_bytes=LIMIT),
        name="layer",
    )(doc_lengths, kept_flags, inputs[0], weights.reshape(4, 2, 32, COLS), cotangent[0])
    return (attention[None], inputs_grad[None], weights_grad)


def solution(mesh):
    in_specs = (
        P("dp", "seq", None),
        P("dp", None),
        P("dp", "seq", None),
        P("dp", None),
        P("dp", None),
    )
    out_specs = (P("dp", "seq", None), P("dp", "seq", None), P(("dp", "seq"), None))
    return jax.shard_map(shards, mesh=mesh, in_specs=in_specs, out_specs=out_specs, check_vma=False)
```

```python
import math

import jax
import jax.numpy as jnp
from jax import lax
from jax.experimental import pallas as pl
from jax.experimental.pallas import tpu as pltpu
from jax.sharding import PartitionSpec as P

MESH = pl.DeviceIdType.MESH
HEAD = 128
HEADS = 8
BLK = 256
WIN = 5
D = 4096
QW = 1024
COLS = 1280
NDOC = 8
SEQN = 8
SCALE = 1.0 / math.sqrt(HEAD)
LOG2E = math.log2(math.e)
F32 = jnp.float32
BF16 = jnp.bfloat16
NT = (((1,), (1,)), ((), ()))
PARTS = (
    (0, 256, "xyz"), (256, 256, "yzx"), (512, 256, "zxy"), (768, 128, "xyz"), (896, 128, "xyz"), (1024, 128, "zxy"), (1152, 128, "yzx"),
)
STEPS = (
    "r30 r40 e00 e10 e20 r50 r60 e30 e40 e01 e11 e21 e50 e60 e31 e41 e02 e12 e22 e51 e61 e32 e42 e52 e62"
).split()


def place():
    dp = lax.axis_index("dp")
    seq = lax.axis_index("seq")
    z = lax.div(dp, 4)
    y = lax.rem(lax.div(dp, 2), 2) * 2 + lax.div(seq, 4)
    return {"z": z, "y": y, "x": lax.rem(seq, 4), "c": lax.rem(dp, 2)}


def device(at):
    dp = at["z"] * 4 + lax.div(at["y"], 2) * 2 + at["c"]
    return (dp, lax.rem(at["y"], 2) * 4 + at["x"])


def moved(at, axis, step):
    count = 2 if axis == "c" else 4
    there = dict(at)
    there[axis] = lax.rem(at[axis] + step, count)
    return there


def barrier_with(devices):
    sem = pltpu.get_barrier_semaphore()
    for there in devices:
        pl.semaphore_signal(sem, inc=1, device_id=there, device_id_type=MESH)
    pl.semaphore_wait(sem, len(devices))


def seq_peers():
    dp = lax.axis_index("dp")
    seq = lax.axis_index("seq")
    return [(dp, lax.rem(seq + step, SEQN)) for step in range(1, SEQN)]


def everyone(at):
    far_y = moved(at, "y", 3 - 2 * lax.rem(at["y"], 2))
    ring = [device(there) for there in (moved(at, "z", 1), moved(at, "z", 2), moved(at, "z", 3), far_y, moved(at, "y", 2))]
    return seq_peers() + ring + [device(moved(at, "c", 1))]


def spread(k):
    return k + lax.div(k, 2) * (1 - 2 * lax.rem(k, 2))


Z_RIGHT, Z_LEFT, Z_FAR, Y_FAR, X_RIGHT, X_LEFT, X_FAR_RIGHT, X_FAR_LEFT, PAIR, STRIP, PEER, SLOTS = (
    0, 4, 8, 12, 16, 20, 24, 28, 32, 40, 48, 52
)


def whole(dims, axis, index):
    return tuple(index if d == axis else slice(None) for d in dims)


def cut(dims, axis, index, half):
    return tuple(index if d == axis else slice(None) for d in dims) + (half,)


def layer_kernel(
    len_ref, flag_ref, x_hbm, w_hbm, cot_hbm, o_ref, ig_ref, wg_ref,
    x_ref, cot_ref, w_all, acc, x_other, xt, kv_ref, s_buf, kt_buf, vt_buf, qt, ct, qr, cr, total, dkv_ref, dproj, dkv_in,
    *rest,
):
    count = len(PARTS)
    data = [rest[3 * part : 3 * part + 3] for part in range(count)]
    bufs = [rest[3 * (count + part) : 3 * (count + part) + 3] for part in range(count)]
    load_sem, send_sem, recv_sem, pair_send, pair_recv, kv_send, kv_recv, ring_send, ring_recv = rest[6 * count :]
    dp = lax.axis_index("dp")
    seq = lax.axis_index("seq")
    at = place()
    z, x, c = at["z"], at["x"], at["c"]
    half_y = lax.rem(lax.div(dp, 2), 2)
    partner = device(moved(at, "c", 1))
    far_y = device(moved(at, "y", 3 - 2 * lax.rem(at["y"], 2)))
    z_right, z_left = device(moved(at, "z", 1)), device(moved(at, "z", 3))
    x_right, x_left = device(moved(at, "x", 1)), device(moved(at, "x", 3))

    def shard(step, other_y=0, other_c=0):
        zz = lax.rem(z + step, 4)
        yy = lax.rem(half_y + other_y, 2)
        return zz * 4 + yy * 2 + lax.rem(c + other_c, 2)

    def quarter(i):
        return lax.rem(x + i, 4)

    def copy(slot, ref, there):
        return pltpu.make_async_remote_copy(
            src_ref=ref, dst_ref=ref, send_sem=send_sem.at[slot], recv_sem=recv_sem.at[slot],
            device_id=there, device_id_type=MESH,
        )

    def to_z_right(i):
        return copy(Z_RIGHT + i, w_all.at[dp, quarter(i)], z_right)

    def to_z_left(i):
        return copy(Z_LEFT + i, w_all.at[dp, quarter(i)], z_left)

    def to_z_far(i):
        if i < 2:
            return copy(Z_FAR + i, w_all.at[shard(3), quarter(i)], z_right)
        return copy(Z_FAR + i, w_all.at[shard(1), quarter(i)], z_left)

    def to_far_y(k):
        return copy(Y_FAR + k, w_all.at[shard(spread(k)), x], far_y)

    def to_x_right(k):
        return copy(X_RIGHT + k, w_all.at[shard(spread(k), 1), x], x_right)

    def to_x_left(k):
        return copy(X_LEFT + k, w_all.at[shard(spread(k), 1), x], x_left)

    def to_x_far_right(k):
        return copy(X_FAR_RIGHT + k, w_all.at[shard(spread(k), 1), quarter(3), 0], x_right)

    def to_x_far_left(k):
        return copy(X_FAR_LEFT + k, w_all.at[shard(spread(k), 1), quarter(1), 1], x_left)

    def to_pair(k, other_y):
        return copy(PAIR + 4 * other_y + k, w_all.at[shard(spread(k), other_y)], partner)

    def strip(j):
        return pltpu.make_async_remote_copy(
            src_ref=x_ref.at[:, pl.ds(pl.multiple_of(j * 512 + (1 - c) * 256, 256), 256)],
            dst_ref=x_other.at[j],
            send_sem=send_sem.at[STRIP + j], recv_sem=recv_sem.at[STRIP + j],
            device_id=partner, device_id_type=MESH,
        )

    def project(s):
        lanes = pl.ds(pl.multiple_of(s * 256, 256), 256)
        acc[...] += jnp.dot(
            x_ref[:, lanes], w_all[s].reshape(256, COLS), preferred_element_type=F32
        )

    own = pltpu.make_async_copy(w_hbm, w_all.at[dp], load_sem.at[0])
    own.start()
    load_x = pltpu.make_async_copy(x_hbm, x_ref, load_sem.at[1])
    load_x.start()
    load_cot = pltpu.make_async_copy(cot_hbm, cot_ref, load_sem.at[2])
    load_cot.start()
    barrier_with(everyone(at))
    own.wait()
    sent = []

    def send(item):
        item.start()
        sent.append(item)

    for i in range(2):
        send(to_z_right(i))
        send(to_z_left(i))
        if i == 0:
            send(to_far_y(0))
    send(to_pair(0, 0))
    load_x.wait()
    for j in range(8):
        send(strip(j))
    acc[...] = jnp.zeros_like(acc)

    def turn_own(j, carry):
        rows = pl.ds(pl.multiple_of(j * 256, 256), 256)
        lanes = pl.ds(pl.multiple_of(j * 512 + c * 256, 256), 256)
        xt[rows, :256] = x_ref[:, lanes].T
        return carry

    lax.fori_loop(0, 8, turn_own, 0)
    to_z_right(0).wait_recv()
    send(to_z_far(0))
    to_z_left(0).wait_recv()
    send(to_far_y(1))
    send(to_far_y(2))
    for i in (2, 3):
        send(to_z_right(i))
        send(to_z_left(i))

    def to_x(k):
        to_far_y(k).wait_recv()
        send(to_x_right(k))
        send(to_x_left(k))

    def pass_x(k):
        to_x_right(k).wait_recv()
        send(to_x_far_right(k))
        to_x_left(k).wait_recv()
        send(to_x_far_left(k))

    def far_done(k):
        to_x_far_right(k).wait_recv()
        to_x_far_left(k).wait_recv()
        send(to_pair(k, 1))

    def near_own(k, carry):
        project(shard(spread(k)))
        return carry

    def near_pair(k, carry):
        to_pair(k, 0).wait_recv()
        project(shard(spread(k), 0, 1))
        return carry

    def far_own(k, carry):
        project(shard(spread(k), 1))
        return carry

    def far_pair(k, carry):
        to_pair(k, 1).wait_recv()
        project(shard(spread(k), 1, 1))
        return carry

    def turn_other(j, carry):
        rows = pl.ds(pl.multiple_of(j * 256, 256), 256)
        strip(j).wait_recv()
        xt[rows, 256:] = x_other[j].T
        return carry

    to_x(0)
    lax.fori_loop(0, 8, turn_other, 0)
    to_z_right(1).wait_recv()
    send(to_z_far(1))
    to_x(1)
    pass_x(0)
    to_z_far(0).wait_recv()
    send(to_far_y(3))
    for i in (1, 2):
        to_z_left(i).wait_recv()
    send(to_z_far(2))
    to_x(2)
    to_z_left(3).wait_recv()
    send(to_z_far(3))
    send(to_pair(1, 0))
    pass_x(1)
    to_x(3)
    for i in (2, 3):
        to_z_right(i).wait_recv()
    send(to_pair(2, 0))
    far_done(0)
    lax.fori_loop(0, 2, near_own, 0)
    pass_x(2)
    lax.fori_loop(0, 2, near_pair, 0)
    for i in (1, 2, 3):
        to_z_far(i).wait_recv()
    send(to_pair(3, 0))
    far_done(1)
    lax.fori_loop(2, 4, near_own, 0)
    pass_x(3)
    far_done(2)
    lax.fori_loop(2, 4, near_pair, 0)
    lax.fori_loop(0, 3, far_own, 0)
    far_done(3)
    lax.fori_loop(0, 3, far_pair, 0)
    lax.fori_loop(3, 4, far_own, 0)
    lax.fori_loop(3, 4, far_pair, 0)

    kv_ref[WIN - 1] = acc[:, QW:].astype(BF16)

    def to_peer(step):
        return pltpu.make_async_remote_copy(
            src_ref=kv_ref.at[WIN - 1],
            dst_ref=kv_ref.at[WIN - 1 - step],
            send_sem=send_sem.at[PEER + step - 1],
            recv_sem=recv_sem.at[PEER + step - 1],
            device_id=(dp, lax.rem(seq + step, SEQN)),
            device_id_type=MESH,
        )

    for step in range(1, WIN):
        @pl.when(seq + step < SEQN)
        def _(step=step):
            to_peer(step).start()

    row0 = seq * BLK
    lane_pos = row0 + lax.broadcasted_iota(jnp.int32, (1, BLK), 1)
    sub_pos = row0 + lax.broadcasted_iota(jnp.int32, (BLK, HEAD), 0)
    doc_start = jnp.int32(0)
    starts = jnp.zeros((1, BLK), jnp.int32)
    keep = jnp.zeros((BLK, HEAD), jnp.int32)
    for doc in range(NDOC):
        doc_end = doc_start + len_ref[0, doc]
        starts = jnp.where((lane_pos >= doc_start) & (lane_pos < doc_end), doc_start, starts)
        keep = jnp.where((sub_pos >= doc_start) & (sub_pos < doc_end), flag_ref[0, doc], keep)
        doc_start = doc_end
    base = seq - (WIN - 1)
    low = jnp.maximum(WIN - 1 - seq, 0)

    load_cot.wait()
    for head in range(HEADS):
        lanes, rows = slice(head * HEAD, (head + 1) * HEAD), slice(head * BLK, (head + 1) * BLK)
        q = acc[:, lanes].astype(BF16)
        cot = jnp.where(keep > 0, cot_ref[:, lanes], jnp.zeros((), BF16))
        qr[rows, :] = q
        cr[rows, :] = cot
        qt[:, rows] = q.T
        ct[:, rows] = cot.T

    def score(back, top):
        j = WIN - 1 - back

        @pl.when(back > 0)
        def _():
            to_peer(back).wait_recv()

        key_pos = (base + j) * BLK + lax.broadcasted_iota(jnp.int32, (BLK, BLK), 0)
        allowed = (key_pos >= starts) & (key_pos <= lane_pos)
        mask = jnp.where(allowed, 0.0, -1e30)
        kt_buf[j] = kv_ref[j, :, :HEAD].T
        vt_buf[j] = kv_ref[j, :, HEAD:].T
        s = jnp.dot(kv_ref[j, :, :HEAD], qt[...], preferred_element_type=F32)
        s = s * (SCALE * LOG2E) + jnp.concatenate([mask] * HEADS, axis=1)
        s_buf[j] = s
        return jnp.maximum(top, jnp.max(s, axis=0, keepdims=True))

    top = lax.fori_loop(0, WIN - low, score, jnp.full((1, HEADS * BLK), -1e30, F32))
    total[...] = jnp.zeros_like(total)

    def weigh(j, mass):
        p = jnp.exp2(s_buf[j] - top)
        s_buf[j] = p
        total[...] += jnp.dot(vt_buf[j], p.astype(BF16), preferred_element_type=F32)
        return mass + jnp.sum(p, axis=0, keepdims=True)

    mass = lax.fori_loop(low, WIN, weigh, jnp.zeros((1, HEADS * BLK), F32))
    inverse = 1.0 / mass
    out = (total[...] * inverse).astype(BF16)
    for head in range(HEADS):
        o_ref[:, head * HEAD : (head + 1) * HEAD] = out[:, head * BLK : (head + 1) * BLK].T
    delta = jnp.sum(ct[...].astype(F32) * out.astype(F32), axis=0, keepdims=True)
    total[...] = jnp.zeros_like(total)

    def kv_copy(step):
        return pltpu.make_async_remote_copy(
            src_ref=dkv_ref.at[WIN - 1 - step],
            dst_ref=dkv_in.at[step - 1],
            send_sem=kv_send.at[step - 1],
            recv_sem=kv_recv.at[step - 1],
            device_id=(dp, lax.rem(seq + SEQN - step, SEQN)),
            device_id_type=MESH,
        )

    def back(j, carry):
        p = s_buf[j] * inverse
        dp = jnp.dot(kv_ref[j, :, HEAD:], ct[...], preferred_element_type=F32)
        ds = (p * (dp - delta)).astype(BF16)
        total[...] += jnp.dot(kt_buf[j], ds, preferred_element_type=F32)
        dk = jnp.dot(ds, qr[...], preferred_element_type=F32) * SCALE
        dkv_ref[j, :, :HEAD] = dk.astype(BF16)
        dkv_ref[j, :, HEAD:] = jnp.dot(p.astype(BF16), cr[...], preferred_element_type=F32).astype(BF16)

        @pl.when(j < WIN - 1)
        def _():
            kv_copy(WIN - 1 - j).start()

        return carry

    lax.fori_loop(low, WIN, back, 0)
    def pair_copy(index, src, columns):
        return pltpu.make_async_remote_copy(
            src_ref=src,
            dst_ref=dproj.at[pl.ds(BLK, BLK), columns],
            send_sem=pair_send.at[index],
            recv_sem=pair_recv.at[index],
            device_id=partner,
            device_id_type=MESH,
        )

    pair_q = []
    for head in range(HEADS):
        dq = (total[:, head * BLK : (head + 1) * BLK] * SCALE).astype(BF16)
        dproj[pl.ds(0, BLK), head * HEAD : (head + 1) * HEAD] = dq.T
        if head % 4 == 3:
            columns = pl.ds((head - 3) * HEAD, 4 * HEAD)
            pair_q.append(pair_copy(head // 4, dproj.at[pl.ds(0, BLK), columns], columns))
            pair_q[-1].start()

    def ring_copy(color, stage, buf, src, there):
        k = (color * 3 + stage) * 6 + buf
        return pltpu.make_async_remote_copy(
            src_ref=src,
            dst_ref=bufs[color][stage].at[buf],
            send_sem=ring_send.at[k],
            recv_sem=ring_recv.at[k],
            device_id=device(there),
            device_id_type=MESH,
        )

    def stage_of(color, stage):
        order = PARTS[color][2]
        dims = [d for d in "zyx" if d in order[stage:]]
        axis = order[stage]
        me = at[axis]
        return (
            dims, axis, me,
            lax.rem(me + 1, 4), lax.rem(me + 2, 4), lax.rem(me + 3, 4),
            moved(at, axis, 1), moved(at, axis, 3),
        )

    started = []

    def open_stage(color, stage):
        dims, axis, me, right, across, left, to_right, to_left = stage_of(color, stage)
        src = data[color][stage]
        if stage == 0:
            pieces = (
                (0, cut(dims, axis, across, 0), to_right),
                (1, cut(dims, axis, across, 1), to_left),
                (3, cut(dims, axis, right, 1), to_right),
                (4, cut(dims, axis, left, 0), to_left),
            )
        else:
            pieces = (
                (2, whole(dims, axis, across), moved(at, axis, 2)),
                (0, whole(dims, axis, right), to_right),
                (1, whole(dims, axis, left), to_left),
            )
        for buf, where, there in pieces:
            copy = ring_copy(color, stage, buf, src.at[where], there)
            copy.start()
            started.append(copy)

    def pass_on(color):
        dims, axis, me, right, across, left, to_right, to_left = stage_of(color, 0)
        src = data[color][0]
        for first, buf, index, half, there in ((0, 2, right, 0, to_right), (1, 5, left, 1, to_left)):
            where = cut(dims, axis, index, half)
            ring_copy(color, 0, first, src.at[where], there).wait_recv()
            src[where] = (src[where].astype(F32) + bufs[color][0][first].astype(F32)).astype(BF16)
            copy = ring_copy(color, 0, buf, src.at[where], there)
            copy.start()
            started.append(copy)

    def close_stage(color, stage):
        dims, axis, me, right, across, left, to_right, to_left = stage_of(color, stage)
        src, got = data[color][stage], bufs[color][stage]
        if stage == 0:
            for half in (0, 1):
                where = cut(dims, axis, me, half)
                summed = src[where].astype(F32)
                for buf in (2 + half, 4 + half):
                    ring_copy(color, 0, buf, src.at[where], to_right).wait_recv()
                    summed = summed + got[buf].astype(F32)
                data[color][1][(slice(None),) * (len(dims) - 1) + (half,)] = summed.astype(BF16)
            return
        where = whole(dims, axis, me)
        summed = src[where].astype(F32)
        for buf in range(3):
            ring_copy(color, stage, buf, src.at[where], to_right).wait_recv()
            summed = summed + got[buf].astype(F32)
        if stage == 1:
            data[color][2][...] = summed.astype(BF16)
        else:
            first, width, _ = PARTS[color]
            wg_ref[:, first : first + width] = summed.reshape(32, width)

    def multiply(color):
        first, width, _ = PARTS[color]

        def body(z, carry):
            rows = pl.ds(pl.multiple_of(z * 512, 512), 512)
            part = jnp.dot(xt[rows, :], dproj[:, first : first + width], preferred_element_type=F32)
            data[color][0][z] = part.astype(BF16).reshape(4, 4, 2, 16, width)
            return carry

        lax.fori_loop(0, 4, body, 0)

    for color in (0, 1, 2, 3, 4):
        if color in (0, 2):
            pair_q[color // 2].wait_recv()
        multiply(color)
        open_stage(color, 0)

    pairs = dkv_ref[WIN - 1].astype(F32)
    for step in range(1, WIN):
        @pl.when(seq + step < SEQN)
        def _(step=step):
            kv_copy(step).wait_recv()

        @pl.when(seq + step >= SEQN)
        def _(step=step):
            dkv_in[step - 1] = jnp.zeros((BLK, 2 * HEAD), BF16)

        pairs = pairs + dkv_in[step - 1].astype(F32)
    dproj[pl.ds(0, BLK), QW:] = pairs.astype(BF16)
    pair_kv = pair_copy(2, dproj.at[pl.ds(0, BLK), pl.ds(QW, 2 * HEAD)], pl.ds(QW, 2 * HEAD))
    pair_kv.start()
    pair_kv.wait_recv()
    for color in (5, 6):
        multiply(color)
        open_stage(color, 0)
    for color in (0, 1, 2):
        pass_on(color)

    def grad_chunk(n, carry):
        rows = pl.ds(pl.multiple_of(n * 512, 512), 512)
        ig_ref[:, rows] = lax.dot_general(
            dproj[pl.ds(0, BLK), :], w_all[pl.ds(2 * n, 2)].reshape(512, COLS), NT, preferred_element_type=F32
        ).astype(BF16)
        return carry

    lax.fori_loop(0, 8, grad_chunk, 0)

    for step in STEPS:
        color, stage = int(step[1]), int(step[2])
        if step[0] == "r":
            pass_on(color)
        else:
            close_stage(color, stage)
            if stage < 2:
                open_stage(color, stage + 1)
    for item in started:
        item.wait_send()
    for item in pair_q:
        item.wait_send()
    pair_kv.wait_send()
    for step in range(1, WIN):
        @pl.when(seq >= step)
        def _(step=step):
            kv_copy(step).wait_send()
    for item in sent:
        item.wait_send()

    for step in range(1, WIN):
        @pl.when(seq + step < SEQN)
        def _(step=step):
            to_peer(step).wait_send()


VM = pl.BlockSpec(memory_space=pltpu.VMEM)
SM = pl.BlockSpec(memory_space=pltpu.SMEM)
ANY = pl.BlockSpec(memory_space=pl.ANY)
DMA = pltpu.SemaphoreType.DMA
LIMIT = 60 * 1024 * 1024


def shape(dims, kind=BF16):
    return jax.ShapeDtypeStruct(dims, kind)


def shards(inputs, weights, cotangent, doc_lengths, kept_flags):
    held, received = [], []
    for _, width, order in PARTS:
        for stage in range(3):
            dims = (4,) * (3 - stage)
            held.append(pltpu.VMEM(dims + (2, 16, width), BF16))
            received.append(pltpu.VMEM(((6,) + dims[1:] if stage == 0 else (3,) + dims[1:] + (2,)) + (16, width), BF16))
    rows = HEADS * BLK
    attention, inputs_grad, weights_grad = pl.pallas_call(
        layer_kernel,
        out_shape=(pltpu.VMEM((BLK, QW), BF16), pltpu.VMEM((BLK, D), BF16), pltpu.VMEM((32, COLS), F32)),
        in_specs=[SM, SM, ANY, ANY, ANY],
        out_specs=(VM, VM, VM),
        scratch_shapes=[
            pltpu.VMEM((BLK, D), BF16),
            pltpu.VMEM((BLK, QW), BF16),
            pltpu.VMEM((16, 4, 2, 32, COLS), BF16),
            pltpu.VMEM((BLK, COLS), F32),
            pltpu.VMEM((8, BLK, 256), BF16),
            pltpu.VMEM((2048, 2 * BLK), BF16),
            pltpu.VMEM((WIN, BLK, 2 * HEAD), BF16),
            pltpu.VMEM((WIN, BLK, rows), F32),
            pltpu.VMEM((WIN, HEAD, BLK), BF16),
            pltpu.VMEM((WIN, HEAD, BLK), BF16),
            pltpu.VMEM((HEAD, rows), BF16),
            pltpu.VMEM((HEAD, rows), BF16),
            pltpu.VMEM((rows, HEAD), BF16),
            pltpu.VMEM((rows, HEAD), BF16),
            pltpu.VMEM((HEAD, rows), F32),
            pltpu.VMEM((WIN, BLK, 2 * HEAD), BF16),
            pltpu.VMEM((2 * BLK, COLS), BF16),
            pltpu.VMEM((WIN - 1, BLK, 2 * HEAD), BF16),
        ]
        + held
        + received
        + [DMA((3,)), DMA((SLOTS,)), DMA((SLOTS,)), DMA((3,)), DMA((3,)), DMA((WIN - 1,)), DMA((WIN - 1,)), DMA((18 * len(PARTS),)), DMA((18 * len(PARTS),))],
        compiler_params=pltpu.CompilerParams(collective_id=0, has_side_effects=True, vmem_limit_bytes=LIMIT),
        name="layer",
    )(doc_lengths, kept_flags, inputs[0], weights.reshape(4, 2, 32, COLS), cotangent[0])
    return (attention[None], inputs_grad[None], weights_grad)


def solution(mesh):
    in_specs = (
        P("dp", "seq", None),
        P("dp", None),
        P("dp", "seq", None),
        P("dp", None),
        P("dp", None),
    )
    out_specs = (P("dp", "seq", None), P("dp", "seq", None), P(("dp", "seq"), None))
    return jax.shard_map(shards, mesh=mesh, in_specs=in_specs, out_specs=out_specs, check_vma=False)
```

```python
import math

import jax
import jax.numpy as jnp
from jax import lax
from jax.experimental import pallas as pl
from jax.experimental.pallas import tpu as pltpu
from jax.sharding import PartitionSpec as P

MESH = pl.DeviceIdType.MESH
HEAD = 128
HEADS = 8
BLK = 256
WIN = 5
D = 4096
QW = 1024
COLS = 1280
NDOC = 8
SEQN = 8
SCALE = 1.0 / math.sqrt(HEAD)
LOG2E = math.log2(math.e)
F32 = jnp.float32
BF16 = jnp.bfloat16
NT = (((1,), (1,)), ((), ()))
PARTS = (
    (0, 256, "xyz"), (256, 256, "yzx"), (512, 256, "zxy"), (768, 128, "xyz"), (896, 128, "yzx"), (1024, 128, "zxy"), (1152, 128, "xyz"),
)
STEPS = (
    "r30 r40 e00 e10 e20 r50 r60 e30 e40 e01 e11 e21 e50 e60 e31 e41 e02 e12 e22 e51 e61 e32 e42 e52 e62"
).split()


def place():
    dp = lax.axis_index("dp")
    seq = lax.axis_index("seq")
    z = lax.div(dp, 4)
    y = lax.rem(lax.div(dp, 2), 2) * 2 + lax.div(seq, 4)
    return {"z": z, "y": y, "x": lax.rem(seq, 4), "c": lax.rem(dp, 2)}


def device(at):
    dp = at["z"] * 4 + lax.div(at["y"], 2) * 2 + at["c"]
    return (dp, lax.rem(at["y"], 2) * 4 + at["x"])


def moved(at, axis, step):
    count = 2 if axis == "c" else 4
    there = dict(at)
    there[axis] = lax.rem(at[axis] + step, count)
    return there


def barrier_with(devices):
    sem = pltpu.get_barrier_semaphore()
    for there in devices:
        pl.semaphore_signal(sem, inc=1, device_id=there, device_id_type=MESH)
    pl.semaphore_wait(sem, len(devices))


def seq_peers():
    dp = lax.axis_index("dp")
    seq = lax.axis_index("seq")
    return [(dp, lax.rem(seq + step, SEQN)) for step in range(1, SEQN)]


def everyone(at):
    far_y = moved(at, "y", 3 - 2 * lax.rem(at["y"], 2))
    ring = [device(there) for there in (moved(at, "z", 1), moved(at, "z", 2), moved(at, "z", 3), far_y, moved(at, "y", 2))]
    return seq_peers() + ring + [device(moved(at, "c", 1))]


def spread(k):
    return k + lax.div(k, 2) * (1 - 2 * lax.rem(k, 2))


Z_RIGHT, Z_LEFT, Z_FAR, Y_FAR, X_RIGHT, X_LEFT, X_FAR_RIGHT, X_FAR_LEFT, PAIR, STRIP, PEER, SLOTS = (
    0, 4, 8, 12, 16, 20, 24, 28, 32, 40, 48, 52
)


def whole(dims, axis, index):
    return tuple(index if d == axis else slice(None) for d in dims)


def cut(dims, axis, index, half):
    return tuple(index if d == axis else slice(None) for d in dims) + (half,)


def layer_kernel(
    len_ref, flag_ref, x_hbm, w_hbm, cot_hbm, o_ref, ig_ref, wg_ref,
    x_ref, cot_ref, w_all, acc, x_other, xt, kv_ref, s_buf, kt_buf, vt_buf, qt, ct, qr, cr, total, dkv_ref, dproj, dkv_in,
    *rest,
):
    count = len(PARTS)
    data = [rest[3 * part : 3 * part + 3] for part in range(count)]
    bufs = [rest[3 * (count + part) : 3 * (count + part) + 3] for part in range(count)]
    load_sem, send_sem, recv_sem, pair_send, pair_recv, kv_send, kv_recv, ring_send, ring_recv = rest[6 * count :]
    dp = lax.axis_index("dp")
    seq = lax.axis_index("seq")
    at = place()
    z, x, c = at["z"], at["x"], at["c"]
    half_y = lax.rem(lax.div(dp, 2), 2)
    partner = device(moved(at, "c", 1))
    far_y = device(moved(at, "y", 3 - 2 * lax.rem(at["y"], 2)))
    z_right, z_left = device(moved(at, "z", 1)), device(moved(at, "z", 3))
    x_right, x_left = device(moved(at, "x", 1)), device(moved(at, "x", 3))

    def shard(step, other_y=0, other_c=0):
        zz = lax.rem(z + step, 4)
        yy = lax.rem(half_y + other_y, 2)
        return zz * 4 + yy * 2 + lax.rem(c + other_c, 2)

    def quarter(i):
        return lax.rem(x + i, 4)

    def copy(slot, ref, there):
        return pltpu.make_async_remote_copy(
            src_ref=ref, dst_ref=ref, send_sem=send_sem.at[slot], recv_sem=recv_sem.at[slot],
            device_id=there, device_id_type=MESH,
        )

    def to_z_right(i):
        return copy(Z_RIGHT + i, w_all.at[dp, quarter(i)], z_right)

    def to_z_left(i):
        return copy(Z_LEFT + i, w_all.at[dp, quarter(i)], z_left)

    def to_z_far(i):
        if i < 2:
            return copy(Z_FAR + i, w_all.at[shard(3), quarter(i)], z_right)
        return copy(Z_FAR + i, w_all.at[shard(1), quarter(i)], z_left)

    def to_far_y(k):
        return copy(Y_FAR + k, w_all.at[shard(spread(k)), x], far_y)

    def to_x_right(k):
        return copy(X_RIGHT + k, w_all.at[shard(spread(k), 1), x], x_right)

    def to_x_left(k):
        return copy(X_LEFT + k, w_all.at[shard(spread(k), 1), x], x_left)

    def to_x_far_right(k):
        return copy(X_FAR_RIGHT + k, w_all.at[shard(spread(k), 1), quarter(3), 0], x_right)

    def to_x_far_left(k):
        return copy(X_FAR_LEFT + k, w_all.at[shard(spread(k), 1), quarter(1), 1], x_left)

    def to_pair(k, other_y):
        return copy(PAIR + 4 * other_y + k, w_all.at[shard(spread(k), other_y)], partner)

    def strip(j):
        return pltpu.make_async_remote_copy(
            src_ref=x_ref.at[:, pl.ds(pl.multiple_of(j * 512 + (1 - c) * 256, 256), 256)],
            dst_ref=x_other.at[j],
            send_sem=send_sem.at[STRIP + j], recv_sem=recv_sem.at[STRIP + j],
            device_id=partner, device_id_type=MESH,
        )

    def project(s):
        lanes = pl.ds(pl.multiple_of(s * 256, 256), 256)
        acc[...] += jnp.dot(
            x_ref[:, lanes], w_all[s].reshape(256, COLS), preferred_element_type=F32
        )

    own = pltpu.make_async_copy(w_hbm, w_all.at[dp], load_sem.at[0])
    own.start()
    load_x = pltpu.make_async_copy(x_hbm, x_ref, load_sem.at[1])
    load_x.start()
    load_cot = pltpu.make_async_copy(cot_hbm, cot_ref, load_sem.at[2])
    load_cot.start()
    barrier_with(everyone(at))
    own.wait()
    sent = []

    def send(item):
        item.start()
        sent.append(item)

    for i in range(2):
        send(to_z_right(i))
        send(to_z_left(i))
        if i == 0:
            send(to_far_y(0))
    send(to_pair(0, 0))
    load_x.wait()
    for j in range(8):
        send(strip(j))
    acc[...] = jnp.zeros_like(acc)

    def turn_own(j, carry):
        rows = pl.ds(pl.multiple_of(j * 256, 256), 256)
        lanes = pl.ds(pl.multiple_of(j * 512 + c * 256, 256), 256)
        xt[rows, :256] = x_ref[:, lanes].T
        return carry

    lax.fori_loop(0, 8, turn_own, 0)
    to_z_right(0).wait_recv()
    send(to_z_far(0))
    to_z_left(0).wait_recv()
    send(to_far_y(1))
    send(to_far_y(2))
    for i in (2, 3):
        send(to_z_right(i))
        send(to_z_left(i))

    def to_x(k):
        to_far_y(k).wait_recv()
        send(to_x_right(k))
        send(to_x_left(k))

    def pass_x(k):
        to_x_right(k).wait_recv()
        send(to_x_far_right(k))
        to_x_left(k).wait_recv()
        send(to_x_far_left(k))

    def far_done(k):
        to_x_far_right(k).wait_recv()
        to_x_far_left(k).wait_recv()
        send(to_pair(k, 1))

    def near_own(k, carry):
        project(shard(spread(k)))
        return carry

    def near_pair(k, carry):
        to_pair(k, 0).wait_recv()
        project(shard(spread(k), 0, 1))
        return carry

    def far_own(k, carry):
        project(shard(spread(k), 1))
        return carry

    def far_pair(k, carry):
        to_pair(k, 1).wait_recv()
        project(shard(spread(k), 1, 1))
        return carry

    def turn_other(j, carry):
        rows = pl.ds(pl.multiple_of(j * 256, 256), 256)
        strip(j).wait_recv()
        xt[rows, 256:] = x_other[j].T
        return carry

    to_x(0)
    lax.fori_loop(0, 8, turn_other, 0)
    to_z_right(1).wait_recv()
    send(to_z_far(1))
    to_x(1)
    pass_x(0)
    to_z_far(0).wait_recv()
    send(to_far_y(3))
    for i in (1, 2):
        to_z_left(i).wait_recv()
    send(to_z_far(2))
    to_x(2)
    to_z_left(3).wait_recv()
    send(to_z_far(3))
    send(to_pair(1, 0))
    pass_x(1)
    to_x(3)
    for i in (2, 3):
        to_z_right(i).wait_recv()
    send(to_pair(2, 0))
    far_done(0)
    lax.fori_loop(0, 2, near_own, 0)
    pass_x(2)
    lax.fori_loop(0, 2, near_pair, 0)
    for i in (1, 2, 3):
        to_z_far(i).wait_recv()
    send(to_pair(3, 0))
    far_done(1)
    lax.fori_loop(2, 4, near_own, 0)
    pass_x(3)
    far_done(2)
    lax.fori_loop(2, 4, near_pair, 0)
    lax.fori_loop(0, 3, far_own, 0)
    far_done(3)
    lax.fori_loop(0, 3, far_pair, 0)
    lax.fori_loop(3, 4, far_own, 0)
    lax.fori_loop(3, 4, far_pair, 0)

    kv_ref[WIN - 1] = acc[:, QW:].astype(BF16)

    def to_peer(step):
        return pltpu.make_async_remote_copy(
            src_ref=kv_ref.at[WIN - 1],
            dst_ref=kv_ref.at[WIN - 1 - step],
            send_sem=send_sem.at[PEER + step - 1],
            recv_sem=recv_sem.at[PEER + step - 1],
            device_id=(dp, lax.rem(seq + step, SEQN)),
            device_id_type=MESH,
        )

    for step in range(1, WIN):
        @pl.when(seq + step < SEQN)
        def _(step=step):
            to_peer(step).start()

    row0 = seq * BLK
    lane_pos = row0 + lax.broadcasted_iota(jnp.int32, (1, BLK), 1)
    sub_pos = row0 + lax.broadcasted_iota(jnp.int32, (BLK, HEAD), 0)
    doc_start = jnp.int32(0)
    starts = jnp.zeros((1, BLK), jnp.int32)
    keep = jnp.zeros((BLK, HEAD), jnp.int32)
    for doc in range(NDOC):
        doc_end = doc_start + len_ref[0, doc]
        starts = jnp.where((lane_pos >= doc_start) & (lane_pos < doc_end), doc_start, starts)
        keep = jnp.where((sub_pos >= doc_start) & (sub_pos < doc_end), flag_ref[0, doc], keep)
        doc_start = doc_end
    base = seq - (WIN - 1)
    low = jnp.maximum(WIN - 1 - seq, 0)

    load_cot.wait()
    for head in range(HEADS):
        lanes, rows = slice(head * HEAD, (head + 1) * HEAD), slice(head * BLK, (head + 1) * BLK)
        q = acc[:, lanes].astype(BF16)
        cot = jnp.where(keep > 0, cot_ref[:, lanes], jnp.zeros((), BF16))
        qr[rows, :] = q
        cr[rows, :] = cot
        qt[:, rows] = q.T
        ct[:, rows] = cot.T

    def score(back, top):
        j = WIN - 1 - back

        @pl.when(back > 0)
        def _():
            to_peer(back).wait_recv()

        key_pos = (base + j) * BLK + lax.broadcasted_iota(jnp.int32, (BLK, BLK), 0)
        allowed = (key_pos >= starts) & (key_pos <= lane_pos)
        mask = jnp.where(allowed, 0.0, -1e30)
        kt_buf[j] = kv_ref[j, :, :HEAD].T
        vt_buf[j] = kv_ref[j, :, HEAD:].T
        s = jnp.dot(kv_ref[j, :, :HEAD], qt[...], preferred_element_type=F32)
        s = s * (SCALE * LOG2E) + jnp.concatenate([mask] * HEADS, axis=1)
        s_buf[j] = s
        return jnp.maximum(top, jnp.max(s, axis=0, keepdims=True))

    top = lax.fori_loop(0, WIN - low, score, jnp.full((1, HEADS * BLK), -1e30, F32))
    total[...] = jnp.zeros_like(total)

    def weigh(j, mass):
        p = jnp.exp2(s_buf[j] - top)
        s_buf[j] = p
        total[...] += jnp.dot(vt_buf[j], p.astype(BF16), preferred_element_type=F32)
        return mass + jnp.sum(p, axis=0, keepdims=True)

    mass = lax.fori_loop(low, WIN, weigh, jnp.zeros((1, HEADS * BLK), F32))
    inverse = 1.0 / mass
    out = (total[...] * inverse).astype(BF16)
    for head in range(HEADS):
        o_ref[:, head * HEAD : (head + 1) * HEAD] = out[:, head * BLK : (head + 1) * BLK].T
    delta = jnp.sum(ct[...].astype(F32) * out.astype(F32), axis=0, keepdims=True)
    total[...] = jnp.zeros_like(total)

    def kv_copy(step):
        return pltpu.make_async_remote_copy(
            src_ref=dkv_ref.at[WIN - 1 - step],
            dst_ref=dkv_in.at[step - 1],
            send_sem=kv_send.at[step - 1],
            recv_sem=kv_recv.at[step - 1],
            device_id=(dp, lax.rem(seq + SEQN - step, SEQN)),
            device_id_type=MESH,
        )

    def back(j, carry):
        p = s_buf[j] * inverse
        dp = jnp.dot(kv_ref[j, :, HEAD:], ct[...], preferred_element_type=F32)
        ds = (p * (dp - delta)).astype(BF16)
        total[...] += jnp.dot(kt_buf[j], ds, preferred_element_type=F32)
        dk = jnp.dot(ds, qr[...], preferred_element_type=F32) * SCALE
        dkv_ref[j, :, :HEAD] = dk.astype(BF16)
        dkv_ref[j, :, HEAD:] = jnp.dot(p.astype(BF16), cr[...], preferred_element_type=F32).astype(BF16)

        @pl.when(j < WIN - 1)
        def _():
            kv_copy(WIN - 1 - j).start()

        return carry

    lax.fori_loop(low, WIN, back, 0)
    def pair_copy(index, src, columns):
        return pltpu.make_async_remote_copy(
            src_ref=src,
            dst_ref=dproj.at[pl.ds(BLK, BLK), columns],
            send_sem=pair_send.at[index],
            recv_sem=pair_recv.at[index],
            device_id=partner,
            device_id_type=MESH,
        )

    pair_q = []
    for head in range(HEADS):
        dq = (total[:, head * BLK : (head + 1) * BLK] * SCALE).astype(BF16)
        dproj[pl.ds(0, BLK), head * HEAD : (head + 1) * HEAD] = dq.T
        if head % 4 == 3:
            columns = pl.ds((head - 3) * HEAD, 4 * HEAD)
            pair_q.append(pair_copy(head // 4, dproj.at[pl.ds(0, BLK), columns], columns))
            pair_q[-1].start()

    def ring_copy(color, stage, buf, src, there):
        k = (color * 3 + stage) * 6 + buf
        return pltpu.make_async_remote_copy(
            src_ref=src,
            dst_ref=bufs[color][stage].at[buf],
            send_sem=ring_send.at[k],
            recv_sem=ring_recv.at[k],
            device_id=device(there),
            device_id_type=MESH,
        )

    def stage_of(color, stage):
        order = PARTS[color][2]
        dims = [d for d in "zyx" if d in order[stage:]]
        axis = order[stage]
        me = at[axis]
        return (
            dims, axis, me,
            lax.rem(me + 1, 4), lax.rem(me + 2, 4), lax.rem(me + 3, 4),
            moved(at, axis, 1), moved(at, axis, 3),
        )

    started = []

    def open_stage(color, stage):
        dims, axis, me, right, across, left, to_right, to_left = stage_of(color, stage)
        src = data[color][stage]
        if stage == 0:
            pieces = (
                (0, cut(dims, axis, across, 0), to_right),
                (1, cut(dims, axis, across, 1), to_left),
                (3, cut(dims, axis, right, 1), to_right),
                (4, cut(dims, axis, left, 0), to_left),
            )
        else:
            pieces = (
                (2, whole(dims, axis, across), moved(at, axis, 2)),
                (0, whole(dims, axis, right), to_right),
                (1, whole(dims, axis, left), to_left),
            )
        for buf, where, there in pieces:
            copy = ring_copy(color, stage, buf, src.at[where], there)
            copy.start()
            started.append(copy)

    def pass_on(color):
        dims, axis, me, right, across, left, to_right, to_left = stage_of(color, 0)
        src = data[color][0]
        for first, buf, index, half, there in ((0, 2, right, 0, to_right), (1, 5, left, 1, to_left)):
            where = cut(dims, axis, index, half)
            ring_copy(color, 0, first, src.at[where], there).wait_recv()
            src[where] = (src[where].astype(F32) + bufs[color][0][first].astype(F32)).astype(BF16)
            copy = ring_copy(color, 0, buf, src.at[where], there)
            copy.start()
            started.append(copy)

    def close_stage(color, stage):
        dims, axis, me, right, across, left, to_right, to_left = stage_of(color, stage)
        src, got = data[color][stage], bufs[color][stage]
        if stage == 0:
            for half in (0, 1):
                where = cut(dims, axis, me, half)
                summed = src[where].astype(F32)
                for buf in (2 + half, 4 + half):
                    ring_copy(color, 0, buf, src.at[where], to_right).wait_recv()
                    summed = summed + got[buf].astype(F32)
                data[color][1][(slice(None),) * (len(dims) - 1) + (half,)] = summed.astype(BF16)
            return
        where = whole(dims, axis, me)
        summed = src[where].astype(F32)
        for buf in range(3):
            ring_copy(color, stage, buf, src.at[where], to_right).wait_recv()
            summed = summed + got[buf].astype(F32)
        if stage == 1:
            data[color][2][...] = summed.astype(BF16)
        else:
            first, width, _ = PARTS[color]
            wg_ref[:, first : first + width] = summed.reshape(32, width)

    def multiply(color):
        first, width, _ = PARTS[color]

        def body(z, carry):
            rows = pl.ds(pl.multiple_of(z * 512, 512), 512)
            part = jnp.dot(xt[rows, :], dproj[:, first : first + width], preferred_element_type=F32)
            data[color][0][z] = part.astype(BF16).reshape(4, 4, 2, 16, width)
            return carry

        lax.fori_loop(0, 4, body, 0)

    for color in (0, 1, 2, 3, 4):
        if color in (0, 2):
            pair_q[color // 2].wait_recv()
        multiply(color)
        open_stage(color, 0)

    pairs = dkv_ref[WIN - 1].astype(F32)
    for step in range(1, WIN):
        @pl.when(seq + step < SEQN)
        def _(step=step):
            kv_copy(step).wait_recv()

        @pl.when(seq + step >= SEQN)
        def _(step=step):
            dkv_in[step - 1] = jnp.zeros((BLK, 2 * HEAD), BF16)

        pairs = pairs + dkv_in[step - 1].astype(F32)
    dproj[pl.ds(0, BLK), QW:] = pairs.astype(BF16)
    pair_kv = pair_copy(2, dproj.at[pl.ds(0, BLK), pl.ds(QW, 2 * HEAD)], pl.ds(QW, 2 * HEAD))
    pair_kv.start()
    for color in (0, 1, 2):
        pass_on(color)
    pair_kv.wait_recv()
    for color in (5, 6):
        multiply(color)
        open_stage(color, 0)

    def grad_chunk(n, carry):
        rows = pl.ds(pl.multiple_of(n * 512, 512), 512)
        ig_ref[:, rows] = lax.dot_general(
            dproj[pl.ds(0, BLK), :], w_all[pl.ds(2 * n, 2)].reshape(512, COLS), NT, preferred_element_type=F32
        ).astype(BF16)
        return carry

    lax.fori_loop(0, 8, grad_chunk, 0)

    for step in STEPS:
        color, stage = int(step[1]), int(step[2])
        if step[0] == "r":
            pass_on(color)
        else:
            close_stage(color, stage)
            if stage < 2:
                open_stage(color, stage + 1)
    for item in started:
        item.wait_send()
    for item in pair_q:
        item.wait_send()
    pair_kv.wait_send()
    for step in range(1, WIN):
        @pl.when(seq >= step)
        def _(step=step):
            kv_copy(step).wait_send()
    for item in sent:
        item.wait_send()

    for step in range(1, WIN):
        @pl.when(seq + step < SEQN)
        def _(step=step):
            to_peer(step).wait_send()


VM = pl.BlockSpec(memory_space=pltpu.VMEM)
SM = pl.BlockSpec(memory_space=pltpu.SMEM)
ANY = pl.BlockSpec(memory_space=pl.ANY)
DMA = pltpu.SemaphoreType.DMA
LIMIT = 60 * 1024 * 1024


def shape(dims, kind=BF16):
    return jax.ShapeDtypeStruct(dims, kind)


def shards(inputs, weights, cotangent, doc_lengths, kept_flags):
    held, received = [], []
    for _, width, order in PARTS:
        for stage in range(3):
            dims = (4,) * (3 - stage)
            held.append(pltpu.VMEM(dims + (2, 16, width), BF16))
            received.append(pltpu.VMEM(((6,) + dims[1:] if stage == 0 else (3,) + dims[1:] + (2,)) + (16, width), BF16))
    rows = HEADS * BLK
    attention, inputs_grad, weights_grad = pl.pallas_call(
        layer_kernel,
        out_shape=(pltpu.VMEM((BLK, QW), BF16), pltpu.VMEM((BLK, D), BF16), pltpu.VMEM((32, COLS), F32)),
        in_specs=[SM, SM, ANY, ANY, ANY],
        out_specs=(VM, VM, VM),
        scratch_shapes=[
            pltpu.VMEM((BLK, D), BF16),
            pltpu.VMEM((BLK, QW), BF16),
            pltpu.VMEM((16, 4, 2, 32, COLS), BF16),
            pltpu.VMEM((BLK, COLS), F32),
            pltpu.VMEM((8, BLK, 256), BF16),
            pltpu.VMEM((2048, 2 * BLK), BF16),
            pltpu.VMEM((WIN, BLK, 2 * HEAD), BF16),
            pltpu.VMEM((WIN, BLK, rows), F32),
            pltpu.VMEM((WIN, HEAD, BLK), BF16),
            pltpu.VMEM((WIN, HEAD, BLK), BF16),
            pltpu.VMEM((HEAD, rows), BF16),
            pltpu.VMEM((HEAD, rows), BF16),
            pltpu.VMEM((rows, HEAD), BF16),
            pltpu.VMEM((rows, HEAD), BF16),
            pltpu.VMEM((HEAD, rows), F32),
            pltpu.VMEM((WIN, BLK, 2 * HEAD), BF16),
            pltpu.VMEM((2 * BLK, COLS), BF16),
            pltpu.VMEM((WIN - 1, BLK, 2 * HEAD), BF16),
        ]
        + held
        + received
        + [DMA((3,)), DMA((SLOTS,)), DMA((SLOTS,)), DMA((3,)), DMA((3,)), DMA((WIN - 1,)), DMA((WIN - 1,)), DMA((18 * len(PARTS),)), DMA((18 * len(PARTS),))],
        compiler_params=pltpu.CompilerParams(collective_id=0, has_side_effects=True, vmem_limit_bytes=LIMIT),
        name="layer",
    )(doc_lengths, kept_flags, inputs[0], weights.reshape(4, 2, 32, COLS), cotangent[0])
    return (attention[None], inputs_grad[None], weights_grad)


def solution(mesh):
    in_specs = (
        P("dp", "seq", None),
        P("dp", None),
        P("dp", "seq", None),
        P("dp", None),
        P("dp", None),
    )
    out_specs = (P("dp", "seq", None), P("dp", "seq", None), P(("dp", "seq"), None))
    return jax.shard_map(shards, mesh=mesh, in_specs=in_specs, out_specs=out_specs, check_vma=False)
```
